32 devices in a mesh: wide: 8 (over z, y), narrow: 4 (over x, core).
Axes of the slice: x: 2, y: 2, z: 4, core: 2. Of those that a mesh axis runs over, the one named last changes fastest.
Arguments:
- frames: bfloat16 [32, 512, 1024], P(('wide', 'narrow')), may hold values from -6 to 6
- lengths: int32 [32], P(('wide', 'narrow')), may hold values from 64 to 512, as said below
- w_query: bfloat16 [1024, 1024], P(('wide', 'narrow')), may hold values from -0.25 to 0.25
- w_key: bfloat16 [1024, 1024], P(('wide', 'narrow')), may hold values from -0.25 to 0.25
- w_value: bfloat16 [1024, 1024], P(('wide', 'narrow')), may hold values from -0.1875 to 0.1875
- w_out: bfloat16 [1024, 1024], P(('wide', 'narrow')), may hold values from -1 to 1
- w_up: bfloat16 [1024, 4096], P(('wide', 'narrow')), may hold values from -0.1875 to 0.1875
- w_down: bfloat16 [4096, 1024], P(('wide', 'narrow')), may hold values from -0.09375 to 0.09375
- gain_attn: bfloat16 [1024], P(('wide', 'narrow')), may hold values from 0.099609375 to 1.8984375
- gain_mlp: bfloat16 [1024], P(('wide', 'narrow')), may hold values from 0.099609375 to 1.8984375
- cotangent: bfloat16 [32, 512, 1024], P(('wide', 'narrow')), may hold values from -6 to 6
Outputs:
- output: bfloat16 [32, 512, 1024], P(('wide', 'narrow'))
- grad_frames: float32 [32, 512, 1024], P(('wide', 'narrow'))
- grad_query: float32 [1024, 1024], P(('wide', 'narrow'))
- grad_key: float32 [1024, 1024], P(('wide', 'narrow'))
- grad_value: float32 [1024, 1024], P(('wide', 'narrow'))
- grad_out: float32 [1024, 1024], P(('wide', 'narrow'))
- grad_up: float32 [1024, 4096], P(('wide', 'narrow'))
- grad_down: float32 [4096, 1024], P(('wide', 'narrow'))
- grad_gain_attn: float32 [1024], P(('wide', 'narrow'))
- grad_gain_mlp: float32 [1024], P(('wide', 'narrow'))
The draws below stay inside these ranges and needn't reach their ends.
Inputs may be any that keep to these rules, and one draw needn't show every extreme that they name: `lengths`: every draw has an item of exactly 512 frames and one of exactly 64.
All inputs are finite; a program needn't handle non-finite values.
Results may differ from the reference program's by a relative error of at most 0.013.
The reference program's roundings to bfloat16 on the way count: a program that leaves them out, or rounds other values in their place, can miss the bound.
Values may be sent and summed in bfloat16 or wider, within the bound.
No kernel may reach another device: no remote copies, remote signals or barrier semaphores. Data moves between devices by JAX's collectives and lax.ppermute only.
A program may use at most 256 MiB of HBM per device.

```python
import jax
import jax.numpy as jnp
from jax import lax

D = 1024
HEADS = 16
HEAD_DIM = 64
FF = 4096
SLOT = 512
ITEMS = 32


def draw_lengths(key, part):
    base = jax.random.randint(key, (ITEMS,), SLOT // 8, SLOT + 1, dtype=jnp.int32)
    order = jax.random.permutation(jax.random.fold_in(key, 7), ITEMS)
    base = base.at[order[0]].set(SLOT).at[order[1]].set(SLOT // 8)
    return base.astype(jnp.int32)


def steps_of(rng, extent, shards, least, top_value):
    def one(axis_at, blocks):
        heights = jax.random.uniform(jax.random.fold_in(jax.random.fold_in(rng, 6), axis_at), (blocks,), jnp.float32, least / len(shards), top_value / len(shards))
        return jnp.repeat(jnp.exp(heights), extent[axis_at] // blocks).reshape((-1,) + (1,) * (len(extent) - axis_at - 1))

    factor_of = one(*shards[0])
    for cut in shards[1:]:
        factor_of = factor_of * one(*cut)
    return factor_of


def noise(own_key, extent, scale, reach, pieces=(), kind=jnp.bfloat16):
    drawn = scale * jax.random.normal(own_key, extent, jnp.float32)
    if pieces:
        drawn = drawn * steps_of(own_key, extent, pieces, -0.22, 0.18)
    return jnp.clip(drawn, -reach, reach).astype(kind)


def setup_inputs(seed: int = 0) -> dict:
    streams_of = jax.random.split(jax.random.key(seed), 12)
    return {
        "frames": noise(streams_of[0], (ITEMS, SLOT, D), 1.0, 6.0, ((0, 32),)),
        "lengths": draw_lengths(jax.random.fold_in(streams_of[11], 71), 0),
        "w_query": noise(streams_of[2], (D, D), (D // 2) ** -0.5, 0.25, ((0, 32),)),
        "w_key": noise(streams_of[3], (D, D), (D // 2) ** -0.5, 0.25, ((0, 32),)),
        "w_value": noise(streams_of[4], (D, D), D ** -0.5, 0.1875, ((0, 32),)),
        "w_out": noise(streams_of[5], (D, D), (D * 16 // SLOT) ** -0.5, 1.0, ((0, 32),)),
        "w_up": noise(streams_of[6], (D, FF), D ** -0.5, 0.1875, ((0, 32),)),
        "w_down": noise(streams_of[7], (FF, D), FF ** -0.5, 0.09375, ((0, 32),)),
        "gain_attn": jnp.clip(1.0 + 0.18 * jax.random.normal(streams_of[8], (D,), jnp.float32), 0.099609375, 1.8984375).astype(jnp.bfloat16),
        "gain_mlp": jnp.clip(1.0 + 0.18 * jax.random.normal(streams_of[9], (D,), jnp.float32), 0.099609375, 1.8984375).astype(jnp.bfloat16),
        "cotangent": noise(streams_of[10], (ITEMS, SLOT, D), 1.0, 6.0, ((0, 32),)),
    }


PRECISE = lax.Precision.HIGHEST
EPSILON = 1e-06

@jax.custom_vjp
def low(v):
    return lax.optimization_barrier(v.astype(jnp.bfloat16)).astype(jnp.float32)

@jax.custom_vjp
def low_back(v):
    return v

def low_keep(v):
    return (low(v), None)

def low_pass(kept, grad):
    return (grad,)

def back_keep(v):
    return (v, None)

def back_low(kept, grad):
    return (low(grad),)
low.defvjp(low_keep, low_pass)
low_back.defvjp(back_keep, back_low)

def product(left, right):
    return jnp.dot(left, right, precision=PRECISE)

def normed(values, gain):
    return values * lax.rsqrt(lax.optimization_barrier(jnp.mean(values * values, axis=-1, keepdims=True)) + EPSILON) * gain

def reference(frames, lengths, w_query, w_key, w_value, w_out, w_up, w_down, gain_attn, gain_mlp, cotangent):
    factor = HEAD_DIM ** (-0.5)

    def forward(inputs, query_mat, key_mat, value_mat, out_mat, up_mat, down_mat, attn_gain, mlp_gain):

        def single(element):
            rows_in, length = element
            key_mask = jnp.arange(SLOT, dtype=jnp.int32) < length
            hidden = low(normed(rows_in, attn_gain))
            queries = low(low_back(product(hidden, query_mat))).reshape(SLOT, HEADS, HEAD_DIM)
            key_rows = low(low_back(product(hidden, key_mat))).reshape(SLOT, HEADS, HEAD_DIM)
            values = low(low_back(product(hidden, value_mat))).reshape(SLOT, HEADS, HEAD_DIM)
            scores = jnp.einsum('qhd,khd->hqk', queries, key_rows, precision=PRECISE) * factor
            scores = jnp.where(key_mask[None, None, :], low_back(scores), -1e+30)
            shares = low(jax.nn.softmax(scores, axis=-1))
            mixed = jnp.einsum('hqk,khd->qhd', shares, values, precision=PRECISE).reshape(SLOT, D)
            mixed = low(low_back(mixed))
            middle = rows_in + low_back(product(mixed, out_mat))
            second = low(normed(middle, mlp_gain))
            upward = low_back(product(second, up_mat))
            active = low(jax.nn.gelu(upward, approximate=True))
            result = middle + low_back(product(active, down_mat))
            return result * key_mask[:, None].astype(jnp.float32)
        return lax.map(jax.checkpoint(single), (inputs, lengths))
    floats = tuple((a.astype(jnp.float32) for a in (frames, w_query, w_key, w_value, w_out, w_up, w_down, gain_attn, gain_mlp)))
    result, pull = jax.vjp(forward, *floats)
    grads = pull(cotangent.astype(jnp.float32))
    return (result.astype(jnp.bfloat16), grads[0], grads[1], grads[2], grads[3], grads[4], grads[5], grads[6], grads[7], grads[8])
```

```python
from functools import partial

import jax
import jax.numpy as jnp
from jax import lax
from jax.sharding import PartitionSpec as P

HEADS = 16
HEAD_DIM = 64


EPSILON = 1e-06


def norm_forward(rows_in, gain):
    inverse = lax.rsqrt(jnp.mean(rows_in * rows_in, axis=-1, keepdims=True) + EPSILON)
    normal = rows_in * inverse
    return (normal * gain, normal, inverse)


def norm_backward(grad_in, gain, normal, inverse):
    scaled = grad_in * gain
    grad_rows = inverse * (scaled - normal * jnp.mean(scaled * normal, axis=-1, keepdims=True))
    return (grad_rows, jnp.sum(grad_in * normal, axis=0))


AXES = ("wide", "narrow")
LANES = 128


def gather_rows(shard):
    return lax.all_gather(shard, AXES, axis=0, tiled=True)


def scatter_rows(grad):
    return lax.psum_scatter(grad.astype(jnp.bfloat16), AXES, scatter_dimension=0, tiled=True).astype(jnp.float32)


def fetch_weights(w_query, w_key, w_value, w_out, w_up, w_down, gain_attn, gain_mlp):
    width = w_query.shape[1]
    gains = jnp.stack((gain_attn, gain_mlp), axis=1)
    gains = jnp.pad(gains, ((0, 0), (0, LANES - 2)))
    attn = gather_rows(jnp.concatenate((w_query, w_key, w_value, w_out, gains), axis=1))
    up_mat = gather_rows(w_up)
    down_mat = gather_rows(w_down)
    gain_pair = attn[:, 4 * width : 4 * width + 2].T
    return (
        attn[:, :width],
        attn[:, width : 2 * width],
        attn[:, 2 * width : 3 * width],
        attn[:, 3 * width : 4 * width],
        up_mat,
        down_mat,
        gain_pair[0],
        gain_pair[1],
    )


def split_halves(values):
    high = values.astype(jnp.bfloat16)
    low = (values - high.astype(jnp.float32)).astype(jnp.bfloat16)
    return (high, low)


def spread_grads(
    grad_query, grad_key, grad_value, grad_outmat, grad_up, grad_down, grad_gain1, grad_gain2
):
    width = grad_query.shape[1]
    down_rows = scatter_rows(grad_down)
    up_rows = scatter_rows(grad_up)
    gains = jnp.stack(split_halves(grad_gain1) + split_halves(grad_gain2), axis=1)
    gains = jnp.pad(gains, ((0, 0), (0, LANES - 4)))
    joined = [part.astype(jnp.bfloat16) for part in (grad_query, grad_key, grad_value, grad_outmat)]
    rows = scatter_rows(jnp.concatenate(joined + [gains], axis=1))
    extra = rows[:, 4 * width :]
    return (
        rows[:, :width],
        rows[:, width : 2 * width],
        rows[:, 2 * width : 3 * width],
        rows[:, 3 * width : 4 * width],
        up_rows,
        down_rows,
        extra[:, 0] + extra[:, 1],
        extra[:, 2] + extra[:, 3],
    )


def masked_scores(queries, key_rows, key_mask):
    factor = HEAD_DIM ** (-0.5)
    scores = (
        jnp.einsum("qhd,khd->hqk", queries, key_rows, preferred_element_type=jnp.float32) * factor
    )
    return jnp.where(key_mask[None, None, :], scores, -1e30)


def attend(element):
    queries, key_rows, values, key_mask = element
    scores = masked_scores(queries, key_rows, key_mask)
    peak_score = jnp.max(scores, axis=-1, keepdims=True)
    expon = jnp.exp(scores - peak_score)
    totals = jnp.sum(expon, axis=-1, keepdims=True)
    shares = (expon / totals).astype(jnp.bfloat16)
    mixed = jnp.einsum("hqk,khd->qhd", shares, values, preferred_element_type=jnp.float32)
    return (mixed, peak_score + jnp.log(totals))


def attend_back(element):
    queries, key_rows, values, key_mask, log_total, grad_mixed = element
    factor = HEAD_DIM ** (-0.5)
    scores = masked_scores(queries, key_rows, key_mask)
    chance = jnp.exp(scores - log_total)
    grad_values = jnp.einsum(
        "hqk,qhd->khd", chance.astype(jnp.bfloat16), grad_mixed, preferred_element_type=jnp.float32
    )
    grad_chance = jnp.einsum("qhd,khd->hqk", grad_mixed, values, preferred_element_type=jnp.float32)
    grad_scores = (
        chance * (grad_chance - jnp.sum(chance * grad_chance, axis=-1, keepdims=True))
    ).astype(jnp.bfloat16)
    grad_queries = (
        jnp.einsum("hqk,khd->qhd", grad_scores, key_rows, preferred_element_type=jnp.float32)
        * factor
    )
    grad_keys = (
        jnp.einsum("hqk,qhd->khd", grad_scores, queries, preferred_element_type=jnp.float32)
        * factor
    )
    return (
        grad_queries.astype(jnp.bfloat16),
        grad_keys.astype(jnp.bfloat16),
        grad_values.astype(jnp.bfloat16),
    )


def recompute(frames, key_mask, row_mask, gathered):
    query_mat, key_mat, value_mat, out_mat, up_mat, down_mat, attn_gain, mlp_gain = gathered
    item_count, slot_len, model_width = frames.shape
    rows_in = frames.reshape(item_count * slot_len, model_width).astype(jnp.float32)
    normed_one, normal1, inverse1 = norm_forward(rows_in, attn_gain.astype(jnp.float32))
    hidden = normed_one.astype(jnp.bfloat16)
    split_shape = (item_count, slot_len, HEADS, HEAD_DIM)
    queries = (
        jnp.dot(hidden, query_mat, preferred_element_type=jnp.float32)
        .astype(jnp.bfloat16)
        .reshape(split_shape)
    )
    key_rows = (
        jnp.dot(hidden, key_mat, preferred_element_type=jnp.float32)
        .astype(jnp.bfloat16)
        .reshape(split_shape)
    )
    values = (
        jnp.dot(hidden, value_mat, preferred_element_type=jnp.float32)
        .astype(jnp.bfloat16)
        .reshape(split_shape)
    )
    mixed, log_total = lax.map(attend, (queries, key_rows, values, key_mask))
    mixed_low = mixed.reshape(item_count * slot_len, model_width).astype(jnp.bfloat16)
    middle = rows_in + jnp.dot(mixed_low, out_mat, preferred_element_type=jnp.float32)
    normed_two, normal2, inverse2 = norm_forward(middle, mlp_gain.astype(jnp.float32))
    second = normed_two.astype(jnp.bfloat16)
    upward = jnp.dot(second, up_mat, preferred_element_type=jnp.float32)
    active = jax.nn.gelu(upward, approximate=True).astype(jnp.bfloat16)
    result = (middle + jnp.dot(active, down_mat, preferred_element_type=jnp.float32)) * row_mask
    return (
        hidden,
        queries,
        key_rows,
        values,
        log_total,
        mixed_low,
        normal1,
        inverse1,
        normal2,
        inverse2,
        second,
        upward,
        active,
        result,
    )


def on_device(
    frames, lengths, w_query, w_key, w_value, w_out, w_up, w_down, gain_attn, gain_mlp, cotangent
):
    item_count, slot_len, model_width = frames.shape
    key_mask = lax.broadcasted_iota(jnp.int32, (item_count, slot_len), 1) < lengths[:, None]
    row_mask = key_mask.reshape(item_count * slot_len, 1).astype(jnp.float32)
    gathered = fetch_weights(w_query, w_key, w_value, w_out, w_up, w_down, gain_attn, gain_mlp)
    forward_state = recompute(frames, key_mask, row_mask, gathered)
    output = forward_state[13].astype(jnp.bfloat16).reshape(frames.shape)
    query_mat, key_mat, value_mat, out_mat, up_mat, down_mat, attn_gain, mlp_gain = gathered
    state = forward_state
    (
        hidden,
        queries,
        key_rows,
        values,
        log_total,
        mixed_low,
        normal1,
        inverse1,
        normal2,
        inverse2,
        second,
        upward,
        active,
        ignored,
    ) = state
    grad_res = cotangent.reshape(item_count * slot_len, model_width).astype(jnp.float32) * row_mask
    grad_branch = grad_res.astype(jnp.bfloat16)
    grad_down = jnp.einsum("rf,rd->fd", active, grad_branch, preferred_element_type=jnp.float32)
    grad_active = jnp.einsum("rd,fd->rf", grad_branch, down_mat, preferred_element_type=jnp.float32)
    unused, gelu_pull = jax.vjp(partial(jax.nn.gelu, approximate=True), upward)
    grad_upward = gelu_pull(grad_active)[0].astype(jnp.bfloat16)
    grad_up = jnp.einsum("rd,rf->df", second, grad_upward, preferred_element_type=jnp.float32)
    grad_second = jnp.einsum("rf,df->rd", grad_upward, up_mat, preferred_element_type=jnp.float32)
    grad_norm2, grad_gain2 = norm_backward(
        grad_second, mlp_gain.astype(jnp.float32), normal2, inverse2
    )
    grad_middle = grad_res + grad_norm2
    grad_attn = grad_middle.astype(jnp.bfloat16)
    grad_outmat = jnp.einsum("rd,re->de", mixed_low, grad_attn, preferred_element_type=jnp.float32)
    grad_mixed = jnp.einsum(
        "re,de->rd", grad_attn, out_mat, preferred_element_type=jnp.float32
    ).astype(jnp.bfloat16)
    grad_mixed = grad_mixed.reshape(item_count, slot_len, HEADS, HEAD_DIM)
    grad_queries, grad_keys, grad_values = lax.map(
        attend_back, (queries, key_rows, values, key_mask, log_total, grad_mixed)
    )
    flat_rows = (item_count * slot_len, model_width)
    grad_queries = grad_queries.reshape(flat_rows)
    grad_keys = grad_keys.reshape(flat_rows)
    grad_values = grad_values.reshape(flat_rows)
    grad_query = jnp.einsum("rd,re->de", hidden, grad_queries, preferred_element_type=jnp.float32)
    grad_key = jnp.einsum("rd,re->de", hidden, grad_keys, preferred_element_type=jnp.float32)
    grad_value = jnp.einsum("rd,re->de", hidden, grad_values, preferred_element_type=jnp.float32)
    grad_hidden = jnp.einsum(
        "re,de->rd", grad_queries, query_mat, preferred_element_type=jnp.float32
    )
    grad_hidden = grad_hidden + jnp.einsum(
        "re,de->rd", grad_keys, key_mat, preferred_element_type=jnp.float32
    )
    grad_hidden = grad_hidden + jnp.einsum(
        "re,de->rd", grad_values, value_mat, preferred_element_type=jnp.float32
    )
    grad_norm1, grad_gain1 = norm_backward(
        grad_hidden, attn_gain.astype(jnp.float32), normal1, inverse1
    )
    grad_frames = (grad_middle + grad_norm1).reshape(frames.shape)
    owned = spread_grads(
        grad_query, grad_key, grad_value, grad_outmat, grad_up, grad_down, grad_gain1, grad_gain2
    )
    return (
        output,
        grad_frames,
        owned[0],
        owned[1],
        owned[2],
        owned[3],
        owned[4],
        owned[5],
        owned[6],
        owned[7],
    )


def solution(mesh):
    return jax.shard_map(
        on_device,
        mesh=mesh,
        in_specs=(
            P(("wide", "narrow"), None, None),
            P(("wide", "narrow")),
            P(("wide", "narrow"), None),
            P(("wide", "narrow"), None),
            P(("wide", "narrow"), None),
            P(("wide", "narrow"), None),
            P(("wide", "narrow"), None),
            P(("wide", "narrow"), None),
            P(("wide", "narrow")),
            P(("wide", "narrow")),
            P(("wide", "narrow"), None, None),
        ),
        out_specs=(
            P(("wide", "narrow"), None, None),
            P(("wide", "narrow"), None, None),
            P(("wide", "narrow"), None),
            P(("wide", "narrow"), None),
            P(("wide", "narrow"), None),
            P(("wide", "narrow"), None),
            P(("wide", "narrow"), None),
            P(("wide", "narrow"), None),
            P(("wide", "narrow")),
            P(("wide", "narrow")),
        ),
        check_vma=False,
    )
```

```python
import functools

import jax
import jax.numpy as jnp
import numpy as np
from jax import lax
from jax.experimental import pallas as pl
from jax.experimental.pallas import tpu as pltpu
from jax.sharding import Mesh, PartitionSpec as P

HEADS = 16
HEAD_DIM = 64
EPSILON = 1e-06
FACTOR = HEAD_DIM ** (-0.5)
LANES = 128
Z_PARTS = 4
PIECES = 8
ALL = ("z", "y", "x", "c")
PLANE = ("y", "x", "c")
SWAP = [(0, 1), (1, 0)]
VMEM_LIMIT = 56 << 20
F32 = jnp.float32
BF16 = jnp.bfloat16
GELU_A = 0.7978845608028654
GELU_B = 0.044715

NN = (((1,), (0,)), ((), ()))
NT = (((1,), (1,)), ((), ()))
TN = (((0,), (0,)), ((), ()))


def mxu(left, right, dims=NN):
    return lax.dot_general(left, right, dims, preferred_element_type=F32)


def plane_pairs(step):
    pairs = []
    for y in range(2):
        for x in range(2):
            for c in range(2):
                flip_y = (c == 0) == (step == 1)
                to = (1 - y, x, c) if flip_y else (y, 1 - x, c)
                pairs.append(((y * 2 + x) * 2 + c, (to[0] * 2 + to[1]) * 2 + to[2]))
    return pairs


def is_plane(sizes):
    return sizes["x"] == 2 and sizes["y"] == 2 and sizes["c"] == 2 and sizes["z"] == Z_PARTS


def piece_blocks(sizes):
    piece = jnp.arange(PIECES, dtype=jnp.int32)
    if not is_plane(sizes):
        return piece
    own = (piece >> 2) & 1
    first = (piece >> 1) & 1
    second = piece & 1
    core = lax.axis_index("c") ^ own
    on_y = jnp.where(core == 0, first, second)
    on_x = jnp.where(core == 0, second, first)
    y = lax.axis_index("y") ^ on_y
    x = lax.axis_index("x") ^ on_x
    return ((y * 2 + x) * 2 + core).astype(jnp.int32)


def gather_pieces(shard, sizes):
    if not is_plane(sizes):
        full = lax.all_gather(shard, ALL, axis=0, tiled=True)
        full = full.reshape(Z_PARTS, PIECES, full.shape[0] // (Z_PARTS * PIECES), full.shape[1])
        full = full.transpose(1, 0, 2, 3).reshape((2, 2, 2, Z_PARTS) + full.shape[2:])
        return (full[0, :, 0], full[0, :, 1], full[1, :, 0], full[1, :, 1])
    column = lax.all_gather(shard, "z", axis=0, tiled=False)
    near = lax.ppermute(column, PLANE, plane_pairs(1))
    own = jnp.stack((column, near))
    far = lax.ppermute(own, PLANE, plane_pairs(2))
    return (own, far, lax.ppermute(own, "c", SWAP), lax.ppermute(far, "c", SWAP))


def total(*parts):
    result = parts[0].astype(F32)
    for part in parts[1:]:
        result = result + part.astype(F32)
    return result


def scatter_pieces(own, other, sizes):
    if not is_plane(sizes):
        full = jnp.stack((own, other))
        full = full.reshape((PIECES,) + full.shape[3:]).transpose(1, 0, 2, 3)
        full = full.reshape(-1, full.shape[-1])
        return lax.psum_scatter(full, ALL, scatter_dimension=0, tiled=True).astype(F32)
    got = lax.ppermute(other, "c", SWAP)
    away = total(own[1], got[1]).astype(BF16)
    near = lax.ppermute(away, PLANE, plane_pairs(1))
    away = total(own[0, 1], got[0, 1], near[1]).astype(BF16)
    far = lax.ppermute(away, PLANE, plane_pairs(2))
    mine = total(own[0, 0], got[0, 0], near[0], far).astype(BF16)
    return lax.psum_scatter(mine, "z", scatter_dimension=0, tiled=False).astype(F32)


def params(**more):
    return pltpu.CompilerParams(vmem_limit_bytes=VMEM_LIMIT, **more)


HBM_SPEC = pl.BlockSpec(memory_space=pl.ANY)
SMEM_SPEC = pl.BlockSpec(memory_space=pltpu.SMEM)


def whole(shape):
    return pl.BlockSpec(shape, lambda *_: (0,) * len(shape))


def piece_copies(pieces, blocks, held, sems, columns):
    rows = pieces[0].shape[2]
    copies = []
    for piece in range(PIECES):
        own, first, second = piece >> 2, (piece >> 1) & 1, piece & 1
        source = pieces[2 * own + second].at[first, :, :, columns]
        start = pl.multiple_of(blocks[piece] * rows, rows)
        copies.append(
            pltpu.make_async_copy(source, held.at[:, pl.ds(start, rows), :], sems.at[piece])
        )
    return copies


def part_copies(pieces, blocks, part, held, sems):
    rows = pieces[0].shape[2]
    copies = []
    for piece in range(PIECES):
        own, first, second = piece >> 2, (piece >> 1) & 1, piece & 1
        source = pieces[2 * own + second].at[first, part]
        start = pl.multiple_of(blocks[piece] * rows, rows)
        copies.append(
            pltpu.make_async_copy(source, held.at[pl.ds(start, rows), :], sems.at[piece])
        )
    return copies


def grad_copies(held, outs, blocks, columns, sems):
    rows = outs[0].shape[3]
    copies = []
    for piece in range(PIECES):
        own, first, second = piece >> 2, (piece >> 1) & 1, piece & 1
        target = outs[own].at[first, second, :, :, columns]
        start = pl.multiple_of(blocks[piece] * rows, rows)
        copies.append(
            pltpu.make_async_copy(held.at[:, pl.ds(start, rows), :], target, sems.at[piece])
        )
    return copies


def grad_part_copies(held, outs, blocks, part, sems):
    rows = outs[0].shape[3]
    copies = []
    for piece in range(PIECES):
        own, first, second = piece >> 2, (piece >> 1) & 1, piece & 1
        target = outs[own].at[first, second, part]
        start = pl.multiple_of(blocks[piece] * rows, rows)
        copies.append(
            pltpu.make_async_copy(held.at[pl.ds(start, rows), :], target, sems.at[piece])
        )
    return copies


def start_all(copies):
    for copy in copies:
        copy.start()


def wait_all(copies):
    for copy in copies:
        copy.wait()


def flat(block):
    return block.reshape(block.shape[0] * block.shape[1], block.shape[2])


def inverse_rms(rows):
    return lax.rsqrt(jnp.mean(rows * rows, axis=-1, keepdims=True) + EPSILON)


def qkv_kernel(blocks, frames, p0, p1, p2, p3, hidden, qkv, gains, held, gain_held, sems):
    step = pl.program_id(0)
    pieces = (p0, p1, p2, p3)
    width = frames.shape[1]

    def copies(part):
        return piece_copies(
            pieces, blocks, held.at[part], sems.at[part], pl.ds(part * width, width)
        )

    @pl.when(step == 0)
    def _():
        gain_copies = piece_copies(
            pieces, blocks, gain_held, sems.at[3], pl.ds(4 * width, LANES)
        )
        start_all(gain_copies)
        for part in range(3):
            start_all(copies(part))
        wait_all(gain_copies)
        across = flat(gain_held[...]).astype(F32).T
        gains[...] = across[:8]
        rows = frames[...].astype(F32)
        hidden[...] = (rows * inverse_rms(rows) * across[0:1]).astype(BF16)
        wait_all(copies(0))

    for part in (1, 2):

        @pl.when(step == part)
        def _():
            wait_all(copies(part))

    result = mxu(hidden[...], flat(held[step]))
    scale = jnp.where(step == 0, FACTOR, 1.0)
    qkv[...] = (result.astype(BF16).astype(F32) * scale).astype(BF16)


def qkv_call(blocks, frames, pieces):
    rows, width = frames.shape
    return pl.pallas_call(
        qkv_kernel,
        grid=(3,),
        in_specs=[SMEM_SPEC, whole((rows, width))] + [HBM_SPEC] * 4,
        out_specs=[
            whole((rows, width)),
            pl.BlockSpec((rows, width), lambda j: (0, j)),
            whole((8, width)),
        ],
        out_shape=[
            jax.ShapeDtypeStruct((rows, width), BF16),
            jax.ShapeDtypeStruct((rows, 3 * width), BF16),
            jax.ShapeDtypeStruct((8, width), F32),
        ],
        scratch_shapes=[
            pltpu.VMEM((3, Z_PARTS, width // Z_PARTS, width), BF16),
            pltpu.VMEM((Z_PARTS, width // Z_PARTS, LANES), BF16),
            pltpu.SemaphoreType.DMA((4, PIECES)),
        ],
        compiler_params=params(),
        cost_estimate=pl.CostEstimate(
            flops=6 * rows * width * width, bytes_accessed=10 * width * width, transcendentals=0
        ),
        name="qkv",
    )(blocks, frames, *pieces)


def attend_kernel(length, queries, keys, values, mixed, log_totals):
    pair = pl.program_id(0)
    rows = queries.shape[0]
    chunk = min(rows, 256)
    bias = jnp.where(
        lax.broadcasted_iota(jnp.int32, (1, rows), 1) < length[0], 0.0, -1e30
    ).astype(F32)
    lane = lax.broadcasted_iota(jnp.int32, (chunk, LANES), 1)

    @pl.when(pair == 0)
    def _():
        log_totals[...] = jnp.zeros_like(log_totals)

    for at in range(0, rows, chunk):
        here = pl.ds(at, chunk)
        part = queries[here, :]
        logs = log_totals[here, :]
        outs = []
        for half in range(2):
            query = jnp.where((lane < HEAD_DIM) == (half == 0), part, jnp.zeros_like(part))
            scores = mxu(query, keys[...], NT) + bias
            peak = jnp.max(scores, axis=-1, keepdims=True)
            expon = jnp.exp(scores - peak)
            sums = jnp.sum(expon, axis=-1, keepdims=True)
            shares = (expon * (1.0 / sums)).astype(BF16)
            outs.append(mxu(shares, values[...]))
            logs = jnp.where(lane == 2 * pair + half, peak + jnp.log(sums), logs)
        mixed[here, :] = jnp.where(lane < HEAD_DIM, outs[0], outs[1]).astype(BF16)
        log_totals[here, :] = logs


def attend_call(length, qkv):
    rows, width = qkv.shape[0], qkv.shape[1] // 3
    pairs = width // LANES
    return pl.pallas_call(
        attend_kernel,
        grid=(pairs,),
        in_specs=[
            SMEM_SPEC,
            pl.BlockSpec((rows, LANES), lambda h: (0, h)),
            pl.BlockSpec((rows, LANES), lambda h: (0, pairs + h)),
            pl.BlockSpec((rows, LANES), lambda h: (0, 2 * pairs + h)),
        ],
        out_specs=[pl.BlockSpec((rows, LANES), lambda h: (0, h)), whole((rows, LANES))],
        out_shape=[
            jax.ShapeDtypeStruct((rows, width), BF16),
            jax.ShapeDtypeStruct((rows, LANES), F32),
        ],
        compiler_params=params(),
        cost_estimate=pl.CostEstimate(
            flops=16 * rows * rows * width,
            bytes_accessed=8 * rows * width,
            transcendentals=HEADS * rows * rows,
        ),
        name="attend",
    )(length, qkv, qkv, qkv)


def out_kernel(blocks, frames, mixed, gains, p0, p1, p2, p3, middle, second, held, sems):
    width = frames.shape[1]
    copies = piece_copies((p0, p1, p2, p3), blocks, held, sems, pl.ds(3 * width, width))
    start_all(copies)
    wait_all(copies)
    result = frames[...].astype(F32) + mxu(mixed[...], flat(held[...]))
    middle[...] = result
    second[...] = (result * inverse_rms(result) * gains[1:2, :]).astype(BF16)


def out_call(blocks, frames, mixed, gains, pieces):
    rows, width = frames.shape
    return pl.pallas_call(
        out_kernel,
        grid=(1,),
        in_specs=[SMEM_SPEC, whole((rows, width)), whole((rows, width)), whole((8, width))]
        + [HBM_SPEC] * 4,
        out_specs=[whole((rows, width)), whole((rows, width))],
        out_shape=[
            jax.ShapeDtypeStruct((rows, width), F32),
            jax.ShapeDtypeStruct((rows, width), BF16),
        ],
        scratch_shapes=[
            pltpu.VMEM((Z_PARTS, width // Z_PARTS, width), BF16),
            pltpu.SemaphoreType.DMA((PIECES,)),
        ],
        compiler_params=params(),
        cost_estimate=pl.CostEstimate(
            flops=2 * rows * width * width, bytes_accessed=6 * width * width, transcendentals=0
        ),
        name="outward",
    )(blocks, frames, mixed, gains, *pieces)


def up_kernel(
    blocks, second, branch, p0, p1, p2, p3, upward, active, own, other,
    held, grads, sems, grad_sems,
):
    step = pl.program_id(0)
    steps = Z_PARTS
    slot = lax.rem(step, 2)
    pieces = (p0, p1, p2, p3)
    columns = held.shape[3]

    def copies(part):
        return piece_copies(
            pieces, blocks, held.at[part], sems.at[part], pl.ds(part * columns, columns)
        )

    def leave(part, at):
        return grad_part_copies(grads.at[at], (own, other), blocks, part, grad_sems.at[at])

    @pl.when(step == 0)
    def _():
        for part in range(steps):
            start_all(copies(part))

    for part in range(steps):

        @pl.when(step == part)
        def _():
            wait_all(copies(part))

    value = mxu(second[...], flat(held[step]))
    upward[...] = value
    bent = 0.5 * value * (1.0 + jnp.tanh(GELU_A * (value + GELU_B * value * value * value)))
    active[...] = bent.astype(BF16)

    @pl.when(step >= 2)
    def _():
        wait_all(leave(step - 2, slot))

    grads[slot] = mxu(active[...], branch[...], TN).astype(BF16)
    start_all(leave(step, slot))

    @pl.when(step == steps - 1)
    def _():
        wait_all(leave(step - 1, 1 - slot))
        wait_all(leave(step, slot))


def up_call(blocks, second, branch, pieces):
    rows, width = second.shape
    inner = pieces[0].shape[3]
    columns = inner // Z_PARTS
    part_rows = inner // (Z_PARTS * PIECES)
    grad = jax.ShapeDtypeStruct((2, 2, Z_PARTS, part_rows, width), BF16)
    return pl.pallas_call(
        up_kernel,
        grid=(Z_PARTS,),
        in_specs=[SMEM_SPEC, whole((rows, width)), whole((rows, width))] + [HBM_SPEC] * 4,
        out_specs=[
            pl.BlockSpec((rows, columns), lambda j: (0, j)),
            pl.BlockSpec((rows, columns), lambda j: (0, j)),
            HBM_SPEC,
            HBM_SPEC,
        ],
        out_shape=[
            jax.ShapeDtypeStruct((rows, inner), F32),
            jax.ShapeDtypeStruct((rows, inner), BF16),
            grad,
            grad,
        ],
        scratch_shapes=[
            pltpu.VMEM((Z_PARTS, Z_PARTS, width // Z_PARTS, columns), BF16),
            pltpu.VMEM((2, columns, width), BF16),
            pltpu.SemaphoreType.DMA((Z_PARTS, PIECES)),
            pltpu.SemaphoreType.DMA((2, PIECES)),
        ],
        compiler_params=params(),
        cost_estimate=pl.CostEstimate(
            flops=4 * rows * width * inner,
            bytes_accessed=4 * width * inner + 6 * rows * inner,
            transcendentals=rows * inner,
        ),
        name="upward",
    )(blocks, second, branch, *pieces)


def down_kernel(
    blocks, branch, second, upward, p0, p1, p2, p3, grad_upward, own, other,
    held, grads, sems, grad_sems,
):
    step = pl.program_id(0)
    steps = Z_PARTS
    slot = lax.rem(step, 2)
    pieces = (p0, p1, p2, p3)
    columns = upward.shape[1]

    def copies(part):
        return part_copies(pieces, blocks, part, held.at[part], sems.at[part])

    def leave(part, at):
        start = pl.multiple_of(part * columns, columns)
        return grad_copies(
            grads.at[at], (own, other), blocks, pl.ds(start, columns), grad_sems.at[at]
        )

    @pl.when(step == 0)
    def _():
        for part in range(steps):
            start_all(copies(part))

    for part in range(steps):

        @pl.when(step == part)
        def _():
            wait_all(copies(part))

    grad_active = mxu(branch[...], held[step], NT)
    value = upward[...]
    square = value * value
    bend = jnp.tanh(GELU_A * value * (1.0 + GELU_B * square))
    slope = 0.5 * (1.0 + bend) + 0.5 * value * (1.0 - bend * bend) * (
        GELU_A * (1.0 + 3.0 * GELU_B * square)
    )
    grad_upward[...] = (grad_active * slope).astype(BF16)

    @pl.when(step >= 2)
    def _():
        wait_all(leave(step - 2, slot))

    grad = mxu(second[...], grad_upward[...], TN).astype(BF16)
    grads[slot] = grad.reshape(grads.shape[1:])
    start_all(leave(step, slot))

    @pl.when(step == steps - 1)
    def _():
        wait_all(leave(step - 1, 1 - slot))
        wait_all(leave(step, slot))


def down_call(blocks, branch, second, upward, pieces):
    rows, width = second.shape
    inner = upward.shape[1]
    columns = inner // Z_PARTS
    grad = jax.ShapeDtypeStruct((2, 2, Z_PARTS, width // (Z_PARTS * PIECES), inner), BF16)
    return pl.pallas_call(
        down_kernel,
        grid=(Z_PARTS,),
        in_specs=[
            SMEM_SPEC,
            whole((rows, width)),
            whole((rows, width)),
            pl.BlockSpec((rows, columns), lambda j: (0, j)),
        ]
        + [HBM_SPEC] * 4,
        out_specs=[pl.BlockSpec((rows, columns), lambda j: (0, j)), HBM_SPEC, HBM_SPEC],
        out_shape=[jax.ShapeDtypeStruct((rows, inner), BF16), grad, grad],
        scratch_shapes=[
            pltpu.VMEM((Z_PARTS, columns, width), BF16),
            pltpu.VMEM((2, Z_PARTS, width // Z_PARTS, columns), BF16),
            pltpu.SemaphoreType.DMA((Z_PARTS, PIECES)),
            pltpu.SemaphoreType.DMA((2, PIECES)),
        ],
        compiler_params=params(),
        cost_estimate=pl.CostEstimate(
            flops=4 * rows * width * inner,
            bytes_accessed=4 * width * inner + 6 * rows * inner,
            transcendentals=rows * inner,
        ),
        name="downward",
    )(blocks, branch, second, upward, *pieces)


def result_kernel(blocks, length, middle, active, p0, p1, p2, p3, output, held, sums, sems):
    step = pl.program_id(0)
    steps = Z_PARTS
    pieces = (p0, p1, p2, p3)

    def copies(part):
        return part_copies(pieces, blocks, part, held.at[part], sems.at[part])

    @pl.when(step == 0)
    def _():
        for part in range(steps):
            start_all(copies(part))
        sums[...] = middle[...]

    for part in range(steps):

        @pl.when(step == part)
        def _():
            wait_all(copies(part))

    sums[...] += mxu(active[...], held[step])

    @pl.when(step == steps - 1)
    def _():
        valid = lax.broadcasted_iota(jnp.int32, (sums.shape[0], 1), 0) < length[0]
        output[...] = (sums[...] * valid.astype(F32)).astype(BF16)


def result_call(blocks, length, middle, active, pieces):
    rows, width = middle.shape
    inner = active.shape[1]
    columns = inner // Z_PARTS
    return pl.pallas_call(
        result_kernel,
        grid=(Z_PARTS,),
        in_specs=[
            SMEM_SPEC,
            SMEM_SPEC,
            whole((rows, width)),
            pl.BlockSpec((rows, columns), lambda j: (0, j)),
        ]
        + [HBM_SPEC] * 4,
        out_specs=whole((rows, width)),
        out_shape=jax.ShapeDtypeStruct((rows, width), BF16),
        scratch_shapes=[
            pltpu.VMEM((Z_PARTS, columns, width), BF16),
            pltpu.VMEM((rows, width), F32),
            pltpu.SemaphoreType.DMA((Z_PARTS, PIECES)),
        ],
        compiler_params=params(),
        cost_estimate=pl.CostEstimate(
            flops=2 * rows * width * inner, bytes_accessed=3 * width * inner, transcendentals=0
        ),
        name="result",
    )(blocks, length, middle, active, *pieces)


def middle_kernel(
    blocks, branch, middle, gains, grad_upward, u0, u1, u2, u3, p0, p1, p2, p3,
    grad_middle, grad_attn, grad_mixed, held, out_held, sums, sems, out_sems,
):
    step = pl.program_id(0)
    steps = Z_PARTS
    width = middle.shape[1]
    columns = grad_upward.shape[1]

    def copies(part):
        return piece_copies(
            (u0, u1, u2, u3), blocks, held.at[part], sems.at[part], pl.ds(part * columns, columns)
        )

    out_copies = piece_copies(
        (p0, p1, p2, p3), blocks, out_held, out_sems, pl.ds(3 * width, width)
    )

    @pl.when(step == 0)
    def _():
        for part in range(steps):
            start_all(copies(part))
        start_all(out_copies)
        sums[...] = jnp.zeros_like(sums)

    for part in range(steps):

        @pl.when(step == part)
        def _():
            wait_all(copies(part))

    sums[...] += mxu(grad_upward[...], flat(held[step]), NT)

    @pl.when(step == steps - 1)
    def _():
        rows = middle[...]
        inverse = inverse_rms(rows)
        normal = rows * inverse
        scaled = sums[...] * gains[1:2, :]
        mean = jnp.mean(scaled * normal, axis=-1, keepdims=True)
        result = branch[...].astype(F32) + inverse * (scaled - normal * mean)
        grad_middle[...] = result
        low = result.astype(BF16)
        grad_attn[...] = low
        wait_all(out_copies)
        grad_mixed[...] = mxu(low, flat(out_held[...]), NT).astype(BF16)


def middle_call(blocks, branch, middle, gains, grad_upward, up_pieces, pieces):
    rows, width = middle.shape
    inner = grad_upward.shape[1]
    columns = inner // Z_PARTS
    return pl.pallas_call(
        middle_kernel,
        grid=(Z_PARTS,),
        in_specs=[
            SMEM_SPEC,
            whole((rows, width)),
            whole((rows, width)),
            whole((8, width)),
            pl.BlockSpec((rows, columns), lambda j: (0, j)),
        ]
        + [HBM_SPEC] * 8,
        out_specs=[whole((rows, width))] * 3,
        out_shape=[
            jax.ShapeDtypeStruct((rows, width), F32),
            jax.ShapeDtypeStruct((rows, width), BF16),
            jax.ShapeDtypeStruct((rows, width), BF16),
        ],
        scratch_shapes=[
            pltpu.VMEM((Z_PARTS, Z_PARTS, width // Z_PARTS, columns), BF16),
            pltpu.VMEM((Z_PARTS, width // Z_PARTS, width), BF16),
            pltpu.VMEM((rows, width), F32),
            pltpu.SemaphoreType.DMA((Z_PARTS, PIECES)),
            pltpu.SemaphoreType.DMA((PIECES,)),
        ],
        compiler_params=params(),
        cost_estimate=pl.CostEstimate(
            flops=2 * rows * width * (inner + width),
            bytes_accessed=3 * width * inner,
            transcendentals=0,
        ),
        name="middle",
    )(blocks, branch, middle, gains, grad_upward, *up_pieces, *pieces)


def attend_back_kernel(length, queries, keys, values, log_totals, grads, grad_qkv, across):
    pair = pl.program_id(0)
    rows = queries.shape[0]
    bias = jnp.where(
        lax.broadcasted_iota(jnp.int32, (rows, 1), 0) < length[0], 0.0, -1e30
    ).astype(F32)
    lane = lax.broadcasted_iota(jnp.int32, (rows, LANES), 1)

    @pl.when(pair == 0)
    def _():
        across[...] = log_totals[...].T

    query, key, value, grad = queries[...], keys[...], values[...], grads[...]
    parts = []
    for half in range(2):
        mine = (lane < HEAD_DIM) == (half == 0)
        query_half = jnp.where(mine, query, jnp.zeros_like(query))
        grad_half = jnp.where(mine, grad, jnp.zeros_like(grad))
        scores = mxu(key, query_half, NT) + bias
        chance = jnp.exp(scores - across[pl.ds(2 * pair + half, 1), :])
        grad_value = mxu(chance.astype(BF16), grad)
        grad_chance = mxu(value, grad_half, NT)
        mean = jnp.sum(chance * grad_chance, axis=0, keepdims=True)
        grad_scores = (chance * (grad_chance - mean)).astype(BF16)
        grad_key = mxu(grad_scores, query)
        grad_query = mxu(grad_scores, key, TN) * FACTOR
        parts.append((grad_query, grad_key, grad_value))
    for place in range(3):
        grad_qkv[place] = jnp.where(lane < HEAD_DIM, parts[0][place], parts[1][place]).astype(BF16)


def attend_back_call(length, qkv, log_totals, grad_mixed):
    rows, width = grad_mixed.shape
    pairs = width // LANES
    return pl.pallas_call(
        attend_back_kernel,
        grid=(pairs,),
        in_specs=[
            SMEM_SPEC,
            pl.BlockSpec((rows, LANES), lambda h: (0, h)),
            pl.BlockSpec((rows, LANES), lambda h: (0, pairs + h)),
            pl.BlockSpec((rows, LANES), lambda h: (0, 2 * pairs + h)),
            whole((rows, LANES)),
            pl.BlockSpec((rows, LANES), lambda h: (0, h)),
        ],
        out_specs=pl.BlockSpec((3, rows, LANES), lambda h: (0, 0, h)),
        out_shape=jax.ShapeDtypeStruct((3, rows, width), BF16),
        scratch_shapes=[pltpu.VMEM((LANES, rows), F32)],
        compiler_params=params(),
        cost_estimate=pl.CostEstimate(
            flops=40 * rows * rows * width,
            bytes_accessed=14 * rows * width,
            transcendentals=HEADS * rows * rows,
        ),
        name="attend_back",
    )(length, qkv, qkv, qkv, log_totals, grad_mixed)


def attn_grad_kernel(
    blocks, hidden, mixed, grad_qkv, grad_attn, own, other, grads, grad_sems
):
    step = pl.program_id(0)
    steps = 4
    slot = lax.rem(step, 2)
    width = hidden.shape[1]

    def leave(part, at):
        start = pl.multiple_of(part * width, width)
        return grad_copies(
            grads.at[at], (own, other), blocks, pl.ds(start, width), grad_sems.at[at]
        )

    @pl.when(step >= 2)
    def _():
        wait_all(leave(step - 2, slot))

    @pl.when(step < 3)
    def _():
        grad = mxu(hidden[...], grad_qkv[0], TN).astype(BF16)
        grads[slot] = grad.reshape(grads.shape[1:])

    @pl.when(step == 3)
    def _():
        grad = mxu(mixed[...], grad_attn[...], TN).astype(BF16)
        grads[slot] = grad.reshape(grads.shape[1:])

    start_all(leave(step, slot))

    @pl.when(step == steps - 1)
    def _():
        wait_all(leave(step - 1, 1 - slot))
        wait_all(leave(step, slot))


def attn_grad_call(blocks, hidden, mixed, grad_qkv, grad_attn):
    rows, width = hidden.shape
    grad = jax.ShapeDtypeStruct((2, 2, Z_PARTS, width // (Z_PARTS * PIECES), 4 * width), BF16)
    return pl.pallas_call(
        attn_grad_kernel,
        grid=(4,),
        in_specs=[
            SMEM_SPEC,
            whole((rows, width)),
            whole((rows, width)),
            pl.BlockSpec((1, rows, width), lambda j: (jnp.minimum(j, 2), 0, 0)),
            whole((rows, width)),
        ],
        out_specs=[HBM_SPEC, HBM_SPEC],
        out_shape=[grad, grad],
        scratch_shapes=[
            pltpu.VMEM((2, Z_PARTS, width // Z_PARTS, width), BF16),
            pltpu.SemaphoreType.DMA((2, PIECES)),
        ],
        compiler_params=params(),
        cost_estimate=pl.CostEstimate(
            flops=8 * rows * width * width,
            bytes_accessed=8 * width * width + 12 * rows * width,
            transcendentals=0,
        ),
        name="attn_grads",
    )(blocks, hidden, mixed, grad_qkv, grad_attn)


def frames_kernel(
    blocks, frames, gains, grad_middle, grad_qkv, p0, p1, p2, p3, grad_frames, held, sums, sems
):
    step = pl.program_id(0)
    width = frames.shape[1]

    def copies(part):
        return piece_copies(
            (p0, p1, p2, p3), blocks, held.at[part], sems.at[part], pl.ds(part * width, width)
        )

    @pl.when(step == 0)
    def _():
        for part in range(3):
            start_all(copies(part))
        sums[...] = jnp.zeros_like(sums)

    for part in range(3):

        @pl.when(step == part)
        def _():
            wait_all(copies(part))

    sums[...] += mxu(grad_qkv[0], flat(held[step]), NT)

    @pl.when(step == 2)
    def _():
        rows = frames[...].astype(F32)
        inverse = inverse_rms(rows)
        normal = rows * inverse
        scaled = sums[...] * gains[0:1, :]
        mean = jnp.mean(scaled * normal, axis=-1, keepdims=True)
        grad_frames[...] = grad_middle[...] + inverse * (scaled - normal * mean)


def frames_call(blocks, frames, gains, grad_middle, grad_qkv, pieces):
    rows, width = frames.shape
    return pl.pallas_call(
        frames_kernel,
        grid=(3,),
        in_specs=[
            SMEM_SPEC,
            whole((rows, width)),
            whole((8, width)),
            whole((rows, width)),
            pl.BlockSpec((1, rows, width), lambda j: (j, 0, 0)),
        ]
        + [HBM_SPEC] * 4,
        out_specs=whole((rows, width)),
        out_shape=jax.ShapeDtypeStruct((rows, width), F32),
        scratch_shapes=[
            pltpu.VMEM((3, Z_PARTS, width // Z_PARTS, width), BF16),
            pltpu.VMEM((rows, width), F32),
            pltpu.SemaphoreType.DMA((3, PIECES)),
        ],
        compiler_params=params(),
        cost_estimate=pl.CostEstimate(
            flops=6 * rows * width * width, bytes_accessed=10 * width * width, transcendentals=0
        ),
        name="frames_back",
    )(blocks, frames, gains, grad_middle, grad_qkv, *pieces)


def on_device(
    sizes, frames, lengths, w_query, w_key, w_value, w_out, w_up, w_down,
    gain_attn, gain_mlp, cotangent,
):
    width = frames.shape[-1]
    blocks = piece_blocks(sizes)
    rows_in = frames[0]
    valid = lax.broadcasted_iota(jnp.int32, (rows_in.shape[0], 1), 0) < lengths[0]
    branch = jnp.where(valid, cotangent[0], jnp.zeros_like(cotangent[0]))
    gains = jnp.pad(jnp.stack((gain_attn, gain_mlp), axis=1), ((0, 0), (0, LANES - 2)))
    attn = jnp.concatenate((w_query, w_key, w_value, w_out, gains), axis=1)
    attn_pieces = gather_pieces(attn, sizes)
    up_pieces = gather_pieces(w_up, sizes)
    down_pieces = gather_pieces(w_down, sizes)

    hidden, qkv, gain_rows = qkv_call(blocks, rows_in, attn_pieces)
    mixed, log_totals = attend_call(lengths, qkv)
    middle, second = out_call(blocks, rows_in, mixed, gain_rows, attn_pieces)
    upward, active, down_own, down_other = up_call(blocks, second, branch, up_pieces)
    down_rows = scatter_pieces(down_own, down_other, sizes)
    grad_upward, up_own, up_other = down_call(blocks, branch, second, upward, down_pieces)
    up_rows = scatter_pieces(up_own, up_other, sizes)
    grad_middle, grad_attn, grad_mixed = middle_call(
        blocks, branch, middle, gain_rows, grad_upward, up_pieces, attn_pieces
    )
    grad_qkv = attend_back_call(lengths, qkv, log_totals, grad_mixed)
    attn_own, attn_other = attn_grad_call(blocks, hidden, mixed, grad_qkv, grad_attn)
    attn_rows = scatter_pieces(attn_own, attn_other, sizes)
    output = result_call(blocks, lengths, middle, active, down_pieces)
    grad_frames = frames_call(blocks, rows_in, gain_rows, grad_middle, grad_qkv, attn_pieces)

    grad_query = attn_rows[:, :width]
    grad_key = attn_rows[:, width : 2 * width]
    grad_value = attn_rows[:, 2 * width : 3 * width]
    grad_out = attn_rows[:, 3 * width :]
    gain_one = (
        jnp.sum(w_query.astype(F32) * grad_query, axis=1)
        + jnp.sum(w_key.astype(F32) * grad_key, axis=1)
        + jnp.sum(w_value.astype(F32) * grad_value, axis=1)
    ) / gain_attn.astype(F32)
    gain_two = jnp.sum(w_up.astype(F32) * up_rows, axis=1) / gain_mlp.astype(F32)
    return (
        output[None], grad_frames[None], grad_query, grad_key, grad_value, grad_out,
        up_rows, down_rows, gain_one, gain_two,
    )


def solution(mesh):
    wide, narrow = mesh.shape["wide"], mesh.shape["narrow"]
    y = 1
    while 4 * y * y <= wide:
        y *= 2
    sizes = {"z": wide // y, "y": y, "x": narrow // 2, "c": 2}
    fine = Mesh(mesh.devices.reshape(tuple(sizes[name] for name in ALL)), ALL)
    split = P(ALL)
    return jax.shard_map(
        functools.partial(on_device, sizes),
        mesh=fine,
        in_specs=(split,) * 11,
        out_specs=(split,) * 10,
        check_vma=False,
    )
```

```python
import functools

import jax
import jax.numpy as jnp
import numpy as np
from jax import lax
from jax.experimental import pallas as pl
from jax.experimental.pallas import tpu as pltpu
from jax.sharding import Mesh, PartitionSpec as P

HEADS = 16
HEAD_DIM = 64
EPSILON = 1e-06
FACTOR = HEAD_DIM ** (-0.5)
LANES = 128
CHUNK = 1024
Z_PARTS = 4
PIECES = 8
ALL = ("z", "y", "x", "c")
PLANE = ("y", "x", "c")
SWAP = [(0, 1), (1, 0)]
VMEM_MIB = {"forward": 32, "upward": 26, "downward": 26, "backward": 46, "result": 20, "frames": 20}
F32 = jnp.float32
BF16 = jnp.bfloat16
GELU_A = 0.7978845608028654
GELU_B = 0.044715

NN = (((1,), (0,)), ((), ()))
NT = (((1,), (1,)), ((), ()))
TN = (((0,), (0,)), ((), ()))


def mxu(left, right, dims=NN):
    return lax.dot_general(left, right, dims, preferred_element_type=F32)


def plane_pairs(step):
    pairs = []
    for y in range(2):
        for x in range(2):
            for c in range(2):
                flip_y = (c == 0) == (step == 1)
                to = (1 - y, x, c) if flip_y else (y, 1 - x, c)
                pairs.append(((y * 2 + x) * 2 + c, (to[0] * 2 + to[1]) * 2 + to[2]))
    return pairs


def is_plane(sizes):
    return sizes["x"] == 2 and sizes["y"] == 2 and sizes["c"] == 2 and sizes["z"] == Z_PARTS


def piece_blocks(sizes):
    piece = jnp.arange(PIECES, dtype=jnp.int32)
    if not is_plane(sizes):
        return piece
    own = (piece >> 2) & 1
    first = (piece >> 1) & 1
    second = piece & 1
    core = lax.axis_index("c") ^ own
    on_y = jnp.where(core == 0, first, second)
    on_x = jnp.where(core == 0, second, first)
    y = lax.axis_index("y") ^ on_y
    x = lax.axis_index("x") ^ on_x
    return ((y * 2 + x) * 2 + core).astype(jnp.int32)


def after(value, *others):
    return lax.optimization_barrier((value,) + others)[0]


def first_hop(value):
    return lax.ppermute(value, PLANE, plane_pairs(1))


def second_hop(value):
    return lax.ppermute(value, PLANE, plane_pairs(2))


def across_cores(value):
    return lax.ppermute(value, "c", SWAP)


def gather_column(shard):
    return lax.all_gather(shard, "z", axis=0, tiled=False)


def gather_whole(shard):
    full = lax.all_gather(shard, ALL, axis=0, tiled=True)
    full = full.reshape(Z_PARTS, PIECES, full.shape[0] // (Z_PARTS * PIECES), full.shape[1])
    full = full.transpose(1, 0, 2, 3).reshape((2, 2, 2, Z_PARTS) + full.shape[2:])
    return (full[0, :, 0], full[0, :, 1], full[1, :, 0], full[1, :, 1])


def total(*parts):
    result = parts[0].astype(F32)
    for part in parts[1:]:
        result = result + part.astype(F32)
    return result


def low_total(*parts):
    return total(*parts).astype(BF16)


def scatter_column(mine):
    return lax.psum_scatter(mine, "z", scatter_dimension=0, tiled=False).astype(F32)


def scatter_whole(parts):
    full = jnp.stack(parts)
    full = full.reshape((PIECES,) + full.shape[2:]).transpose(1, 0, 2, 3)
    full = full.reshape(-1, full.shape[-1])
    return lax.psum_scatter(full, ALL, scatter_dimension=0, tiled=True).astype(F32)


COST_SHARE = 0.02


def cost(flops, bytes_accessed, transcendentals):
    return pl.CostEstimate(
        flops=int(COST_SHARE * flops), bytes_accessed=int(COST_SHARE * bytes_accessed),
        transcendentals=int(COST_SHARE * transcendentals),
    )


def params(name):
    return pltpu.CompilerParams(vmem_limit_bytes=VMEM_MIB[name] << 20)


HBM_SPEC = pl.BlockSpec(memory_space=pl.ANY)
SMEM_SPEC = pl.BlockSpec(memory_space=pltpu.SMEM)


def whole(shape):
    return pl.BlockSpec(
        shape, lambda *_: (0,) * len(shape), pipeline_mode=pl.Buffered(1)
    )


def piece_copies(pieces, blocks, held, sems, columns):
    rows = pieces[0].shape[2]
    copies = []
    for piece in range(PIECES):
        own, first, second = piece >> 2, (piece >> 1) & 1, piece & 1
        source = pieces[2 * own + second].at[first, :, :, columns]
        start = pl.multiple_of(blocks[piece] * rows, rows)
        copies.append(
            pltpu.make_async_copy(source, held.at[:, pl.ds(start, rows), :], sems.at[piece])
        )
    return copies


def packed_copies(pieces, blocks, part, held, sems):
    rows = held.shape[1] // PIECES
    copies = []
    for piece in range(PIECES):
        own, first, second = piece >> 2, (piece >> 1) & 1, piece & 1
        source = pieces[2 * own + second].at[first, :, pl.ds(part * rows, rows), :]
        start = pl.multiple_of(blocks[piece] * rows, rows)
        copies.append(
            pltpu.make_async_copy(source, held.at[:, pl.ds(start, rows), :], sems.at[piece])
        )
    return copies


def part_copies(pieces, blocks, part, held, sems):
    rows = pieces[0].shape[2]
    copies = []
    for piece in range(PIECES):
        own, first, second = piece >> 2, (piece >> 1) & 1, piece & 1
        source = pieces[2 * own + second].at[part, first]
        start = pl.multiple_of(blocks[piece] * rows, rows)
        copies.append(
            pltpu.make_async_copy(source, held.at[pl.ds(start, rows), :], sems.at[piece])
        )
    return copies


def grad_copies(held, outs, blocks, columns, sems):
    rows = outs[0].shape[2]
    copies = []
    for piece in range(PIECES):
        own, first, second = piece >> 2, (piece >> 1) & 1, piece & 1
        target = outs[2 * own + first].at[second, :, :, columns]
        start = pl.multiple_of(blocks[piece] * rows, rows)
        copies.append(
            pltpu.make_async_copy(held.at[:, pl.ds(start, rows), :], target, sems.at[piece])
        )
    return copies


def grad_part_copies(held, outs, blocks, part, sems):
    rows = outs[0].shape[2]
    copies = []
    for piece in range(PIECES):
        own, first, second = piece >> 2, (piece >> 1) & 1, piece & 1
        target = outs[2 * own + first].at[second, part]
        start = pl.multiple_of(blocks[piece] * rows, rows)
        copies.append(
            pltpu.make_async_copy(held.at[pl.ds(start, rows), :], target, sems.at[piece])
        )
    return copies


def start_all(copies):
    for copy in copies:
        copy.start()


def wait_all(copies):
    for copy in copies:
        copy.wait()


def prefetch(step, steps, copies):
    @pl.when(step == 0)
    def _():
        start_all(copies(0))
        start_all(copies(1))

    for part in range(steps):

        @pl.when(step == part)
        def _():
            if part + 2 < steps:
                start_all(copies(part + 2))
            wait_all(copies(part))


def flat(block):
    return block.reshape(block.shape[0] * block.shape[1], block.shape[2])


def inverse_rms(rows):
    return lax.rsqrt(jnp.mean(rows * rows, axis=-1, keepdims=True) + EPSILON)


def store(source, target, sem):
    return pltpu.make_async_copy(source, target, sem)


def lane_pair(pair):
    return pl.ds(pl.multiple_of(pair * LANES, LANES), LANES)


def forward_kernel(
    blocks, length, frames, p0, p1, p2, p3,
    hidden_out, qkv_out, mixed_out, gains, log_totals, middle, second,
    held, gain_held, hidden, qkv, mixed, sems, out_sems,
):
    pieces = (p0, p1, p2, p3)
    rows, width = frames.shape
    gain_copies = piece_copies(pieces, blocks, gain_held, sems.at[4], pl.ds(4 * width, LANES))
    copies = [
        piece_copies(pieces, blocks, held.at[part], sems.at[part], pl.ds(part * width, width))
        for part in range(4)
    ]
    start_all(gain_copies)
    for part in range(4):
        start_all(copies[part])
    value = frames[...].astype(F32)
    normal = value * inverse_rms(value)
    wait_all(gain_copies)
    across = flat(gain_held[...]).astype(F32).T
    gains[...] = across[:8]
    hidden[...] = (normal * across[0:1]).astype(BF16)
    leaving = [store(hidden, hidden_out, out_sems.at[3])]
    leaving[0].start()
    for part in range(3):
        wait_all(copies[part])
        result = mxu(hidden[...], flat(held[part])).astype(BF16)
        if part == 0:
            result = (result.astype(F32) * FACTOR).astype(BF16)
        qkv[part] = result
        leaving.append(store(qkv.at[part], qkv_out.at[part], out_sems.at[part]))
        leaving[-1].start()

    bias = jnp.where(
        lax.broadcasted_iota(jnp.int32, (rows, 1), 0) < length[0], 0.0, -1e30
    ).astype(F32)
    lane = lax.broadcasted_iota(jnp.int32, (rows, LANES), 1)

    @pl.loop(0, width // LANES)
    def _(pair):
        here = lane_pair(pair)
        query, key, value = qkv[0, :, here], qkv[1, :, here], qkv[2, :, here]
        outs = []
        for half in range(2):
            mine = (lane < HEAD_DIM) == (half == 0)
            scores = mxu(key, jnp.where(mine, query, jnp.zeros_like(query)), NT) + bias
            peak = jnp.max(scores, axis=0, keepdims=True)
            expon = jnp.exp(scores - peak)
            sums = jnp.sum(expon, axis=0, keepdims=True)
            log_totals[pl.ds(2 * pair + half, 1), :] = peak + jnp.log(sums)
            shares = (expon * (1.0 / sums)).astype(BF16)
            outs.append(mxu(shares, value, TN))
        mixed[:, here] = jnp.where(lane < HEAD_DIM, outs[0], outs[1]).astype(BF16)

    leaving.append(store(mixed, mixed_out, out_sems.at[4]))
    leaving[-1].start()
    wait_all(copies[3])
    result = frames[...].astype(F32) + mxu(mixed[...], flat(held[3]))
    middle[...] = result
    second[...] = (result * inverse_rms(result) * gains[1:2, :]).astype(BF16)
    wait_all(leaving)


def forward_call(blocks, length, frames, pieces):
    rows, width = frames.shape
    full = jax.ShapeDtypeStruct((rows, width), BF16)
    return pl.pallas_call(
        forward_kernel,
        grid=(1,),
        in_specs=[SMEM_SPEC, SMEM_SPEC, whole((rows, width))] + [HBM_SPEC] * 4,
        out_specs=[HBM_SPEC] * 3
        + [whole((8, width)), whole((HEADS, rows)), whole((rows, width)), whole((rows, width))],
        out_shape=[
            full,
            jax.ShapeDtypeStruct((3, rows, width), BF16),
            full,
            jax.ShapeDtypeStruct((8, width), F32),
            jax.ShapeDtypeStruct((HEADS, rows), F32),
            jax.ShapeDtypeStruct((rows, width), F32),
            full,
        ],
        scratch_shapes=[
            pltpu.VMEM((4, Z_PARTS, width // Z_PARTS, width), BF16),
            pltpu.VMEM((Z_PARTS, width // Z_PARTS, LANES), BF16),
            pltpu.VMEM((rows, width), BF16),
            pltpu.VMEM((3, rows, width), BF16),
            pltpu.VMEM((rows, width), BF16),
            pltpu.SemaphoreType.DMA((5, PIECES)),
            pltpu.SemaphoreType.DMA((5,)),
        ],
        compiler_params=params("forward"),
        cost_estimate=cost(10 * rows * width * width, 16 * width * width, rows * rows),
        name="forward",
    )(blocks, length, frames, *pieces)


def up_kernel(
    blocks, second, branch, p0, p1, p2, p3, slope, active, g0, g1, g2, g3,
    held, grads, sems, grad_sems,
):
    step = pl.program_id(0)
    steps = Z_PARTS
    slot = lax.rem(step, 2)
    pieces = (p0, p1, p2, p3)

    def copies(part):
        return packed_copies(pieces, blocks, part, held.at[part], sems.at[part])

    def leave(part, at):
        return grad_part_copies(grads.at[at], (g0, g1, g2, g3), blocks, part, grad_sems.at[at])

    prefetch(step, steps, copies)

    @pl.when(step >= 2)
    def _():
        wait_all(leave(step - 2, slot))

    columns = held.shape[3]
    chunk = min(columns, CHUNK)
    for at in range(0, columns, chunk):
        here = pl.ds(at, chunk)
        weight = held[step, :, :, here]
        value = mxu(second[...], flat(weight))
        square = value * value
        bend = jnp.tanh(GELU_A * value * (1.0 + GELU_B * square))
        share = 0.5 * (1.0 + bend)
        low = (value * share).astype(BF16)
        active[:, here] = low
        slope[:, here] = (
            share
            + 0.5 * value * (1.0 - bend * bend) * (GELU_A * (1.0 + 3.0 * GELU_B * square))
        ).astype(BF16)
        grads[slot, here, :] = mxu(low, branch[...], TN).astype(BF16)
    start_all(leave(step, slot))

    @pl.when(step == steps - 1)
    def _():
        wait_all(leave(step - 1, 1 - slot))
        wait_all(leave(step, slot))


def up_call(blocks, second, branch, pieces):
    rows, width = second.shape
    inner = pieces[0].shape[2] * pieces[0].shape[3] * PIECES * Z_PARTS // width
    columns = inner // Z_PARTS
    part_rows = inner // (Z_PARTS * PIECES)
    grad = jax.ShapeDtypeStruct((2, Z_PARTS, part_rows, width), BF16)
    return pl.pallas_call(
        up_kernel,
        grid=(Z_PARTS,),
        in_specs=[SMEM_SPEC, whole((rows, width)), whole((rows, width))] + [HBM_SPEC] * 4,
        out_specs=[
            pl.BlockSpec((rows, columns), lambda j: (0, j)),
            pl.BlockSpec((rows, columns), lambda j: (0, j)),
        ]
        + [HBM_SPEC] * 4,
        out_shape=[
            jax.ShapeDtypeStruct((rows, inner), BF16),
            jax.ShapeDtypeStruct((rows, inner), BF16),
        ]
        + [grad] * 4,
        scratch_shapes=[
            pltpu.VMEM((Z_PARTS, Z_PARTS, width // Z_PARTS, columns), BF16),
            pltpu.VMEM((2, columns, width), BF16),
            pltpu.SemaphoreType.DMA((Z_PARTS, PIECES)),
            pltpu.SemaphoreType.DMA((2, PIECES)),
        ],
        compiler_params=params("upward"),
        cost_estimate=cost(
            flops=4 * rows * width * inner,
            bytes_accessed=4 * width * inner + 6 * rows * inner,
            transcendentals=rows * inner,
        ),
        name="upward",
    )(blocks, second, branch, *pieces)


def down_kernel(
    blocks, branch, second, slope, p0, p1, p2, p3, grad_upward, g0, g1, g2, g3,
    held, grads, sems, grad_sems,
):
    step = pl.program_id(0)
    steps = Z_PARTS
    slot = lax.rem(step, 2)
    pieces = (p0, p1, p2, p3)
    columns = slope.shape[1]

    def copies(part):
        return part_copies(pieces, blocks, part, held.at[part], sems.at[part])

    def leave(part, at):
        start = pl.multiple_of(part * columns, columns)
        return grad_copies(
            grads.at[at], (g0, g1, g2, g3), blocks, pl.ds(start, columns), grad_sems.at[at]
        )

    prefetch(step, steps, copies)

    @pl.when(step >= 2)
    def _():
        wait_all(leave(step - 2, slot))

    chunk = min(columns, CHUNK)
    for at in range(0, columns, chunk):
        here = pl.ds(at, chunk)
        value = mxu(branch[...], held[step, here, :], NT)
        low = (value * slope[:, here].astype(F32)).astype(BF16)
        grad_upward[:, here] = low
        grad = mxu(second[...], low, TN).astype(BF16)
        grads[slot, :, :, here] = grad.reshape(grads.shape[1:3] + (chunk,))
    start_all(leave(step, slot))

    @pl.when(step == steps - 1)
    def _():
        wait_all(leave(step - 1, 1 - slot))
        wait_all(leave(step, slot))


def down_call(blocks, branch, second, slope, pieces):
    rows, width = second.shape
    inner = slope.shape[1]
    columns = inner // Z_PARTS
    grad = jax.ShapeDtypeStruct((2, Z_PARTS, width // (Z_PARTS * PIECES), inner), BF16)
    return pl.pallas_call(
        down_kernel,
        grid=(Z_PARTS,),
        in_specs=[
            SMEM_SPEC,
            whole((rows, width)),
            whole((rows, width)),
            pl.BlockSpec((rows, columns), lambda j: (0, j)),
        ]
        + [HBM_SPEC] * 4,
        out_specs=[pl.BlockSpec((rows, columns), lambda j: (0, j))] + [HBM_SPEC] * 4,
        out_shape=[jax.ShapeDtypeStruct((rows, inner), BF16)] + [grad] * 4,
        scratch_shapes=[
            pltpu.VMEM((Z_PARTS, columns, width), BF16),
            pltpu.VMEM((2, Z_PARTS, width // Z_PARTS, columns), BF16),
            pltpu.SemaphoreType.DMA((Z_PARTS, PIECES)),
            pltpu.SemaphoreType.DMA((2, PIECES)),
        ],
        compiler_params=params("downward"),
        cost_estimate=cost(
            flops=4 * rows * width * inner,
            bytes_accessed=4 * width * inner + 6 * rows * inner,
            transcendentals=rows * inner,
        ),
        name="downward",
    )(blocks, branch, second, slope, *pieces)


def result_kernel(blocks, length, middle, active, p0, p1, p2, p3, output, held, sums, sems):
    step = pl.program_id(0)
    steps = Z_PARTS
    pieces = (p0, p1, p2, p3)

    def copies(part):
        return part_copies(pieces, blocks, part, held.at[part], sems.at[part])

    @pl.when(step == 0)
    def _():
        for part in range(steps):
            start_all(copies(part))
        sums[...] = middle[...]

    for part in range(steps):

        @pl.when(step == part)
        def _():
            wait_all(copies(part))

    sums[...] += mxu(active[...], held[step])

    @pl.when(step == steps - 1)
    def _():
        valid = lax.broadcasted_iota(jnp.int32, (sums.shape[0], 1), 0) < length[0]
        output[...] = (sums[...] * valid.astype(F32)).astype(BF16)


def result_call(blocks, length, middle, active, pieces):
    rows, width = middle.shape
    inner = active.shape[1]
    columns = inner // Z_PARTS
    return pl.pallas_call(
        result_kernel,
        grid=(Z_PARTS,),
        in_specs=[
            SMEM_SPEC,
            SMEM_SPEC,
            whole((rows, width)),
            pl.BlockSpec((rows, columns), lambda j: (0, j)),
        ]
        + [HBM_SPEC] * 4,
        out_specs=whole((rows, width)),
        out_shape=jax.ShapeDtypeStruct((rows, width), BF16),
        scratch_shapes=[
            pltpu.VMEM((Z_PARTS, columns, width), BF16),
            pltpu.VMEM((rows, width), F32),
            pltpu.SemaphoreType.DMA((Z_PARTS, PIECES)),
        ],
        compiler_params=params("result"),
        cost_estimate=cost(
            flops=2 * rows * width * inner, bytes_accessed=3 * width * inner, transcendentals=0
        ),
        name="result",
    )(blocks, length, middle, active, *pieces)


def backward_kernel(
    blocks, length, branch, middle, gains, log_totals, grad_upward, qkv_in, hidden_in, mixed_in,
    u0, u1, u2, u3, p0, p1, p2, p3,
    grad_middle, grad_qkv_out, g0, g1, g2, g3,
    held, out_held, wide, qkv, hidden, mixed, sums, grad_attn, grad_mixed, grad_qkv, grads,
    sems, out_sems, wide_sems, in_sems, leave_sems, grad_sems,
):
    steps = Z_PARTS
    rows, width = middle.shape
    columns = wide.shape[2]
    outs = (g0, g1, g2, g3)
    copies, wide_copies = [], []
    for part in range(steps):
        copies.append(
            packed_copies((u0, u1, u2, u3), blocks, part, held.at[part], sems.at[part])
        )
        wide_copies.append(
            store(
                grad_upward.at[:, pl.ds(part * columns, columns)],
                wide.at[part],
                wide_sems.at[part],
            )
        )
        start_all(copies[part])
        wide_copies[part].start()
    out_copies = piece_copies(
        (p0, p1, p2, p3), blocks, out_held, out_sems, pl.ds(3 * width, width)
    )
    entering = [
        store(qkv_in, qkv, in_sems.at[0]),
        store(hidden_in, hidden, in_sems.at[1]),
        store(mixed_in, mixed, in_sems.at[2]),
    ]
    start_all(out_copies)
    start_all(entering)

    for part in range(steps):
        wide_copies[part].wait()
        wait_all(copies[part])
        term = mxu(wide[part], flat(held[part]), NT)
        if part == 0:
            sums[...] = term
        else:
            sums[...] += term

    value = middle[...]
    inverse = inverse_rms(value)
    normal = value * inverse
    scaled = sums[...] * gains[1:2, :]
    mean = jnp.mean(scaled * normal, axis=-1, keepdims=True)
    result = branch[...].astype(F32) + inverse * (scaled - normal * mean)
    sums[...] = result
    leaving = [store(sums, grad_middle, leave_sems.at[0])]
    leaving[0].start()
    grad_attn[...] = result.astype(BF16)
    wait_all(out_copies)
    grad_mixed[...] = mxu(grad_attn[...], flat(out_held[...]), NT).astype(BF16)
    wait_all(entering)

    bias = jnp.where(
        lax.broadcasted_iota(jnp.int32, (rows, 1), 0) < length[0], 0.0, -1e30
    ).astype(F32)
    lane = lax.broadcasted_iota(jnp.int32, (rows, LANES), 1)

    @pl.loop(0, width // LANES)
    def _(pair):
        here = lane_pair(pair)
        query, key, value = qkv[0, :, here], qkv[1, :, here], qkv[2, :, here]
        grad = grad_mixed[:, here]
        parts = []
        for half in range(2):
            mine = (lane < HEAD_DIM) == (half == 0)
            scores = mxu(key, jnp.where(mine, query, jnp.zeros_like(query)), NT) + bias
            chance = jnp.exp(scores - log_totals[pl.ds(2 * pair + half, 1), :])
            grad_value = mxu(chance.astype(BF16), grad)
            grad_chance = mxu(value, jnp.where(mine, grad, jnp.zeros_like(grad)), NT)
            mean = jnp.sum(chance * grad_chance, axis=0, keepdims=True)
            grad_scores = (chance * (grad_chance - mean)).astype(BF16)
            grad_key = mxu(grad_scores, query)
            grad_query = mxu(grad_scores, key, TN) * FACTOR
            parts.append((grad_query, grad_key, grad_value))
        for place in range(3):
            grad_qkv[place, :, here] = jnp.where(
                lane < HEAD_DIM, parts[0][place], parts[1][place]
            ).astype(BF16)

    leaving.append(store(grad_qkv, grad_qkv_out, leave_sems.at[1]))
    leaving[-1].start()
    pending = []
    for part in range(4):
        slot = part % 2
        if part >= 2:
            wait_all(pending[part - 2])
        left, right = (mixed, grad_attn[...]) if part == 3 else (hidden, grad_qkv[part])
        grad = mxu(left[...], right, TN).astype(BF16)
        grads[slot] = grad.reshape(grads.shape[1:])
        pending.append(
            grad_copies(
                grads.at[slot], outs, blocks, pl.ds(part * width, width), grad_sems.at[slot]
            )
        )
        start_all(pending[part])
    wait_all(pending[2])
    wait_all(pending[3])
    wait_all(leaving)


def backward_call(
    blocks, length, branch, middle, gains, log_totals, grad_upward, qkv, hidden, mixed,
    up_pieces, pieces,
):
    rows, width = middle.shape
    inner = grad_upward.shape[1]
    columns = inner // Z_PARTS
    grad = jax.ShapeDtypeStruct((2, Z_PARTS, width // (Z_PARTS * PIECES), 4 * width), BF16)
    full = pltpu.VMEM((rows, width), BF16)
    return pl.pallas_call(
        backward_kernel,
        grid=(1,),
        in_specs=[
            SMEM_SPEC,
            SMEM_SPEC,
            whole((rows, width)),
            whole((rows, width)),
            whole((8, width)),
            whole((HEADS, rows)),
        ]
        + [HBM_SPEC] * 12,
        out_specs=[HBM_SPEC] * 6,
        out_shape=[
            jax.ShapeDtypeStruct((rows, width), F32),
            jax.ShapeDtypeStruct((3, rows, width), BF16),
        ]
        + [grad] * 4,
        scratch_shapes=[
            pltpu.VMEM((Z_PARTS, Z_PARTS, width // Z_PARTS, columns), BF16),
            pltpu.VMEM((Z_PARTS, width // Z_PARTS, width), BF16),
            pltpu.VMEM((Z_PARTS, rows, columns), BF16),
            pltpu.VMEM((3, rows, width), BF16),
            full,
            full,
            pltpu.VMEM((rows, width), F32),
            full,
            full,
            pltpu.VMEM((3, rows, width), BF16),
            pltpu.VMEM((2, Z_PARTS, width // Z_PARTS, width), BF16),
            pltpu.SemaphoreType.DMA((Z_PARTS, PIECES)),
            pltpu.SemaphoreType.DMA((PIECES,)),
            pltpu.SemaphoreType.DMA((Z_PARTS,)),
            pltpu.SemaphoreType.DMA((3,)),
            pltpu.SemaphoreType.DMA((2,)),
            pltpu.SemaphoreType.DMA((2, PIECES)),
        ],
        compiler_params=params("backward"),
        cost_estimate=cost(20 * rows * width * width, 40 * width * width, rows * rows),
        name="backward",
    )(
        blocks, length, branch, middle, gains, log_totals, grad_upward, qkv, hidden, mixed,
        *up_pieces, *pieces,
    )


def frames_kernel(
    blocks, frames, gains, grad_middle, grad_qkv, p0, p1, p2, p3, grad_frames, held, sums, sems
):
    step = pl.program_id(0)
    width = frames.shape[1]

    def copies(part):
        return piece_copies(
            (p0, p1, p2, p3), blocks, held.at[part], sems.at[part], pl.ds(part * width, width)
        )

    @pl.when(step == 0)
    def _():
        for part in range(3):
            start_all(copies(part))
        sums[...] = jnp.zeros_like(sums)

    for part in range(3):

        @pl.when(step == part)
        def _():
            wait_all(copies(part))

    sums[...] += mxu(grad_qkv[0], flat(held[step]), NT)

    @pl.when(step == 2)
    def _():
        rows = frames[...].astype(F32)
        inverse = inverse_rms(rows)
        normal = rows * inverse
        scaled = sums[...] * gains[0:1, :]
        mean = jnp.mean(scaled * normal, axis=-1, keepdims=True)
        grad_frames[...] = grad_middle[...] + inverse * (scaled - normal * mean)


def frames_call(blocks, frames, gains, grad_middle, grad_qkv, pieces):
    rows, width = frames.shape
    return pl.pallas_call(
        frames_kernel,
        grid=(3,),
        in_specs=[
            SMEM_SPEC,
            whole((rows, width)),
            whole((8, width)),
            whole((rows, width)),
            pl.BlockSpec((1, rows, width), lambda j: (j, 0, 0)),
        ]
        + [HBM_SPEC] * 4,
        out_specs=whole((rows, width)),
        out_shape=jax.ShapeDtypeStruct((rows, width), F32),
        scratch_shapes=[
            pltpu.VMEM((3, Z_PARTS, width // Z_PARTS, width), BF16),
            pltpu.VMEM((rows, width), F32),
            pltpu.SemaphoreType.DMA((3, PIECES)),
        ],
        compiler_params=params("frames"),
        cost_estimate=cost(
            flops=6 * rows * width * width, bytes_accessed=10 * width * width, transcendentals=0
        ),
        name="frames_back",
    )(blocks, frames, gains, grad_middle, grad_qkv, *pieces)


def kernels_chain(blocks, rows_in, lengths, branch, attn_pieces, up_pieces, down_pieces):
    hidden, qkv, mixed, gain_rows, log_totals, middle, second = forward_call(
        blocks, lengths, rows_in, attn_pieces
    )
    slope, active, *down_grads = up_call(blocks, second, branch, up_pieces)
    grad_upward, *up_grads = down_call(blocks, branch, second, slope, down_pieces)
    grad_middle, grad_qkv, *attn_grads = backward_call(
        blocks, lengths, branch, middle, gain_rows, log_totals, grad_upward, qkv, hidden, mixed,
        up_pieces, attn_pieces,
    )
    output = result_call(blocks, lengths, middle, active, down_pieces)
    grad_frames = frames_call(blocks, rows_in, gain_rows, grad_middle, grad_qkv, attn_pieces)
    return output, grad_frames, attn_grads, up_grads, down_grads


def layer_whole(blocks, rows_in, lengths, branch, attn, w_up, w_down):
    attn_pieces, up_pieces, down_pieces = (gather_whole(part) for part in (attn, w_up, w_down))
    up_pieces = tuple(pack_columns(part, 4) for part in up_pieces)
    down_pieces = tuple(jnp.swapaxes(part, 0, 1) for part in down_pieces)
    output, grad_frames, *grads = kernels_chain(
        blocks, rows_in, lengths, branch, attn_pieces, up_pieces, down_pieces
    )
    return (output, grad_frames) + tuple(scatter_whole(part) for part in grads)


def pack_columns(value, parts):
    *lead, rows, columns = value.shape
    split = value.reshape(*lead, rows, parts, columns // parts)
    return jnp.swapaxes(split, -3, -2).reshape(*lead, parts * rows, columns // parts)


def layer_plane(blocks, rows_in, lengths, branch, attn, w_up, w_down):
    attn_column = gather_column(attn)
    up_column = gather_column(pack_columns(w_up, 4))
    down_near = jnp.stack((w_down, first_hop(w_down)))
    attn_column = after(attn_column, down_near)
    down_near = gather_column(down_near)
    attn_near = jnp.stack((attn_column, first_hop(attn_column)))
    attn_far = second_hop(attn_near)
    up_column = after(up_column, attn_near)
    up_next = first_hop(up_column)
    attn_pieces = (attn_near, attn_far, across_cores(attn_near), across_cores(attn_far))
    up_near = jnp.stack((up_column, up_next))
    up_far = second_hop(up_near)

    hidden, qkv, mixed, gain_rows, log_totals, middle, second = forward_call(
        blocks, lengths, after(rows_in, up_near), attn_pieces
    )

    up_far = after(up_far, second)
    down_near = after(down_near, up_far)
    down_far = second_hop(down_near)
    up_pieces = (up_near, up_far, across_cores(up_near), across_cores(up_far))
    slope, active, *down_grads = up_call(blocks, after(second, down_near), branch, up_pieces)
    down_far = after(down_far, down_grads[0])

    down_got_away = across_cores(down_grads[3])
    down_got = across_cores(down_grads[2])
    down_away = low_total(down_grads[1], down_got_away)
    down_one = first_hop(down_away)
    down_pieces = (
        down_near, down_far, across_cores(down_near), across_cores(down_far)
    )
    grad_upward, *up_grads = down_call(
        blocks, after(branch, down_away), second, slope, down_pieces
    )

    up_got_away = across_cores(up_grads[3])
    up_got = across_cores(up_grads[2])
    down_one = after(down_one, up_grads[0])
    down_away = low_total(down_grads[0][1], down_got[1], down_one[1])
    down_two = second_hop(down_away)
    up_away = low_total(up_grads[1], after(up_got_away, down_away))
    up_one = first_hop(up_away)
    grad_middle, grad_qkv, *attn_grads = backward_call(
        blocks, lengths, after(branch, down_away, up_away), middle, gain_rows, log_totals,
        grad_upward, qkv, hidden, mixed, up_pieces, attn_pieces,
    )

    attn_got_away = across_cores(attn_grads[3])
    attn_got = across_cores(attn_grads[2])
    down_two = after(down_two, grad_qkv)
    down_last = low_total(down_grads[0][0], down_got[0], down_one[0], down_two)
    down_rows = scatter_column(down_last)
    up_one = after(up_one, grad_qkv)
    up_away = low_total(up_grads[0][1], up_got[1], up_one[1])
    up_two = second_hop(up_away)
    attn_away = low_total(attn_grads[1], after(attn_got_away, up_away, down_last))
    attn_one = first_hop(attn_away)
    grad_frames = frames_call(
        blocks, rows_in, gain_rows, after(grad_middle, attn_away), grad_qkv, attn_pieces
    )

    up_two = after(up_two, grad_frames)
    up_last = low_total(up_grads[0][0], up_got[0], up_one[0], up_two)
    up_rows = scatter_column(up_last)
    output = result_call(blocks, lengths, after(middle, up_last), active, down_pieces)

    attn_one = after(attn_one, output)
    attn_away = low_total(attn_grads[0][1], attn_got[1], attn_one[1])
    attn_two = second_hop(attn_away)
    attn_last = low_total(attn_grads[0][0], attn_got[0], attn_one[0], attn_two)
    attn_rows = scatter_column(attn_last)
    return output, grad_frames, attn_rows, up_rows, down_rows


def on_device(
    sizes, frames, lengths, w_query, w_key, w_value, w_out, w_up, w_down,
    gain_attn, gain_mlp, cotangent,
):
    width = frames.shape[-1]
    blocks = piece_blocks(sizes)
    rows_in = frames[0]
    valid = lax.broadcasted_iota(jnp.int32, (rows_in.shape[0], 1), 0) < lengths[0]
    branch = jnp.where(valid, cotangent[0], jnp.zeros_like(cotangent[0]))
    gains = jnp.pad(jnp.stack((gain_attn, gain_mlp), axis=1), ((0, 0), (0, LANES - 2)))
    attn = jnp.concatenate((w_query, w_key, w_value, w_out, gains), axis=1)
    layer = layer_plane if is_plane(sizes) else layer_whole
    output, grad_frames, attn_rows, up_rows, down_rows = layer(
        blocks, rows_in, lengths, branch, attn, w_up, w_down
    )
    grad_query = attn_rows[:, :width]
    grad_key = attn_rows[:, width : 2 * width]
    grad_value = attn_rows[:, 2 * width : 3 * width]
    grad_out = attn_rows[:, 3 * width :]
    gain_one = (
        jnp.sum(w_query.astype(F32) * grad_query, axis=1)
        + jnp.sum(w_key.astype(F32) * grad_key, axis=1)
        + jnp.sum(w_value.astype(F32) * grad_value, axis=1)
    ) / gain_attn.astype(F32)
    gain_two = jnp.sum(w_up.astype(F32) * up_rows, axis=1) / gain_mlp.astype(F32)
    return (
        output[None], grad_frames[None], grad_query, grad_key, grad_value, grad_out,
        up_rows, down_rows, gain_one, gain_two,
    )


def solution(mesh):
    wide, narrow = mesh.shape["wide"], mesh.shape["narrow"]
    y = 1
    while 4 * y * y <= wide:
        y *= 2
    sizes = {"z": wide // y, "y": y, "x": narrow // 2, "c": 2}
    fine = Mesh(mesh.devices.reshape(tuple(sizes[name] for name in ALL)), ALL)
    split = P(ALL)
    return jax.shard_map(
        functools.partial(on_device, sizes),
        mesh=fine,
        in_specs=(split,) * 11,
        out_specs=(split,) * 10,
        check_vma=False,
    )
```

```python
import functools

import jax
import jax.numpy as jnp
import numpy as np
from jax import lax
from jax.experimental import pallas as pl
from jax.experimental.pallas import tpu as pltpu
from jax.sharding import Mesh, PartitionSpec as P

HEADS = 16
HEAD_DIM = 64
EPSILON = 1e-06
FACTOR = HEAD_DIM ** (-0.5)
LANES = 128
Z_PARTS = 4
PIECES = 8
QUARTERS = 4
ALL = ("z", "y", "x", "c")
PLANE = ("y", "x", "c")
SWAP = [(0, 1), (1, 0)]
VMEM_MIB = {"forward": 32, "upward": 26, "downward": 26, "middle": 24, "attend_back": 26, "grads": 24, "result": 20, "frames": 20}
F32 = jnp.float32
BF16 = jnp.bfloat16
GELU_A = 0.7978845608028654
GELU_B = 0.044715

NN = (((1,), (0,)), ((), ()))
NT = (((1,), (1,)), ((), ()))
TN = (((0,), (0,)), ((), ()))


def mxu(left, right, dims=NN):
    return lax.dot_general(left, right, dims, preferred_element_type=F32)


def plane_pairs(step):
    pairs = []
    for y in range(2):
        for x in range(2):
            for c in range(2):
                flip_y = (c == 0) == (step == 1)
                to = (1 - y, x, c) if flip_y else (y, 1 - x, c)
                pairs.append(((y * 2 + x) * 2 + c, (to[0] * 2 + to[1]) * 2 + to[2]))
    return pairs


def is_plane(sizes):
    return sizes["x"] == 2 and sizes["y"] == 2 and sizes["c"] == 2 and sizes["z"] == Z_PARTS


def place_table(sizes):
    core = lax.axis_index("c")
    piece = jnp.arange(PIECES + QUARTERS + 1, dtype=jnp.int32)
    side = core ^ jnp.where(piece < PIECES, (piece >> 2) & 1, 0)
    first = (piece >> 1) & 1
    second = piece & 1
    if is_plane(sizes):
        y = lax.axis_index("y") ^ jnp.where(side == 0, first, second)
        x = lax.axis_index("x") ^ jnp.where(side == 0, second, first)
    else:
        y, x = first, second
    place = y * 2 + x
    place = jnp.where(piece < PIECES, place * 2 + side, place)
    return jnp.where(piece < PIECES + QUARTERS, place, core).astype(jnp.int32)


def after(value, *others):
    return lax.optimization_barrier((value,) + others)[0]


def first_hop(value, name="pieces"):
    with jax.named_scope(name):
        return lax.ppermute(value, PLANE, plane_pairs(1))


def second_hop(value, name="pieces"):
    with jax.named_scope(name):
        return lax.ppermute(value, PLANE, plane_pairs(2))


def across_cores(value, name="pieces"):
    with jax.named_scope(name):
        return lax.ppermute(value, "c", SWAP)


def gather_column(shard):
    return lax.all_gather(shard, "z", axis=0, tiled=False)


def gather_whole(shard):
    full = lax.all_gather(shard, ALL, axis=0, tiled=True)
    full = full.reshape(Z_PARTS, 2, 2, 2, full.shape[0] // (Z_PARTS * PIECES), full.shape[1])
    even, odd = full[:, :, :, 0], full[:, :, :, 1]
    upper = lax.axis_index("c") == 1
    pieces = []
    for side in (jnp.where(upper, odd, even), jnp.where(upper, even, odd)):
        pieces += [jnp.swapaxes(side[:, :, second], 0, 1) for second in range(2)]
    return tuple(pieces)


def total(*parts):
    result = parts[0].astype(F32)
    for part in parts[1:]:
        result = result + part.astype(F32)
    return result


def low_total(*parts):
    return total(*parts).astype(BF16)


def scatter_column(mine):
    return lax.psum_scatter(mine, "z", scatter_dimension=0, tiled=False).astype(F32)


def scatter_whole(parts):
    mine = jnp.stack(parts, axis=1)[:, :, None]
    here = lax.broadcasted_iota(jnp.int32, (1, 1, 2, 1, 1), 2) == lax.axis_index("c")
    full = jnp.where(here, mine, jnp.zeros_like(mine))
    full = full.reshape(-1, full.shape[-1])
    return lax.psum_scatter(full, ALL, scatter_dimension=0, tiled=True).astype(F32)


COST_SHARE = 0.02


def cost(flops, bytes_accessed, transcendentals):
    return pl.CostEstimate(
        flops=int(COST_SHARE * flops), bytes_accessed=int(COST_SHARE * bytes_accessed),
        transcendentals=int(COST_SHARE * transcendentals),
    )


def in_hbm(pieces):
    return [pltpu.with_memory_space_constraint(part, pltpu.HBM) for part in pieces]


def params(name):
    return pltpu.CompilerParams(vmem_limit_bytes=VMEM_MIB[name] << 20)


HBM_SPEC = pl.BlockSpec(memory_space=pl.ANY)
SMEM_SPEC = pl.BlockSpec(memory_space=pltpu.SMEM)


def whole(shape):
    return pl.BlockSpec(
        shape, lambda *_: (0,) * len(shape), pipeline_mode=pl.Buffered(1)
    )


def low_part(shape):
    return pl.BlockSpec(shape, lambda j: (0, jnp.minimum(j, Z_PARTS // 2 - 1)))


def high_part(shape):
    return pl.BlockSpec(shape, lambda j: (0, jnp.maximum(j - Z_PARTS // 2, 0)))


def piece_copies(pieces, blocks, held, sems, columns):
    rows = pieces[0].shape[2]
    copies = []
    for piece in range(PIECES):
        own, first, second = piece >> 2, (piece >> 1) & 1, piece & 1
        source = pieces[2 * own + second].at[first, :, :, columns]
        start = pl.multiple_of(blocks[piece] * rows, rows)
        copies.append(
            pltpu.make_async_copy(source, held.at[:, pl.ds(start, rows), :], sems.at[piece])
        )
    return copies


def packed_copies(pieces, blocks, part, held, sems):
    rows = held.shape[1] // PIECES
    copies = []
    for piece in range(PIECES):
        own, first, second = piece >> 2, (piece >> 1) & 1, piece & 1
        source = pieces[2 * own + second].at[first, :, pl.ds(part * rows, rows), :]
        start = pl.multiple_of(blocks[piece] * rows, rows)
        copies.append(
            pltpu.make_async_copy(source, held.at[:, pl.ds(start, rows), :], sems.at[piece])
        )
    return copies


def part_copies(pieces, blocks, part, held, sems, by_class=False):
    rows = pieces[0].shape[2]
    copies = []
    for piece in range(PIECES):
        own, first, second = piece >> 2, (piece >> 1) & 1, piece & 1
        source = pieces[2 * own + second].at[part, first]
        place = QUARTERS * own + (blocks[piece] >> 1) if by_class else blocks[piece]
        start = pl.multiple_of(place * rows, rows)
        copies.append(
            pltpu.make_async_copy(source, held.at[pl.ds(start, rows), :], sems.at[piece])
        )
    return copies


def grad_copies(held, outs, table, columns, sems):
    rows = outs[0].shape[1]
    copies = []
    for piece in range(QUARTERS):
        target = outs[piece].at[:, :, columns]
        start = pl.multiple_of(table[PIECES + piece] * rows, rows)
        copies.append(
            pltpu.make_async_copy(held.at[:, pl.ds(start, rows), :], target, sems.at[piece])
        )
    return copies


def grad_part_copies(held, outs, table, part, sems):
    rows = outs[0].shape[1]
    copies = []
    for piece in range(QUARTERS):
        target = outs[piece].at[part]
        start = pl.multiple_of(table[PIECES + piece] * rows, rows)
        copies.append(
            pltpu.make_async_copy(held.at[pl.ds(start, rows), :], target, sems.at[piece])
        )
    return copies


def start_all(copies):
    for copy in copies:
        copy.start()


def wait_all(copies):
    for copy in copies:
        copy.wait()


def prefetch(step, steps, copies):
    @pl.when(step == 0)
    def _():
        start_all(copies(0))
        start_all(copies(1))

    for part in range(steps):

        @pl.when(step == part)
        def _():
            if part + 2 < steps:
                start_all(copies(part + 2))
            wait_all(copies(part))


def flat(block):
    return block.reshape(block.shape[0] * block.shape[1], block.shape[2])


def inverse_rms(rows):
    return lax.rsqrt(jnp.mean(rows * rows, axis=-1, keepdims=True) + EPSILON)


def store(source, target, sem):
    return pltpu.make_async_copy(source, target, sem)


def lane_pair(pair):
    return pl.ds(pl.multiple_of(pair * LANES, LANES), LANES)


def split_turned(table, value, place, turned, own, other):
    turned[...] = value.T
    rows = turned.shape[0] // (Z_PARTS * PIECES)
    core = table[PIECES + QUARTERS]
    for block in range(Z_PARTS * QUARTERS):
        here = pl.ds(block * rows, rows)
        mine = pl.multiple_of((2 * block + core) * rows, rows)
        rest = pl.multiple_of((2 * block + 1 - core) * rows, rows)
        own[place, here, :] = turned[pl.ds(mine, rows), :]
        other[place, here, :] = turned[pl.ds(rest, rows), :]


def forward_kernel(
    blocks, length, frames, p0, p1, p2, p3,
    qkv_out, own_turned, other_turned, gains, log_totals, middle, second,
    held, gain_held, hidden, qkv, mixed, turned, sems, out_sems,
):
    pieces = (p0, p1, p2, p3)
    rows, width = frames.shape
    gain_copies = piece_copies(pieces, blocks, gain_held, sems.at[4], pl.ds(4 * width, LANES))
    copies = [
        piece_copies(pieces, blocks, held.at[part], sems.at[part], pl.ds(part * width, width))
        for part in range(4)
    ]
    start_all(gain_copies)
    for part in range(4):
        start_all(copies[part])
    value = frames[...].astype(F32)
    normal = value * inverse_rms(value)
    wait_all(gain_copies)
    across = flat(gain_held[...]).astype(F32).T
    gains[...] = across[:8]
    hidden[...] = (normal * across[0:1]).astype(BF16)
    leaving = []
    split_turned(blocks, hidden[...], 0, turned, own_turned, other_turned)
    for part in range(3):
        wait_all(copies[part])
        result = mxu(hidden[...], flat(held[part])).astype(BF16)
        if part == 0:
            result = (result.astype(F32) * FACTOR).astype(BF16)
        qkv[part] = result
        leaving.append(store(qkv.at[part], qkv_out.at[part], out_sems.at[part]))
        leaving[-1].start()

    bias = jnp.where(
        lax.broadcasted_iota(jnp.int32, (rows, 1), 0) < length[0], 0.0, -1e30
    ).astype(F32)
    lane = lax.broadcasted_iota(jnp.int32, (rows, LANES), 1)

    @pl.loop(0, width // LANES)
    def _(pair):
        here = lane_pair(pair)
        query, key, value = qkv[0, :, here], qkv[1, :, here], qkv[2, :, here]
        outs = []
        for half in range(2):
            mine = (lane < HEAD_DIM) == (half == 0)
            scores = mxu(key, jnp.where(mine, query, jnp.zeros_like(query)), NT) + bias
            peak = jnp.max(scores, axis=0, keepdims=True)
            expon = jnp.exp(scores - peak)
            sums = jnp.sum(expon, axis=0, keepdims=True)
            log_totals[pl.ds(2 * pair + half, 1), :] = peak + jnp.log(sums)
            shares = (expon * (1.0 / sums)).astype(BF16)
            outs.append(mxu(shares, value, TN))
        mixed[:, here] = jnp.where(lane < HEAD_DIM, outs[0], outs[1]).astype(BF16)

    split_turned(blocks, mixed[...], 1, turned, own_turned, other_turned)
    wait_all(copies[3])
    result = frames[...].astype(F32) + mxu(mixed[...], flat(held[3]))
    middle[...] = result
    low = (result * inverse_rms(result) * gains[1:2, :]).astype(BF16)
    second[...] = low
    split_turned(blocks, low, 2, turned, own_turned, other_turned)
    wait_all(leaving)


def forward_call(blocks, length, frames, pieces):
    rows, width = frames.shape
    turned = jax.ShapeDtypeStruct((3, width // 2, rows), BF16)
    return pl.pallas_call(
        forward_kernel,
        grid=(1,),
        in_specs=[SMEM_SPEC, SMEM_SPEC, whole((rows, width))] + [HBM_SPEC] * 4,
        out_specs=[HBM_SPEC, whole(turned.shape), whole(turned.shape)]
        + [whole((8, width)), whole((HEADS, rows)), whole((rows, width)), whole((rows, width))],
        out_shape=[
            pltpu.HBM((3, rows, width), BF16),
            turned,
            turned,
            jax.ShapeDtypeStruct((8, width), F32),
            jax.ShapeDtypeStruct((HEADS, rows), F32),
            pltpu.HBM((rows, width), F32),
            jax.ShapeDtypeStruct((rows, width), BF16),
        ],
        scratch_shapes=[
            pltpu.VMEM((4, Z_PARTS, width // Z_PARTS, width), BF16),
            pltpu.VMEM((Z_PARTS, width // Z_PARTS, LANES), BF16),
            pltpu.VMEM((rows, width), BF16),
            pltpu.VMEM((3, rows, width), BF16),
            pltpu.VMEM((rows, width), BF16),
            pltpu.VMEM((width, rows), BF16),
            pltpu.SemaphoreType.DMA((5, PIECES)),
            pltpu.SemaphoreType.DMA((3,)),
        ],
        compiler_params=params("forward"),
        cost_estimate=cost(10 * rows * width * width, 16 * width * width, rows * rows),
        name="forward",
    )(blocks, length, frames, *pieces)


def up_kernel(
    blocks, second, p0, p1, p2, p3, slope, own, low_half, high_half, held, active, sems,
):
    step = pl.program_id(0)
    pieces = (p0, p1, p2, p3)

    def copies(part):
        return packed_copies(pieces, blocks, part, held.at[part], sems.at[part])

    prefetch(step, Z_PARTS, copies)
    value = mxu(second[...], flat(held[step]))
    square = value * value
    bend = jnp.tanh(GELU_A * value * (1.0 + GELU_B * square))
    share = 0.5 * (1.0 + bend)
    active[...] = (value * share).astype(BF16)
    slope[...] = (
        share + 0.5 * value * (1.0 - bend * bend) * (GELU_A * (1.0 + 3.0 * GELU_B * square))
    ).astype(BF16)
    core = blocks[PIECES + QUARTERS]
    width = active.shape[1] // PIECES
    for block in range(QUARTERS):
        here = pl.ds(block * width, width)
        mine = pl.multiple_of((2 * block + core) * width, width)
        rest = pl.multiple_of((2 * block + 1 - core) * width, width)
        own[:, here] = active[:, pl.ds(mine, width)]

        @pl.when(step < Z_PARTS // 2)
        def _():
            low_half[:, here] = active[:, pl.ds(rest, width)]

        @pl.when(step >= Z_PARTS // 2)
        def _():
            high_half[:, here] = active[:, pl.ds(rest, width)]


def up_call(blocks, second, pieces):
    rows, width = second.shape
    inner = pieces[0].shape[2] * pieces[0].shape[3] * PIECES * Z_PARTS // width
    columns = inner // Z_PARTS
    quarter = jax.ShapeDtypeStruct((rows, inner // 4), BF16)
    return pl.pallas_call(
        up_kernel,
        grid=(Z_PARTS,),
        in_specs=[SMEM_SPEC, whole((rows, width))] + [HBM_SPEC] * 4,
        out_specs=[
            pl.BlockSpec((rows, columns), lambda j: (0, j)),
            pl.BlockSpec((rows, columns // 2), lambda j: (0, j)),
            low_part((rows, columns // 2)),
            high_part((rows, columns // 2)),
        ],
        out_shape=[
            jax.ShapeDtypeStruct((rows, inner), BF16),
            jax.ShapeDtypeStruct((rows, inner // 2), BF16),
            quarter,
            quarter,
        ],
        scratch_shapes=[
            pltpu.VMEM((Z_PARTS, Z_PARTS, width // Z_PARTS, columns), BF16),
            pltpu.VMEM((rows, columns), BF16),
            pltpu.SemaphoreType.DMA((Z_PARTS, PIECES)),
        ],
        compiler_params=params("upward"),
        cost_estimate=cost(2 * rows * width * inner, 2 * width * inner, rows * inner),
        name="upward",
    )(blocks, second, *pieces)


def down_grad_kernel(
    blocks, mine, low_half, high_half, branch, other_branch, g0, g1, away, grads, grad_sems,
):
    step = pl.program_id(0)
    slot = lax.rem(step, 2)

    def leave(part, at):
        return grad_part_copies(grads.at[at], (g0, g1, away.at[0], away.at[1]), blocks, part, grad_sems.at[at])

    @pl.when(step >= 2)
    def _():
        wait_all(leave(step - 2, slot))

    for half, theirs in enumerate((low_half, high_half)):

        @pl.when((step >= Z_PARTS // 2) == (half == 1))
        def _():
            grads[slot] = (
                mxu(mine[...], branch[...], TN) + mxu(theirs[...], other_branch[...], TN)
            ).astype(BF16)

    start_all(leave(step, slot))

    @pl.when(step == Z_PARTS - 1)
    def _():
        wait_all(leave(step - 1, 1 - slot))
        wait_all(leave(step, slot))


def down_grad_call(blocks, mine, halves, branch, other_branch):
    rows, width = branch.shape
    columns = mine.shape[1] // Z_PARTS
    grad = jax.ShapeDtypeStruct((Z_PARTS, columns // QUARTERS, width), BF16)
    part = pl.BlockSpec((rows, columns), lambda j: (0, j))
    return pl.pallas_call(
        down_grad_kernel,
        grid=(Z_PARTS,),
        in_specs=[
            SMEM_SPEC,
            part,
            low_part((rows, columns)),
            high_part((rows, columns)),
            whole((rows, width)),
            whole((rows, width)),
        ],
        out_specs=[HBM_SPEC] * 3,
        out_shape=[grad, grad, jax.ShapeDtypeStruct((2,) + grad.shape, BF16)],
        scratch_shapes=[
            pltpu.VMEM((2, columns, width), BF16),
            pltpu.SemaphoreType.DMA((2, QUARTERS)),
        ],
        compiler_params=params("grads"),
        cost_estimate=cost(8 * rows * width * columns, 8 * width * columns, 0),
        name="down_grads",
    )(blocks, mine, *halves, branch, other_branch)


def down_kernel(blocks, branch, slope, p0, p1, p2, p3, low_half, high_half, held, sems):
    step = pl.program_id(0)
    pieces = (p0, p1, p2, p3)

    def copies(part):
        return part_copies(pieces, blocks, part, held.at[part], sems.at[part])

    prefetch(step, Z_PARTS, copies)
    value = mxu(branch[...], held[step], NT)
    low = (value * slope[...].astype(F32)).astype(BF16)

    @pl.when(step < Z_PARTS // 2)
    def _():
        low_half[...] = low

    @pl.when(step >= Z_PARTS // 2)
    def _():
        high_half[...] = low


def down_call(blocks, branch, slope, pieces):
    rows, width = branch.shape
    inner = slope.shape[1]
    columns = inner // Z_PARTS
    half = Z_PARTS // 2
    out = jax.ShapeDtypeStruct((rows, inner // 2), BF16)
    return pl.pallas_call(
        down_kernel,
        grid=(Z_PARTS,),
        in_specs=[
            SMEM_SPEC,
            whole((rows, width)),
            pl.BlockSpec((rows, columns), lambda j: (0, j)),
        ]
        + [HBM_SPEC] * 4,
        out_specs=[
            pl.BlockSpec((rows, columns), lambda j: (0, jnp.minimum(j, half - 1))),
            pl.BlockSpec((rows, columns), lambda j: (0, jnp.maximum(j - half, 0))),
        ],
        out_shape=[out, out],
        scratch_shapes=[
            pltpu.VMEM((Z_PARTS, columns, width), BF16),
            pltpu.SemaphoreType.DMA((Z_PARTS, PIECES)),
        ],
        compiler_params=params("downward"),
        cost_estimate=cost(2 * rows * width * inner, 2 * width * inner, 0),
        name="downward",
    )(blocks, branch, slope, *pieces)


def up_grad_kernel(
    blocks, mine, theirs, low_half, high_half, low_other, high_other, g0, g1, g2, g3, grads, grad_sems,
):
    step = pl.program_id(0)
    slot = lax.rem(step, 2)
    columns = low_half.shape[1]

    def leave(part, at):
        start = pl.multiple_of(part * columns, columns)
        return grad_copies(
            grads.at[at], (g0, g1, g2, g3), blocks, pl.ds(start, columns), grad_sems.at[at]
        )

    @pl.when(step >= 2)
    def _():
        wait_all(leave(step - 2, slot))

    for half, (near, far) in enumerate(((low_half, low_other), (high_half, high_other))):

        @pl.when((step >= Z_PARTS // 2) == (half == 1))
        def _():
            grad = mxu(mine[0], near[...]) + mxu(theirs[0], far[...])
            grads[slot] = grad.astype(BF16).reshape(grads.shape[1:])

    start_all(leave(step, slot))

    @pl.when(step == Z_PARTS - 1)
    def _():
        wait_all(leave(step - 1, 1 - slot))
        wait_all(leave(step, slot))


def up_grad_call(blocks, own_turned, other_turned, halves, other_halves):
    _, width, rows = own_turned.shape
    inner = 2 * halves[0].shape[1]
    columns = inner // Z_PARTS
    half = Z_PARTS // 2
    part_rows = width // Z_PARTS
    grad = jax.ShapeDtypeStruct((Z_PARTS, part_rows // QUARTERS, inner), BF16)
    turned = pl.BlockSpec((1, width, rows), lambda j: (2, 0, 0), pipeline_mode=pl.Buffered(1))
    low = pl.BlockSpec((rows, columns), lambda j: (0, jnp.minimum(j, half - 1)))
    high = pl.BlockSpec((rows, columns), lambda j: (0, jnp.maximum(j - half, 0)))
    return pl.pallas_call(
        up_grad_kernel,
        grid=(Z_PARTS,),
        in_specs=[SMEM_SPEC, turned, turned, low, high, low, high],
        out_specs=[HBM_SPEC] * QUARTERS,
        out_shape=[grad] * QUARTERS,
        scratch_shapes=[
            pltpu.VMEM((2, Z_PARTS, part_rows, columns), BF16),
            pltpu.SemaphoreType.DMA((2, QUARTERS)),
        ],
        compiler_params=params("grads"),
        cost_estimate=cost(4 * rows * width * inner, 2 * width * inner, 0),
        name="up_grads",
    )(blocks, own_turned, other_turned, *halves, *other_halves)


def result_kernel(blocks, length, middle, own, low_half, high_half, p0, p1, p2, p3, output, held, sums, sems):
    step = pl.program_id(0)
    steps = Z_PARTS
    pieces = (p0, p1, p2, p3)

    def copies(part):
        return part_copies(pieces, blocks, part, held.at[part], sems.at[part], by_class=True)

    @pl.when(step == 0)
    def _():
        for part in range(steps):
            start_all(copies(part))
        sums[...] = middle[...]

    for part in range(steps):

        @pl.when(step == part)
        def _():
            wait_all(copies(part))

    half = own.shape[1]
    for place, other in enumerate((low_half, high_half)):

        @pl.when((step >= Z_PARTS // 2) == (place == 1))
        def _():
            sums[...] += mxu(own[...], held[step, :half, :]) + mxu(
                other[...], held[step, half:, :]
            )


    @pl.when(step == steps - 1)
    def _():
        valid = lax.broadcasted_iota(jnp.int32, (sums.shape[0], 1), 0) < length[0]
        output[...] = (sums[...] * valid.astype(F32)).astype(BF16)


def result_call(blocks, length, middle, own, halves, pieces):
    rows, width = middle.shape
    inner = 2 * own.shape[1]
    columns = inner // Z_PARTS
    return pl.pallas_call(
        result_kernel,
        grid=(Z_PARTS,),
        in_specs=[
            SMEM_SPEC,
            SMEM_SPEC,
            whole((rows, width)),
            pl.BlockSpec((rows, columns // 2), lambda j: (0, j)),
            low_part((rows, columns // 2)),
            high_part((rows, columns // 2)),
        ]
        + [HBM_SPEC] * 4,
        out_specs=whole((rows, width)),
        out_shape=jax.ShapeDtypeStruct((rows, width), BF16),
        scratch_shapes=[
            pltpu.VMEM((Z_PARTS, columns, width), BF16),
            pltpu.VMEM((rows, width), F32),
            pltpu.SemaphoreType.DMA((Z_PARTS, PIECES)),
        ],
        compiler_params=params("result"),
        cost_estimate=cost(
            flops=2 * rows * width * inner, bytes_accessed=3 * width * inner, transcendentals=0
        ),
        name="result",
    )(blocks, length, middle, own, *halves, *in_hbm(pieces))


def middle_kernel(
    blocks, branch, middle, gains, low_half, high_half, u0, u1, u2, u3, p0, p1, p2, p3,
    grad_middle, grad_attn, grad_mixed, held, out_held, sums, sems, out_sems,
):
    step = pl.program_id(0)
    steps = Z_PARTS
    width = middle.shape[1]

    def copies(part):
        return packed_copies((u0, u1, u2, u3), blocks, part, held.at[part], sems.at[part])

    out_copies = piece_copies(
        (p0, p1, p2, p3), blocks, out_held, out_sems, pl.ds(3 * width, width)
    )
    prefetch(step, steps, copies)

    @pl.when(step == 1)
    def _():
        start_all(out_copies)

    @pl.when(step == 0)
    def _():
        sums[...] = mxu(low_half[...], flat(held[step]), NT)

    @pl.when((step > 0) & (step < steps // 2))
    def _():
        sums[...] += mxu(low_half[...], flat(held[step]), NT)

    @pl.when(step >= steps // 2)
    def _():
        sums[...] += mxu(high_half[...], flat(held[step]), NT)

    @pl.when(step == steps - 1)
    def _():
        value = middle[...]
        inverse = inverse_rms(value)
        normal = value * inverse
        scaled = sums[...] * gains[1:2, :]
        mean = jnp.mean(scaled * normal, axis=-1, keepdims=True)
        result = branch[...].astype(F32) + inverse * (scaled - normal * mean)
        grad_middle[...] = result
        low = result.astype(BF16)
        grad_attn[...] = low
        wait_all(out_copies)
        grad_mixed[...] = mxu(low, flat(out_held[...]), NT).astype(BF16)


def middle_call(blocks, branch, middle, gains, halves, up_pieces, pieces):
    rows, width = middle.shape
    inner = 2 * halves[0].shape[1]
    half = Z_PARTS // 2
    columns = inner // Z_PARTS
    return pl.pallas_call(
        middle_kernel,
        grid=(Z_PARTS,),
        in_specs=[
            SMEM_SPEC,
            whole((rows, width)),
            whole((rows, width)),
            whole((8, width)),
            pl.BlockSpec((rows, columns), lambda j: (0, jnp.minimum(j, half - 1))),
            pl.BlockSpec((rows, columns), lambda j: (0, jnp.maximum(j - half, 0))),
        ]
        + [HBM_SPEC] * 8,
        out_specs=[whole((rows, width))] * 3,
        out_shape=[
            pltpu.HBM((rows, width), F32),
            jax.ShapeDtypeStruct((rows, width), BF16),
            jax.ShapeDtypeStruct((rows, width), BF16),
        ],
        scratch_shapes=[
            pltpu.VMEM((Z_PARTS, Z_PARTS, width // Z_PARTS, columns), BF16),
            pltpu.VMEM((Z_PARTS, width // Z_PARTS, width), BF16),
            pltpu.VMEM((rows, width), F32),
            pltpu.SemaphoreType.DMA((Z_PARTS, PIECES)),
            pltpu.SemaphoreType.DMA((PIECES,)),
        ],
        compiler_params=params("middle"),
        cost_estimate=cost(2 * rows * width * (inner + width), 3 * width * inner, 0),
        name="middle",
    )(blocks, branch, middle, gains, *halves, *up_pieces, *pieces)


def attend_back_kernel(
    length, queries, keys, values, log_totals, grads, grad_query, grad_key, grad_value,
):
    rows, width = grads.shape
    bias = jnp.where(
        lax.broadcasted_iota(jnp.int32, (rows, 1), 0) < length[0], 0.0, -1e30
    ).astype(F32)
    lane = lax.broadcasted_iota(jnp.int32, (rows, LANES), 1)

    @pl.loop(0, width // LANES)
    def _(pair):
        here = lane_pair(pair)
        query, key, value, grad = queries[0, :, here], keys[0, :, here], values[0, :, here], grads[:, here]
        parts = []
        for half in range(2):
            mine = (lane < HEAD_DIM) == (half == 0)
            scores = mxu(key, jnp.where(mine, query, jnp.zeros_like(query)), NT) + bias
            chance = jnp.exp(scores - log_totals[pl.ds(2 * pair + half, 1), :])
            to_value = mxu(chance.astype(BF16), grad)
            grad_chance = mxu(value, jnp.where(mine, grad, jnp.zeros_like(grad)), NT)
            mean = jnp.sum(chance * grad_chance, axis=0, keepdims=True)
            grad_scores = (chance * (grad_chance - mean)).astype(BF16)
            to_key = mxu(grad_scores, query)
            to_query = mxu(grad_scores, key, TN) * FACTOR
            parts.append((to_query, to_key, to_value))
        for place, out in enumerate((grad_query, grad_key, grad_value)):
            out[:, here] = jnp.where(lane < HEAD_DIM, parts[0][place], parts[1][place]).astype(BF16)


def attend_back_call(length, log_totals, qkv, grad_mixed):
    rows, width = grad_mixed.shape

    def plane(place):
        return pl.BlockSpec(
            (1, rows, width), lambda j: (place, 0, 0), pipeline_mode=pl.Buffered(1)
        )

    return pl.pallas_call(
        attend_back_kernel,
        grid=(1,),
        in_specs=[
            SMEM_SPEC, plane(0), plane(1), plane(2), whole((HEADS, rows)), whole((rows, width)),
        ],
        out_specs=[whole((rows, width))] * 3,
        out_shape=[jax.ShapeDtypeStruct((rows, width), BF16)] * 3,
        compiler_params=params("attend_back"),
        cost_estimate=cost(20 * rows * width * width, 40 * width * width, rows * rows),
        name="attend_back",
    )(length, qkv, qkv, qkv, log_totals, grad_mixed)


def attn_grad_kernel(
    blocks, mine_in, theirs_in, a0, a1, a2, a3, b0, b1, b2, b3, g0, g1, g2, g3,
    turned, near, far, grads, turned_sems, load_sems, grad_sems,
):
    columns = a0.shape[1]
    turned_loads = [
        store(source.at[pl.ds(0, 2)], turned.at[at], turned_sems.at[at])
        for at, source in enumerate((mine_in, theirs_in))
    ]
    start_all(turned_loads)
    loads = []
    for part, sources in enumerate(((a0, b0), (a1, b1), (a2, b2), (a3, b3))):
        loads.append(
            [
                store(source, target.at[part], load_sems.at[at, part])
                for at, (source, target) in enumerate(zip(sources, (near, far)))
            ]
        )
        start_all(loads[part])
    wait_all(turned_loads)
    pending = []
    for part in range(4):
        wait_all(loads[part])
        left = part // 3
        grad = mxu(turned[0, left], near[part]) + mxu(turned[1, left], far[part])
        grads[part] = grad.astype(BF16).reshape(grads.shape[1:])
        pending.append(
            grad_copies(
                grads.at[part], (g0, g1, g2, g3), blocks, pl.ds(part * columns, columns), grad_sems.at[part]
            )
        )
        start_all(pending[part])
    for copies in pending:
        wait_all(copies)


def attn_grad_call(blocks, own_turned, other_turned, near, far):
    _, width, rows = own_turned.shape
    columns = near[0].shape[1]
    part_rows = width // Z_PARTS
    grad = jax.ShapeDtypeStruct((Z_PARTS, part_rows // QUARTERS, 4 * columns), BF16)
    return pl.pallas_call(
        attn_grad_kernel,
        grid=(1,),
        in_specs=[SMEM_SPEC] + [HBM_SPEC] * 10,
        out_specs=[HBM_SPEC] * QUARTERS,
        out_shape=[grad] * QUARTERS,
        scratch_shapes=[
            pltpu.VMEM((2, 2, width, rows), BF16),
            pltpu.VMEM((4, rows, columns), BF16),
            pltpu.VMEM((4, rows, columns), BF16),
            pltpu.VMEM((4, Z_PARTS, part_rows, columns), BF16),
            pltpu.SemaphoreType.DMA((2,)),
            pltpu.SemaphoreType.DMA((2, 4)),
            pltpu.SemaphoreType.DMA((4, QUARTERS)),
        ],
        compiler_params=params("grads"),
        cost_estimate=cost(16 * rows * width * columns, 16 * width * columns, 0),
        name="attn_grads",
    )(blocks, own_turned, other_turned, *near, *far)


def frames_kernel(
    blocks, frames, gains, grad_middle, grad_query, grad_key, grad_value, p0, p1, p2, p3, grad_frames,
    held, sums, sems,
):
    step = pl.program_id(0)
    width = frames.shape[1]

    def copies(part):
        return piece_copies(
            (p0, p1, p2, p3), blocks, held.at[part], sems.at[part], pl.ds(part * width, width)
        )

    prefetch(step, 3, copies)
    for part, grad in enumerate((grad_query, grad_key, grad_value)):

        @pl.when(step == part)
        def _():
            term = mxu(grad[...], flat(held[part]), NT)
            sums[...] = term if part == 0 else sums[...] + term

    @pl.when(step == 2)
    def _():
        rows = frames[...].astype(F32)
        inverse = inverse_rms(rows)
        normal = rows * inverse
        scaled = sums[...] * gains[0:1, :]
        mean = jnp.mean(scaled * normal, axis=-1, keepdims=True)
        grad_frames[...] = grad_middle[...] + inverse * (scaled - normal * mean)


def frames_call(blocks, frames, gains, grad_middle, grad_qkv, pieces):
    rows, width = frames.shape
    return pl.pallas_call(
        frames_kernel,
        grid=(3,),
        in_specs=[
            SMEM_SPEC,
            whole((rows, width)),
            whole((8, width)),
            whole((rows, width)),
            whole((rows, width)),
            whole((rows, width)),
            whole((rows, width)),
        ]
        + [HBM_SPEC] * 4,
        out_specs=whole((rows, width)),
        out_shape=jax.ShapeDtypeStruct((rows, width), F32),
        scratch_shapes=[
            pltpu.VMEM((3, Z_PARTS, width // Z_PARTS, width), BF16),
            pltpu.VMEM((rows, width), F32),
            pltpu.SemaphoreType.DMA((3, PIECES)),
        ],
        compiler_params=params("frames"),
        cost_estimate=cost(6 * rows * width * width, 10 * width * width, 0),
        name="frames_back",
    )(blocks, frames, gains, grad_middle, *grad_qkv, *in_hbm(pieces))


def kernels_chain(blocks, rows_in, lengths, branch, attn_pieces, up_pieces, down_pieces, swap):
    qkv, own_turned, other_turned, gain_rows, log_totals, middle, second = forward_call(
        blocks, lengths, rows_in, attn_pieces
    )
    their_turned = swap(other_turned)
    slope, active, *other_active = up_call(blocks, second, up_pieces)
    down_grads = down_grad_call(
        blocks, active, [swap(half) for half in other_active], branch, swap(branch)
    )
    halves = down_call(blocks, branch, slope, down_pieces)
    grad_middle, grad_attn, grad_mixed = middle_call(
        blocks, branch, middle, gain_rows, halves, up_pieces, attn_pieces
    )
    up_grads = up_grad_call(
        blocks, own_turned, their_turned, halves, [swap(half) for half in halves]
    )
    grad_qkv = attend_back_call(lengths, log_totals, qkv, grad_mixed)
    factors = (*grad_qkv, grad_attn)
    attn_grads = attn_grad_call(
        blocks, own_turned, their_turned, factors, [swap(factor) for factor in factors]
    )
    output = result_call(blocks, lengths, middle, active, other_active, down_pieces)
    grad_frames = frames_call(blocks, rows_in, gain_rows, grad_middle, grad_qkv, attn_pieces)
    return output, grad_frames, attn_grads, up_grads, (*down_grads[:2], *down_grads[2])


def layer_whole(blocks, rows_in, lengths, branch, attn, w_up, w_down):
    attn_pieces, up_pieces, down_pieces = (gather_whole(part) for part in (attn, w_up, w_down))
    up_pieces = tuple(pack_columns(part, 4) for part in up_pieces)
    down_pieces = tuple(jnp.swapaxes(part, 0, 1) for part in down_pieces)
    output, grad_frames, *grads = kernels_chain(
        blocks, rows_in, lengths, branch, attn_pieces, up_pieces, down_pieces, across_cores
    )
    return (output, grad_frames) + tuple(scatter_whole(part) for part in grads)


def pack_columns(value, parts):
    *lead, rows, columns = value.shape
    split = value.reshape(*lead, rows, parts, columns // parts)
    return jnp.swapaxes(split, -3, -2).reshape(*lead, parts * rows, columns // parts)


def layer_plane(blocks, rows_in, lengths, branch, attn, w_up, w_down):
    attn_column = gather_column(attn)
    up_column = gather_column(pack_columns(w_up, 4))
    down_near = jnp.stack((w_down, first_hop(w_down)))
    their_branch = across_cores(branch, "their_branch")
    attn_column = after(attn_column, down_near, their_branch)
    down_near = gather_column(down_near)
    attn_near = jnp.stack((attn_column, first_hop(attn_column)))
    attn_far = second_hop(attn_near, "attn_far")
    up_column = after(up_column, attn_near)
    up_next = first_hop(up_column, "up_next")
    attn_pieces = (attn_near, attn_far, across_cores(attn_near), across_cores(attn_far))
    up_near = jnp.stack((up_column, up_next))
    up_far = second_hop(up_near, "up_far")

    qkv, own_turned, other_turned, gain_rows, log_totals, middle, second = forward_call(
        blocks, lengths, after(rows_in, up_near), attn_pieces
    )

    up_far = after(up_far, second, down_near)
    up_pieces = (up_near, up_far, across_cores(up_near), across_cores(up_far))
    down_near = after(down_near, up_far)
    down_far = second_hop(down_near, "down_far")
    slope, active, *other_active = up_call(blocks, after(second, down_near), up_pieces)
    their_active = [across_cores(half, "their_active") for half in other_active]
    their_turned = across_cores(after(other_turned, slope), "their_turned")
    down_grads = down_grad_call(blocks, active, their_active, branch, their_branch)
    down_one = first_hop(down_grads[2], "down_one")

    down_far = after(down_far, down_grads[0])
    down_pieces = (down_near, down_far, across_cores(down_near), across_cores(down_far))
    halves = down_call(blocks, after(branch, down_grads[0]), slope, down_pieces)
    their_halves = [across_cores(half, "their_half") for half in halves]
    grad_middle, grad_attn, grad_mixed = middle_call(
        blocks, branch, middle, gain_rows, halves, up_pieces, attn_pieces
    )
    their_attn = across_cores(grad_attn, "their_attn")
    down_one = after(down_one, grad_mixed)
    down_away = low_total(down_grads[1], down_one[1])
    down_two = second_hop(down_away, "down_two")
    up_grads = up_grad_call(
        blocks, after(own_turned, down_away), their_turned, halves, their_halves
    )
    up_one_away = first_hop(up_grads[3], "up_one_away")
    up_one = first_hop(up_grads[2], "up_one")
    grad_qkv = attend_back_call(lengths, log_totals, qkv, after(grad_mixed, up_grads[0]))
    their_qkv = [across_cores(grad, "their_qkv") for grad in grad_qkv]

    down_two = after(down_two, grad_qkv[0])
    down_last = low_total(down_grads[0], down_one[0], down_two)
    down_rows = scatter_column(down_last)
    up_one_away = after(up_one_away, down_last, up_one)
    up_away = low_total(up_grads[1], up_one_away)
    up_two = second_hop(up_away, "up_two")
    attn_grads = attn_grad_call(
        blocks, after(own_turned, up_away), their_turned, (*grad_qkv, grad_attn),
        (*their_qkv, their_attn),
    )
    attn_one_away = first_hop(attn_grads[3], "attn_one_away")
    attn_one = first_hop(attn_grads[2], "attn_one")
    grad_frames = frames_call(
        blocks, rows_in, gain_rows, after(grad_middle, attn_grads[0]), grad_qkv, attn_pieces
    )

    up_two = after(up_two, grad_frames)
    up_last = low_total(up_grads[0], up_one, up_two)
    up_rows = scatter_column(up_last)
    attn_one_away = after(attn_one_away, up_last)
    attn_away = low_total(attn_grads[1], attn_one_away)
    attn_two = second_hop(attn_away, "attn_two")
    output = result_call(
        blocks, lengths, after(middle, attn_away), active, other_active, down_pieces
    )
    attn_one = after(attn_one, output)
    attn_last = low_total(attn_grads[0], attn_one, attn_two)
    attn_rows = scatter_column(attn_last)
    return output, grad_frames, attn_rows, up_rows, down_rows


def on_device(
    sizes, frames, lengths, w_query, w_key, w_value, w_out, w_up, w_down,
    gain_attn, gain_mlp, cotangent,
):
    width = frames.shape[-1]
    blocks = place_table(sizes)
    rows_in = frames[0]
    valid = lax.broadcasted_iota(jnp.int32, (rows_in.shape[0], 1), 0) < lengths[0]
    branch = jnp.where(valid, cotangent[0], jnp.zeros_like(cotangent[0]))
    gains = jnp.pad(jnp.stack((gain_attn, gain_mlp), axis=1), ((0, 0), (0, LANES - 2)))
    attn = jnp.concatenate((w_query, w_key, w_value, w_out, gains), axis=1)
    layer = layer_plane if is_plane(sizes) else layer_whole
    output, grad_frames, attn_rows, up_rows, down_rows = layer(
        blocks, rows_in, lengths, branch, attn, w_up, w_down
    )
    grad_query, grad_key, grad_value, grad_out = (
        attn_rows[:, place * width : (place + 1) * width] for place in range(4)
    )
    gain_one = (
        jnp.sum(w_query.astype(F32) * grad_query, axis=1)
        + jnp.sum(w_key.astype(F32) * grad_key, axis=1)
        + jnp.sum(w_value.astype(F32) * grad_value, axis=1)
    ) / gain_attn.astype(F32)
    gain_two = jnp.sum(w_up.astype(F32) * up_rows, axis=1) / gain_mlp.astype(F32)
    return (
        output[None], grad_frames[None], grad_query, grad_key, grad_value, grad_out,
        up_rows, down_rows, gain_one, gain_two,
    )


def solution(mesh):
    wide, narrow = mesh.shape["wide"], mesh.shape["narrow"]
    y = 1
    while 4 * y * y <= wide:
        y *= 2
    sizes = {"z": wide // y, "y": y, "x": narrow // 2, "c": 2}
    fine = Mesh(mesh.devices.reshape(tuple(sizes[name] for name in ALL)), ALL)
    split = P(ALL)
    return jax.shard_map(
        functools.partial(on_device, sizes),
        mesh=fine,
        in_specs=(split,) * 11,
        out_specs=(split,) * 10,
        check_vma=False,
    )
```

```python
import functools

import jax
import jax.numpy as jnp
import numpy as np
from jax import lax
from jax.experimental import pallas as pl
from jax.experimental.pallas import tpu as pltpu
from jax.sharding import Mesh, PartitionSpec as P

HEADS = 16
HEAD_DIM = 64
EPSILON = 1e-06
FACTOR = HEAD_DIM ** (-0.5)
LANES = 128
Z_PARTS = 4
PIECES = 8
QUARTERS = 4
ALL = ("z", "y", "x", "c")
PLANE = ("y", "x", "c")
SWAP = [(0, 1), (1, 0)]
VMEM_MIB = {"forward": 32, "upward": 26, "downward": 26, "middle": 24, "attend_back": 26, "grads": 24, "result": 20, "frames": 20}
F32 = jnp.float32
BF16 = jnp.bfloat16
GELU_A = 0.7978845608028654
GELU_B = 0.044715

NN = (((1,), (0,)), ((), ()))
NT = (((1,), (1,)), ((), ()))
TN = (((0,), (0,)), ((), ()))


def mxu(left, right, dims=NN):
    return lax.dot_general(left, right, dims, preferred_element_type=F32)


def plane_pairs(step):
    pairs = []
    for y in range(2):
        for x in range(2):
            for c in range(2):
                flip_y = (c == 0) == (step == 1)
                to = (1 - y, x, c) if flip_y else (y, 1 - x, c)
                pairs.append(((y * 2 + x) * 2 + c, (to[0] * 2 + to[1]) * 2 + to[2]))
    return pairs


def is_plane(sizes):
    return sizes["x"] == 2 and sizes["y"] == 2 and sizes["c"] == 2 and sizes["z"] == Z_PARTS


def place_table(sizes):
    core = lax.axis_index("c")
    piece = jnp.arange(PIECES + QUARTERS + 1, dtype=jnp.int32)
    side = core ^ jnp.where(piece < PIECES, (piece >> 2) & 1, 0)
    first = (piece >> 1) & 1
    second = piece & 1
    if is_plane(sizes):
        y = lax.axis_index("y") ^ jnp.where(side == 0, first, second)
        x = lax.axis_index("x") ^ jnp.where(side == 0, second, first)
    else:
        y, x = first, second
    place = y * 2 + x
    place = jnp.where(piece < PIECES, place * 2 + side, place)
    return jnp.where(piece < PIECES + QUARTERS, place, core).astype(jnp.int32)


def after(value, *others):
    return lax.optimization_barrier((value,) + others)[0]


def first_hop(value, name="pieces"):
    with jax.named_scope(name):
        return lax.ppermute(value, PLANE, plane_pairs(1))


def second_hop(value, name="pieces"):
    with jax.named_scope(name):
        return lax.ppermute(value, PLANE, plane_pairs(2))


def across_cores(value, name="pieces"):
    with jax.named_scope(name):
        return lax.ppermute(value, "c", SWAP)


def with_other_core(near, far):
    other_near = across_cores(near, "other_near")
    far = after(far, other_near)
    return (near, far, other_near, across_cores(far, "other_far"))


def gather_column(shard):
    return lax.all_gather(shard, "z", axis=0, tiled=False)


def gather_whole(shard):
    full = lax.all_gather(shard, ALL, axis=0, tiled=True)
    full = full.reshape(Z_PARTS, 2, 2, 2, full.shape[0] // (Z_PARTS * PIECES), full.shape[1])
    even, odd = full[:, :, :, 0], full[:, :, :, 1]
    upper = lax.axis_index("c") == 1
    pieces = []
    for side in (jnp.where(upper, odd, even), jnp.where(upper, even, odd)):
        pieces += [jnp.swapaxes(side[:, :, second], 0, 1) for second in range(2)]
    return tuple(pieces)


def total(*parts):
    result = parts[0].astype(F32)
    for part in parts[1:]:
        result = result + part.astype(F32)
    return result


def low_total(*parts):
    return total(*parts).astype(BF16)


def scatter_column(mine):
    return lax.psum_scatter(mine, "z", scatter_dimension=0, tiled=False).astype(F32)


def scatter_whole(parts):
    mine = jnp.stack(parts, axis=1)[:, :, None]
    here = lax.broadcasted_iota(jnp.int32, (1, 1, 2, 1, 1), 2) == lax.axis_index("c")
    full = jnp.where(here, mine, jnp.zeros_like(mine))
    full = full.reshape(-1, full.shape[-1])
    return lax.psum_scatter(full, ALL, scatter_dimension=0, tiled=True).astype(F32)


COST_SHARE = 0.02


def cost(flops, bytes_accessed, transcendentals):
    return pl.CostEstimate(
        flops=int(COST_SHARE * flops), bytes_accessed=int(COST_SHARE * bytes_accessed),
        transcendentals=int(COST_SHARE * transcendentals),
    )


def in_hbm(pieces):
    return [pltpu.with_memory_space_constraint(part, pltpu.HBM) for part in pieces]


def params(name):
    return pltpu.CompilerParams(vmem_limit_bytes=VMEM_MIB[name] << 20)


HBM_SPEC = pl.BlockSpec(memory_space=pl.ANY)
SMEM_SPEC = pl.BlockSpec(memory_space=pltpu.SMEM)


def whole(shape):
    return pl.BlockSpec(
        shape, lambda *_: (0,) * len(shape), pipeline_mode=pl.Buffered(1)
    )


def low_part(shape):
    return pl.BlockSpec(shape, lambda j: (0, jnp.minimum(j, Z_PARTS // 2 - 1)))


def high_part(shape):
    return pl.BlockSpec(shape, lambda j: (0, jnp.maximum(j - Z_PARTS // 2, 0)))


def piece_copies(pieces, blocks, held, sems, columns):
    rows = pieces[0].shape[2]
    copies = []
    for piece in range(PIECES):
        own, first, second = piece >> 2, (piece >> 1) & 1, piece & 1
        source = pieces[2 * own + second].at[first, :, :, columns]
        start = pl.multiple_of(blocks[piece] * rows, rows)
        copies.append(
            pltpu.make_async_copy(source, held.at[:, pl.ds(start, rows), :], sems.at[piece])
        )
    return copies


def packed_copies(pieces, blocks, part, held, sems):
    rows = held.shape[1] // PIECES
    copies = []
    for piece in range(PIECES):
        own, first, second = piece >> 2, (piece >> 1) & 1, piece & 1
        source = pieces[2 * own + second].at[first, :, pl.ds(part * rows, rows), :]
        start = pl.multiple_of(blocks[piece] * rows, rows)
        copies.append(
            pltpu.make_async_copy(source, held.at[:, pl.ds(start, rows), :], sems.at[piece])
        )
    return copies


def part_copies(pieces, blocks, part, held, sems, by_class=False):
    rows = pieces[0].shape[2]
    copies = []
    for piece in range(PIECES):
        own, first, second = piece >> 2, (piece >> 1) & 1, piece & 1
        source = pieces[2 * own + second].at[part, first]
        place = QUARTERS * own + (blocks[piece] >> 1) if by_class else blocks[piece]
        start = pl.multiple_of(place * rows, rows)
        copies.append(
            pltpu.make_async_copy(source, held.at[pl.ds(start, rows), :], sems.at[piece])
        )
    return copies


def grad_copies(held, outs, table, columns, sems):
    rows = outs[0].shape[1]
    copies = []
    for piece in range(QUARTERS):
        target = outs[piece].at[:, :, columns]
        start = pl.multiple_of(table[PIECES + piece] * rows, rows)
        copies.append(
            pltpu.make_async_copy(held.at[:, pl.ds(start, rows), :], target, sems.at[piece])
        )
    return copies


def grad_part_copies(held, outs, table, part, sems):
    rows = outs[0].shape[1]
    copies = []
    for piece in range(QUARTERS):
        target = outs[piece].at[part]
        start = pl.multiple_of(table[PIECES + piece] * rows, rows)
        copies.append(
            pltpu.make_async_copy(held.at[pl.ds(start, rows), :], target, sems.at[piece])
        )
    return copies


def start_all(copies):
    for copy in copies:
        copy.start()


def wait_all(copies):
    for copy in copies:
        copy.wait()


def prefetch(step, steps, copies):
    @pl.when(step == 0)
    def _():
        start_all(copies(0))
        start_all(copies(1))

    for part in range(steps):

        @pl.when(step == part)
        def _():
            if part + 2 < steps:
                start_all(copies(part + 2))
            wait_all(copies(part))


def flat(block):
    return block.reshape(block.shape[0] * block.shape[1], block.shape[2])


def inverse_rms(rows):
    return lax.rsqrt(jnp.mean(rows * rows, axis=-1, keepdims=True) + EPSILON)


def store(source, target, sem):
    return pltpu.make_async_copy(source, target, sem)


def lane_pair(pair):
    return pl.ds(pl.multiple_of(pair * LANES, LANES), LANES)


def pack_kernel(w_query, w_key, w_value, w_out, gains, w_up, attn, upper):
    width = w_query.shape[1]
    rows = w_up.shape[0]
    for part, weight in enumerate((w_query, w_key, w_value, w_out)):
        attn[:, part * width : (part + 1) * width] = weight[...]
    attn[:, 4 * width :] = gains[...]
    for block in range(w_up.shape[1] // width):
        upper[block * rows : (block + 1) * rows, :] = w_up[:, block * width : (block + 1) * width]


def pack_call(w_query, w_key, w_value, w_out, gains, w_up):
    rows, width = w_query.shape
    return pl.pallas_call(
        pack_kernel,
        out_shape=[
            jax.ShapeDtypeStruct((rows, 4 * width + gains.shape[1]), BF16),
            jax.ShapeDtypeStruct((w_up.shape[1] // width * rows, width), BF16),
        ],
        name="pack",
    )(w_query, w_key, w_value, w_out, gains, w_up)


def split_turned(table, value, place, turned, own, other):
    turned[...] = value.T
    rows = turned.shape[0] // (Z_PARTS * PIECES)
    core = table[PIECES + QUARTERS]
    for block in range(Z_PARTS * QUARTERS):
        here = pl.ds(block * rows, rows)
        mine = pl.multiple_of((2 * block + core) * rows, rows)
        rest = pl.multiple_of((2 * block + 1 - core) * rows, rows)
        own[place, here, :] = turned[pl.ds(mine, rows), :]
        other[place, here, :] = turned[pl.ds(rest, rows), :]


def forward_kernel(
    blocks, length, frames, p0, p1, p2, p3,
    qkv_out, own_turned, other_turned, gains, log_totals, middle, second,
    held, gain_held, hidden, qkv, mixed, turned, sems, out_sems,
):
    pieces = (p0, p1, p2, p3)
    rows, width = frames.shape
    gain_copies = piece_copies(pieces, blocks, gain_held, sems.at[4], pl.ds(4 * width, LANES))
    copies = [
        piece_copies(pieces, blocks, held.at[part], sems.at[part], pl.ds(part * width, width))
        for part in range(4)
    ]
    start_all(gain_copies)
    for part in range(4):
        start_all(copies[part])
    value = frames[...].astype(F32)
    normal = value * inverse_rms(value)
    wait_all(gain_copies)
    across = flat(gain_held[...]).astype(F32).T
    gains[...] = across[:8]
    hidden[...] = (normal * across[0:1]).astype(BF16)
    leaving = []
    split_turned(blocks, hidden[...], 0, turned, own_turned, other_turned)
    for part in range(3):
        wait_all(copies[part])
        result = mxu(hidden[...], flat(held[part])).astype(BF16)
        if part == 0:
            result = (result.astype(F32) * FACTOR).astype(BF16)
        qkv[part] = result
        leaving.append(store(qkv.at[part], qkv_out.at[part], out_sems.at[part]))
        leaving[-1].start()

    bias = jnp.where(
        lax.broadcasted_iota(jnp.int32, (rows, 1), 0) < length[0], 0.0, -1e30
    ).astype(F32)
    lane = lax.broadcasted_iota(jnp.int32, (rows, LANES), 1)

    @pl.loop(0, width // LANES)
    def _(pair):
        here = lane_pair(pair)
        query, key, value = qkv[0, :, here], qkv[1, :, here], qkv[2, :, here]
        outs = []
        for half in range(2):
            mine = (lane < HEAD_DIM) == (half == 0)
            scores = mxu(key, jnp.where(mine, query, jnp.zeros_like(query)), NT) + bias
            peak = jnp.max(scores, axis=0, keepdims=True)
            expon = jnp.exp(scores - peak)
            sums = jnp.sum(expon, axis=0, keepdims=True)
            log_totals[pl.ds(2 * pair + half, 1), :] = peak + jnp.log(sums)
            shares = (expon * (1.0 / sums)).astype(BF16)
            outs.append(mxu(shares, value, TN))
        mixed[:, here] = jnp.where(lane < HEAD_DIM, outs[0], outs[1]).astype(BF16)

    split_turned(blocks, mixed[...], 1, turned, own_turned, other_turned)
    wait_all(copies[3])
    result = frames[...].astype(F32) + mxu(mixed[...], flat(held[3]))
    middle[...] = result
    low = (result * inverse_rms(result) * gains[1:2, :]).astype(BF16)
    second[...] = low
    split_turned(blocks, low, 2, turned, own_turned, other_turned)
    wait_all(leaving)


def forward_call(blocks, length, frames, pieces):
    rows, width = frames.shape
    turned = pltpu.HBM((3, width // 2, rows), BF16)
    return pl.pallas_call(
        forward_kernel,
        grid=(1,),
        in_specs=[SMEM_SPEC, SMEM_SPEC, whole((rows, width))] + [HBM_SPEC] * 4,
        out_specs=[HBM_SPEC, whole((3, width // 2, rows)), whole((3, width // 2, rows))]
        + [whole((8, width)), whole((HEADS, rows)), whole((rows, width)), whole((rows, width))],
        out_shape=[
            pltpu.HBM((3, rows, width), BF16),
            turned,
            turned,
            jax.ShapeDtypeStruct((8, width), F32),
            jax.ShapeDtypeStruct((HEADS, rows), F32),
            pltpu.HBM((rows, width), F32),
            pltpu.HBM((rows, width), BF16),
        ],
        scratch_shapes=[
            pltpu.VMEM((4, Z_PARTS, width // Z_PARTS, width), BF16),
            pltpu.VMEM((Z_PARTS, width // Z_PARTS, LANES), BF16),
            pltpu.VMEM((rows, width), BF16),
            pltpu.VMEM((3, rows, width), BF16),
            pltpu.VMEM((rows, width), BF16),
            pltpu.VMEM((width, rows), BF16),
            pltpu.SemaphoreType.DMA((5, PIECES)),
            pltpu.SemaphoreType.DMA((3,)),
        ],
        compiler_params=params("forward"),
        cost_estimate=cost(10 * rows * width * width, 16 * width * width, rows * rows),
        name="forward",
    )(blocks, length, *in_hbm([frames]), *pieces)


def up_kernel(
    blocks, second, p0, p1, p2, p3, slope, own, low_half, high_half, held, active, sems,
):
    step = pl.program_id(0)
    pieces = (p0, p1, p2, p3)

    def copies(part):
        return packed_copies(pieces, blocks, part, held.at[part], sems.at[part])

    prefetch(step, Z_PARTS, copies)
    value = mxu(second[...], flat(held[step]))
    square = value * value
    bend = jnp.tanh(GELU_A * value * (1.0 + GELU_B * square))
    share = 0.5 * (1.0 + bend)
    active[...] = (value * share).astype(BF16)
    slope[...] = (
        share + 0.5 * value * (1.0 - bend * bend) * (GELU_A * (1.0 + 3.0 * GELU_B * square))
    ).astype(BF16)
    core = blocks[PIECES + QUARTERS]
    width = active.shape[1] // PIECES
    for block in range(QUARTERS):
        here = pl.ds(block * width, width)
        mine = pl.multiple_of((2 * block + core) * width, width)
        rest = pl.multiple_of((2 * block + 1 - core) * width, width)
        own[:, here] = active[:, pl.ds(mine, width)]

        @pl.when(step < Z_PARTS // 2)
        def _():
            low_half[:, here] = active[:, pl.ds(rest, width)]

        @pl.when(step >= Z_PARTS // 2)
        def _():
            high_half[:, here] = active[:, pl.ds(rest, width)]


def up_call(blocks, second, pieces):
    rows, width = second.shape
    inner = pieces[0].shape[2] * pieces[0].shape[3] * PIECES * Z_PARTS // width
    columns = inner // Z_PARTS
    quarter = pltpu.HBM((rows, inner // 4), BF16)
    return pl.pallas_call(
        up_kernel,
        grid=(Z_PARTS,),
        in_specs=[SMEM_SPEC, whole((rows, width))] + [HBM_SPEC] * 4,
        out_specs=[
            pl.BlockSpec((rows, columns), lambda j: (0, j)),
            pl.BlockSpec((rows, columns // 2), lambda j: (0, j)),
            low_part((rows, columns // 2)),
            high_part((rows, columns // 2)),
        ],
        out_shape=[
            jax.ShapeDtypeStruct((rows, inner), BF16),
            jax.ShapeDtypeStruct((rows, inner // 2), BF16),
            quarter,
            quarter,
        ],
        scratch_shapes=[
            pltpu.VMEM((Z_PARTS, Z_PARTS, width // Z_PARTS, columns), BF16),
            pltpu.VMEM((rows, columns), BF16),
            pltpu.SemaphoreType.DMA((Z_PARTS, PIECES)),
        ],
        compiler_params=params("upward"),
        cost_estimate=cost(2 * rows * width * inner, 2 * width * inner, rows * inner),
        name="upward",
    )(blocks, *in_hbm([second]), *pieces)


def down_grad_kernel(
    blocks, mine, low_half, high_half, branch, other_branch, g0, g1, away, grads, grad_sems,
):
    step = pl.program_id(0)
    slot = lax.rem(step, 2)

    def leave(part, at):
        return grad_part_copies(grads.at[at], (g0, g1, away.at[0], away.at[1]), blocks, part, grad_sems.at[at])

    @pl.when(step >= 2)
    def _():
        wait_all(leave(step - 2, slot))

    for half, theirs in enumerate((low_half, high_half)):

        @pl.when((step >= Z_PARTS // 2) == (half == 1))
        def _():
            grads[slot] = (
                mxu(mine[...], branch[...], TN) + mxu(theirs[...], other_branch[...], TN)
            ).astype(BF16)

    start_all(leave(step, slot))

    @pl.when(step == Z_PARTS - 1)
    def _():
        wait_all(leave(step - 1, 1 - slot))
        wait_all(leave(step, slot))


def down_grad_call(blocks, mine, halves, branch, other_branch):
    rows, width = branch.shape
    columns = mine.shape[1] // Z_PARTS
    grad = jax.ShapeDtypeStruct((Z_PARTS, columns // QUARTERS, width), BF16)
    part = pl.BlockSpec((rows, columns), lambda j: (0, j))
    return pl.pallas_call(
        down_grad_kernel,
        grid=(Z_PARTS,),
        in_specs=[
            SMEM_SPEC,
            part,
            low_part((rows, columns)),
            high_part((rows, columns)),
            whole((rows, width)),
            whole((rows, width)),
        ],
        out_specs=[HBM_SPEC] * 3,
        out_shape=[grad, grad, jax.ShapeDtypeStruct((2,) + grad.shape, BF16)],
        scratch_shapes=[
            pltpu.VMEM((2, columns, width), BF16),
            pltpu.SemaphoreType.DMA((2, QUARTERS)),
        ],
        compiler_params=params("grads"),
        cost_estimate=cost(8 * rows * width * columns, 8 * width * columns, 0),
        name="down_grads",
    )(blocks, mine, *halves, branch, other_branch)


def down_kernel(blocks, branch, slope, p0, p1, p2, p3, low_half, high_half, held, sems):
    step = pl.program_id(0)
    pieces = (p0, p1, p2, p3)

    def copies(part):
        return part_copies(pieces, blocks, part, held.at[part], sems.at[part])

    prefetch(step, Z_PARTS, copies)
    value = mxu(branch[...], held[step], NT)
    low = (value * slope[...].astype(F32)).astype(BF16)

    @pl.when(step < Z_PARTS // 2)
    def _():
        low_half[...] = low

    @pl.when(step >= Z_PARTS // 2)
    def _():
        high_half[...] = low


def down_call(blocks, branch, slope, pieces):
    rows, width = branch.shape
    inner = slope.shape[1]
    columns = inner // Z_PARTS
    half = Z_PARTS // 2
    out = jax.ShapeDtypeStruct((rows, inner // 2), BF16)
    return pl.pallas_call(
        down_kernel,
        grid=(Z_PARTS,),
        in_specs=[
            SMEM_SPEC,
            whole((rows, width)),
            pl.BlockSpec((rows, columns), lambda j: (0, j)),
        ]
        + [HBM_SPEC] * 4,
        out_specs=[
            pl.BlockSpec((rows, columns), lambda j: (0, jnp.minimum(j, half - 1))),
            pl.BlockSpec((rows, columns), lambda j: (0, jnp.maximum(j - half, 0))),
        ],
        out_shape=[out, out],
        scratch_shapes=[
            pltpu.VMEM((Z_PARTS, columns, width), BF16),
            pltpu.SemaphoreType.DMA((Z_PARTS, PIECES)),
        ],
        compiler_params=params("downward"),
        cost_estimate=cost(2 * rows * width * inner, 2 * width * inner, 0),
        name="downward",
    )(blocks, branch, slope, *pieces)


def up_grad_kernel(
    blocks, mine, theirs, low_half, high_half, low_other, high_other, g0, g1, g2, g3, grads, grad_sems,
):
    step = pl.program_id(0)
    slot = lax.rem(step, 2)
    columns = low_half.shape[1]

    def leave(part, at):
        start = pl.multiple_of(part * columns, columns)
        return grad_copies(
            grads.at[at], (g0, g1, g2, g3), blocks, pl.ds(start, columns), grad_sems.at[at]
        )

    @pl.when(step >= 2)
    def _():
        wait_all(leave(step - 2, slot))

    for half, (near, far) in enumerate(((low_half, low_other), (high_half, high_other))):

        @pl.when((step >= Z_PARTS // 2) == (half == 1))
        def _():
            grad = mxu(mine[0], near[...]) + mxu(theirs[0], far[...])
            grads[slot] = grad.astype(BF16).reshape(grads.shape[1:])

    start_all(leave(step, slot))

    @pl.when(step == Z_PARTS - 1)
    def _():
        wait_all(leave(step - 1, 1 - slot))
        wait_all(leave(step, slot))


def up_grad_call(blocks, own_turned, other_turned, halves, other_halves):
    _, width, rows = own_turned.shape
    inner = 2 * halves[0].shape[1]
    columns = inner // Z_PARTS
    half = Z_PARTS // 2
    part_rows = width // Z_PARTS
    grad = jax.ShapeDtypeStruct((Z_PARTS, part_rows // QUARTERS, inner), BF16)
    turned = pl.BlockSpec((1, width, rows), lambda j: (2, 0, 0), pipeline_mode=pl.Buffered(1))
    low = pl.BlockSpec((rows, columns), lambda j: (0, jnp.minimum(j, half - 1)))
    high = pl.BlockSpec((rows, columns), lambda j: (0, jnp.maximum(j - half, 0)))
    return pl.pallas_call(
        up_grad_kernel,
        grid=(Z_PARTS,),
        in_specs=[SMEM_SPEC, turned, turned, low, high, low, high],
        out_specs=[HBM_SPEC] * QUARTERS,
        out_shape=[grad] * QUARTERS,
        scratch_shapes=[
            pltpu.VMEM((2, Z_PARTS, part_rows, columns), BF16),
            pltpu.SemaphoreType.DMA((2, QUARTERS)),
        ],
        compiler_params=params("grads"),
        cost_estimate=cost(4 * rows * width * inner, 2 * width * inner, 0),
        name="up_grads",
    )(blocks, own_turned, other_turned, *halves, *other_halves)


def result_kernel(blocks, length, middle, own, low_half, high_half, p0, p1, p2, p3, output, held, sums, sems):
    step = pl.program_id(0)
    steps = Z_PARTS
    pieces = (p0, p1, p2, p3)

    def copies(part):
        return part_copies(pieces, blocks, part, held.at[part], sems.at[part], by_class=True)

    @pl.when(step == 0)
    def _():
        for part in range(steps):
            start_all(copies(part))
        sums[...] = middle[...]

    for part in range(steps):

        @pl.when(step == part)
        def _():
            wait_all(copies(part))

    half = own.shape[1]
    for place, other in enumerate((low_half, high_half)):

        @pl.when((step >= Z_PARTS // 2) == (place == 1))
        def _():
            sums[...] += mxu(own[...], held[step, :half, :]) + mxu(
                other[...], held[step, half:, :]
            )


    @pl.when(step == steps - 1)
    def _():
        valid = lax.broadcasted_iota(jnp.int32, (sums.shape[0], 1), 0) < length[0]
        output[...] = (sums[...] * valid.astype(F32)).astype(BF16)


def result_call(blocks, length, middle, own, halves, pieces):
    rows, width = middle.shape
    inner = 2 * own.shape[1]
    columns = inner // Z_PARTS
    return pl.pallas_call(
        result_kernel,
        grid=(Z_PARTS,),
        in_specs=[
            SMEM_SPEC,
            SMEM_SPEC,
            whole((rows, width)),
            pl.BlockSpec((rows, columns // 2), lambda j: (0, j)),
            low_part((rows, columns // 2)),
            high_part((rows, columns // 2)),
        ]
        + [HBM_SPEC] * 4,
        out_specs=whole((rows, width)),
        out_shape=jax.ShapeDtypeStruct((rows, width), BF16),
        scratch_shapes=[
            pltpu.VMEM((Z_PARTS, columns, width), BF16),
            pltpu.VMEM((rows, width), F32),
            pltpu.SemaphoreType.DMA((Z_PARTS, PIECES)),
        ],
        compiler_params=params("result"),
        cost_estimate=cost(
            flops=2 * rows * width * inner, bytes_accessed=3 * width * inner, transcendentals=0
        ),
        name="result",
    )(blocks, length, middle, own, *halves, *in_hbm(pieces))


def middle_kernel(
    blocks, branch, middle, gains, low_half, high_half, u0, u1, u2, u3, p0, p1, p2, p3,
    grad_middle, grad_attn, grad_mixed, held, out_held, sums, sems, out_sems,
):
    step = pl.program_id(0)
    steps = Z_PARTS
    width = middle.shape[1]

    def copies(part):
        return packed_copies((u0, u1, u2, u3), blocks, part, held.at[part], sems.at[part])

    out_copies = piece_copies(
        (p0, p1, p2, p3), blocks, out_held, out_sems, pl.ds(3 * width, width)
    )
    prefetch(step, steps, copies)

    @pl.when(step == 1)
    def _():
        start_all(out_copies)

    @pl.when(step == 0)
    def _():
        sums[...] = mxu(low_half[...], flat(held[step]), NT)

    @pl.when((step > 0) & (step < steps // 2))
    def _():
        sums[...] += mxu(low_half[...], flat(held[step]), NT)

    @pl.when(step >= steps // 2)
    def _():
        sums[...] += mxu(high_half[...], flat(held[step]), NT)

    @pl.when(step == steps - 1)
    def _():
        value = middle[...]
        inverse = inverse_rms(value)
        normal = value * inverse
        scaled = sums[...] * gains[1:2, :]
        mean = jnp.mean(scaled * normal, axis=-1, keepdims=True)
        result = branch[...].astype(F32) + inverse * (scaled - normal * mean)
        grad_middle[...] = result
        low = result.astype(BF16)
        grad_attn[...] = low
        wait_all(out_copies)
        grad_mixed[...] = mxu(low, flat(out_held[...]), NT).astype(BF16)


def middle_call(blocks, branch, middle, gains, halves, up_pieces, pieces):
    rows, width = middle.shape
    inner = 2 * halves[0].shape[1]
    half = Z_PARTS // 2
    columns = inner // Z_PARTS
    return pl.pallas_call(
        middle_kernel,
        grid=(Z_PARTS,),
        in_specs=[
            SMEM_SPEC,
            whole((rows, width)),
            whole((rows, width)),
            whole((8, width)),
            pl.BlockSpec((rows, columns), lambda j: (0, jnp.minimum(j, half - 1))),
            pl.BlockSpec((rows, columns), lambda j: (0, jnp.maximum(j - half, 0))),
        ]
        + [HBM_SPEC] * 8,
        out_specs=[whole((rows, width))] * 3,
        out_shape=[
            pltpu.HBM((rows, width), F32),
            jax.ShapeDtypeStruct((rows, width), BF16),
            jax.ShapeDtypeStruct((rows, width), BF16),
        ],
        scratch_shapes=[
            pltpu.VMEM((Z_PARTS, Z_PARTS, width // Z_PARTS, columns), BF16),
            pltpu.VMEM((Z_PARTS, width // Z_PARTS, width), BF16),
            pltpu.VMEM((rows, width), F32),
            pltpu.SemaphoreType.DMA((Z_PARTS, PIECES)),
            pltpu.SemaphoreType.DMA((PIECES,)),
        ],
        compiler_params=params("middle"),
        cost_estimate=cost(2 * rows * width * (inner + width), 3 * width * inner, 0),
        name="middle",
    )(blocks, branch, middle, gains, *halves, *up_pieces, *pieces)


def attend_back_kernel(
    length, queries, keys, values, log_totals, grads, grad_query, grad_key, grad_value,
):
    rows, width = grads.shape
    bias = jnp.where(
        lax.broadcasted_iota(jnp.int32, (rows, 1), 0) < length[0], 0.0, -1e30
    ).astype(F32)
    lane = lax.broadcasted_iota(jnp.int32, (rows, LANES), 1)

    @pl.loop(0, width // LANES)
    def _(pair):
        here = lane_pair(pair)
        query, key, value, grad = queries[0, :, here], keys[0, :, here], values[0, :, here], grads[:, here]
        parts = []
        for half in range(2):
            mine = (lane < HEAD_DIM) == (half == 0)
            scores = mxu(key, jnp.where(mine, query, jnp.zeros_like(query)), NT) + bias
            chance = jnp.exp(scores - log_totals[pl.ds(2 * pair + half, 1), :])
            to_value = mxu(chance.astype(BF16), grad)
            grad_chance = mxu(value, jnp.where(mine, grad, jnp.zeros_like(grad)), NT)
            mean = jnp.sum(chance * grad_chance, axis=0, keepdims=True)
            grad_scores = (chance * (grad_chance - mean)).astype(BF16)
            to_key = mxu(grad_scores, query)
            to_query = mxu(grad_scores, key, TN) * FACTOR
            parts.append((to_query, to_key, to_value))
        for place, out in enumerate((grad_query, grad_key, grad_value)):
            out[:, here] = jnp.where(lane < HEAD_DIM, parts[0][place], parts[1][place]).astype(BF16)


def attend_back_call(length, log_totals, qkv, grad_mixed):
    rows, width = grad_mixed.shape

    def plane(place):
        return pl.BlockSpec(
            (1, rows, width), lambda j: (place, 0, 0), pipeline_mode=pl.Buffered(1)
        )

    return pl.pallas_call(
        attend_back_kernel,
        grid=(1,),
        in_specs=[
            SMEM_SPEC, plane(0), plane(1), plane(2), whole((HEADS, rows)), whole((rows, width)),
        ],
        out_specs=[whole((rows, width))] * 3,
        out_shape=[jax.ShapeDtypeStruct((rows, width), BF16)] * 3,
        compiler_params=params("attend_back"),
        cost_estimate=cost(20 * rows * width * width, 40 * width * width, rows * rows),
        name="attend_back",
    )(length, qkv, qkv, qkv, log_totals, grad_mixed)


def attn_grad_kernel(
    blocks, mine_in, theirs_in, a0, a1, a2, a3, b0, b1, b2, b3, g0, g1, g2, g3,
    turned, near, far, grads, turned_sems, load_sems, grad_sems,
):
    columns = a0.shape[1]
    turned_loads = [
        store(source.at[pl.ds(0, 2)], turned.at[at], turned_sems.at[at])
        for at, source in enumerate((mine_in, theirs_in))
    ]
    start_all(turned_loads)
    loads = []
    for part, sources in enumerate(((a0, b0), (a1, b1), (a2, b2), (a3, b3))):
        loads.append(
            [
                store(source, target.at[part], load_sems.at[at, part])
                for at, (source, target) in enumerate(zip(sources, (near, far)))
            ]
        )
        start_all(loads[part])
    wait_all(turned_loads)
    pending = []
    for part in range(4):
        wait_all(loads[part])
        left = part // 3
        grad = mxu(turned[0, left], near[part]) + mxu(turned[1, left], far[part])
        grads[part] = grad.astype(BF16).reshape(grads.shape[1:])
        pending.append(
            grad_copies(
                grads.at[part], (g0, g1, g2, g3), blocks, pl.ds(part * columns, columns), grad_sems.at[part]
            )
        )
        start_all(pending[part])
    for copies in pending:
        wait_all(copies)


def attn_grad_call(blocks, own_turned, other_turned, near, far):
    _, width, rows = own_turned.shape
    columns = near[0].shape[1]
    part_rows = width // Z_PARTS
    grad = jax.ShapeDtypeStruct((Z_PARTS, part_rows // QUARTERS, 4 * columns), BF16)
    return pl.pallas_call(
        attn_grad_kernel,
        grid=(1,),
        in_specs=[SMEM_SPEC] + [HBM_SPEC] * 10,
        out_specs=[HBM_SPEC] * QUARTERS,
        out_shape=[grad] * QUARTERS,
        scratch_shapes=[
            pltpu.VMEM((2, 2, width, rows), BF16),
            pltpu.VMEM((4, rows, columns), BF16),
            pltpu.VMEM((4, rows, columns), BF16),
            pltpu.VMEM((4, Z_PARTS, part_rows, columns), BF16),
            pltpu.SemaphoreType.DMA((2,)),
            pltpu.SemaphoreType.DMA((2, 4)),
            pltpu.SemaphoreType.DMA((4, QUARTERS)),
        ],
        compiler_params=params("grads"),
        cost_estimate=cost(16 * rows * width * columns, 16 * width * columns, 0),
        name="attn_grads",
    )(blocks, own_turned, other_turned, *near, *far)


def frames_kernel(
    blocks, frames, gains, grad_middle, grad_query, grad_key, grad_value, p0, p1, p2, p3, grad_frames,
    held, sums, sems,
):
    step = pl.program_id(0)
    width = frames.shape[1]

    def copies(part):
        return piece_copies(
            (p0, p1, p2, p3), blocks, held.at[part], sems.at[part], pl.ds(part * width, width)
        )

    prefetch(step, 3, copies)
    for part, grad in enumerate((grad_query, grad_key, grad_value)):

        @pl.when(step == part)
        def _():
            term = mxu(grad[...], flat(held[part]), NT)
            sums[...] = term if part == 0 else sums[...] + term

    @pl.when(step == 2)
    def _():
        rows = frames[...].astype(F32)
        inverse = inverse_rms(rows)
        normal = rows * inverse
        scaled = sums[...] * gains[0:1, :]
        mean = jnp.mean(scaled * normal, axis=-1, keepdims=True)
        grad_frames[...] = grad_middle[...] + inverse * (scaled - normal * mean)


def frames_call(blocks, frames, gains, grad_middle, grad_qkv, pieces):
    rows, width = frames.shape
    return pl.pallas_call(
        frames_kernel,
        grid=(3,),
        in_specs=[
            SMEM_SPEC,
            whole((rows, width)),
            whole((8, width)),
            whole((rows, width)),
            whole((rows, width)),
            whole((rows, width)),
            whole((rows, width)),
        ]
        + [HBM_SPEC] * 4,
        out_specs=whole((rows, width)),
        out_shape=jax.ShapeDtypeStruct((rows, width), F32),
        scratch_shapes=[
            pltpu.VMEM((3, Z_PARTS, width // Z_PARTS, width), BF16),
            pltpu.VMEM((rows, width), F32),
            pltpu.SemaphoreType.DMA((3, PIECES)),
        ],
        compiler_params=params("frames"),
        cost_estimate=cost(6 * rows * width * width, 10 * width * width, 0),
        name="frames_back",
    )(blocks, frames, gains, grad_middle, *grad_qkv, *in_hbm(pieces))


def kernels_chain(blocks, rows_in, lengths, branch, attn_pieces, up_pieces, down_pieces, swap):
    qkv, own_turned, other_turned, gain_rows, log_totals, middle, second = forward_call(
        blocks, lengths, rows_in, attn_pieces
    )
    their_turned = swap(other_turned)
    slope, active, *other_active = up_call(blocks, second, up_pieces)
    down_grads = down_grad_call(
        blocks, active, [swap(half) for half in other_active], branch, swap(branch)
    )
    halves = down_call(blocks, branch, slope, down_pieces)
    grad_middle, grad_attn, grad_mixed = middle_call(
        blocks, branch, middle, gain_rows, halves, up_pieces, attn_pieces
    )
    up_grads = up_grad_call(
        blocks, own_turned, their_turned, halves, [swap(half) for half in halves]
    )
    grad_qkv = attend_back_call(lengths, log_totals, qkv, grad_mixed)
    factors = (*grad_qkv, grad_attn)
    attn_grads = attn_grad_call(
        blocks, own_turned, their_turned, factors, [swap(factor) for factor in factors]
    )
    output = result_call(blocks, lengths, middle, active, other_active, down_pieces)
    grad_frames = frames_call(blocks, rows_in, gain_rows, grad_middle, grad_qkv, attn_pieces)
    return output, grad_frames, attn_grads, up_grads, (*down_grads[:2], *down_grads[2])


def layer_whole(blocks, rows_in, lengths, branch, attn, upper, w_down):
    attn_pieces, down_pieces = (gather_whole(part) for part in (attn, w_down))
    rows = attn.shape[0]
    parts = [gather_whole(upper[at : at + rows]) for at in range(0, upper.shape[0], rows)]
    up_pieces = tuple(jnp.concatenate(part, axis=-2) for part in zip(*parts))
    down_pieces = tuple(jnp.swapaxes(part, 0, 1) for part in down_pieces)
    output, grad_frames, *grads = kernels_chain(
        blocks, rows_in, lengths, branch, attn_pieces, up_pieces, down_pieces, across_cores
    )
    return (output, grad_frames) + tuple(scatter_whole(part) for part in grads)


def layer_plane(blocks, rows_in, lengths, branch, attn, upper, w_down):
    attn_column = gather_column(attn)
    up_column = gather_column(upper)
    down_near = jnp.stack((w_down, first_hop(w_down)))
    their_branch = across_cores(branch, "their_branch")
    attn_column = after(attn_column, down_near, their_branch)
    down_near = gather_column(down_near)
    attn_near = jnp.stack((attn_column, first_hop(attn_column)))
    attn_far = second_hop(attn_near, "attn_far")
    up_column = after(up_column, attn_near)
    up_next = first_hop(up_column, "up_next")
    attn_pieces = with_other_core(attn_near, attn_far)
    up_near = jnp.stack((up_column, up_next))
    up_far = second_hop(up_near, "up_far")

    qkv, own_turned, other_turned, gain_rows, log_totals, middle, second = forward_call(
        blocks, lengths, after(rows_in, up_near), attn_pieces
    )

    up_far = after(up_far, second, down_near)
    up_pieces = with_other_core(up_near, up_far)
    down_near = after(down_near, up_far)
    down_far = second_hop(down_near, "down_far")
    slope, active, *other_active = up_call(blocks, after(second, down_near), up_pieces)
    their_active = [across_cores(half, "their_active") for half in other_active]
    their_turned = across_cores(after(other_turned, slope), "their_turned")
    down_grads = down_grad_call(blocks, active, their_active, branch, their_branch)
    down_one = first_hop(down_grads[2], "down_one")

    down_pieces = with_other_core(down_near, after(down_far, down_grads[0]))
    halves = down_call(blocks, after(branch, down_grads[0]), slope, down_pieces)
    their_halves = [across_cores(half, "their_half") for half in halves]
    grad_middle, grad_attn, grad_mixed = middle_call(
        blocks, branch, middle, gain_rows, halves, up_pieces, attn_pieces
    )
    their_attn = across_cores(grad_attn, "their_attn")
    down_one = after(down_one, grad_mixed)
    down_away = low_total(down_grads[1], down_one[1])
    down_two = second_hop(down_away, "down_two")
    up_grads = up_grad_call(
        blocks, after(own_turned, down_away), their_turned, halves, their_halves
    )
    up_one_away = first_hop(up_grads[3], "up_one_away")
    up_one = first_hop(up_grads[2], "up_one")
    grad_qkv = attend_back_call(lengths, log_totals, qkv, after(grad_mixed, up_grads[0]))
    their_qkv = [across_cores(grad, "their_qkv") for grad in grad_qkv]

    down_two = after(down_two, grad_qkv[0])
    down_last = low_total(down_grads[0], down_one[0], down_two)
    down_rows = scatter_column(down_last)
    up_one_away = after(up_one_away, down_last, up_one)
    up_away = low_total(up_grads[1], up_one_away)
    up_two = second_hop(up_away, "up_two")
    attn_grads = attn_grad_call(
        blocks, after(own_turned, up_away), their_turned, (*grad_qkv, grad_attn),
        (*their_qkv, their_attn),
    )
    attn_one_away = first_hop(attn_grads[3], "attn_one_away")
    attn_one = first_hop(attn_grads[2], "attn_one")
    grad_frames = frames_call(
        blocks, rows_in, gain_rows, after(grad_middle, attn_grads[0]), grad_qkv, attn_pieces
    )

    up_two = after(up_two, grad_frames)
    up_last = low_total(up_grads[0], up_one, up_two)
    up_rows = scatter_column(up_last)
    attn_one_away = after(attn_one_away, up_last)
    attn_away = low_total(attn_grads[1], attn_one_away)
    attn_two = second_hop(attn_away, "attn_two")
    output = result_call(
        blocks, lengths, after(middle, attn_away), active, other_active, down_pieces
    )
    attn_one = after(attn_one, output)
    attn_last = low_total(attn_grads[0], attn_one, attn_two)
    attn_rows = scatter_column(attn_last)
    return output, grad_frames, attn_rows, up_rows, down_rows


def on_device(
    sizes, frames, lengths, w_query, w_key, w_value, w_out, w_up, w_down,
    gain_attn, gain_mlp, cotangent,
):
    width = frames.shape[-1]
    blocks = place_table(sizes)
    rows_in = frames[0]
    valid = lax.broadcasted_iota(jnp.int32, (rows_in.shape[0], 1), 0) < lengths[0]
    branch = jnp.where(valid, cotangent[0], jnp.zeros_like(cotangent[0]))
    gains = jnp.pad(jnp.stack((gain_attn, gain_mlp), axis=1), ((0, 0), (0, LANES - 2)))
    attn, upper = pack_call(w_query, w_key, w_value, w_out, gains, w_up)
    layer = layer_plane if is_plane(sizes) else layer_whole
    output, grad_frames, attn_rows, up_rows, down_rows = layer(
        blocks, rows_in, lengths, branch, attn, upper, w_down
    )
    grad_query, grad_key, grad_value, grad_out = (
        attn_rows[:, place * width : (place + 1) * width] for place in range(4)
    )
    gain_one = (
        jnp.sum(w_query.astype(F32) * grad_query, axis=1)
        + jnp.sum(w_key.astype(F32) * grad_key, axis=1)
        + jnp.sum(w_value.astype(F32) * grad_value, axis=1)
    ) / gain_attn.astype(F32)
    gain_two = jnp.sum(w_up.astype(F32) * up_rows, axis=1) / gain_mlp.astype(F32)
    return (
        output[None], grad_frames[None], grad_query, grad_key, grad_value, grad_out,
        up_rows, down_rows, gain_one, gain_two,
    )


def solution(mesh):
    wide, narrow = mesh.shape["wide"], mesh.shape["narrow"]
    y = 1
    while 4 * y * y <= wide:
        y *= 2
    sizes = {"z": wide // y, "y": y, "x": narrow // 2, "c": 2}
    fine = Mesh(mesh.devices.reshape(tuple(sizes[name] for name in ALL)), ALL)
    split = P(ALL)
    return jax.shard_map(
        functools.partial(on_device, sizes),
        mesh=fine,
        in_specs=(split,) * 11,
        out_specs=(split,) * 10,
        check_vma=False,
    )
```

```python
import functools

import jax
import jax.numpy as jnp
import numpy as np
from jax import lax
from jax.experimental import pallas as pl
from jax.experimental.pallas import tpu as pltpu
from jax.sharding import Mesh, PartitionSpec as P

HEADS = 16
HEAD_DIM = 64
EPSILON = 1e-06
FACTOR = HEAD_DIM ** (-0.5)
LANES = 128
Z_PARTS = 4
PIECES = 8
QUARTERS = 4
ALL = ("z", "y", "x", "c")
PLANE = ("y", "x", "c")
SWAP = [(0, 1), (1, 0)]
VMEM_MIB = {"forward": 32, "upward": 26, "downward": 26, "middle": 24, "attend_back": 26, "grads": 24, "result": 20, "frames": 20}
F32 = jnp.float32
BF16 = jnp.bfloat16
GELU_A = 0.7978845608028654
GELU_B = 0.044715

NN = (((1,), (0,)), ((), ()))
NT = (((1,), (1,)), ((), ()))
TN = (((0,), (0,)), ((), ()))


def mxu(left, right, dims=NN):
    return lax.dot_general(left, right, dims, preferred_element_type=F32)


def plane_pairs(step):
    pairs = []
    for y in range(2):
        for x in range(2):
            for c in range(2):
                flip_y = (c == 0) == (step == 1)
                to = (1 - y, x, c) if flip_y else (y, 1 - x, c)
                pairs.append(((y * 2 + x) * 2 + c, (to[0] * 2 + to[1]) * 2 + to[2]))
    return pairs


def is_plane(sizes):
    return sizes["x"] == 2 and sizes["y"] == 2 and sizes["c"] == 2 and sizes["z"] == Z_PARTS


def place_table(sizes):
    core = lax.axis_index("c")
    piece = jnp.arange(PIECES + QUARTERS + 1, dtype=jnp.int32)
    side = core ^ jnp.where(piece < PIECES, (piece >> 2) & 1, 0)
    first = (piece >> 1) & 1
    second = piece & 1
    if is_plane(sizes):
        y = lax.axis_index("y") ^ jnp.where(side == 0, first, second)
        x = lax.axis_index("x") ^ jnp.where(side == 0, second, first)
    else:
        y, x = first, second
    place = y * 2 + x
    place = jnp.where(piece < PIECES, place * 2 + side, place)
    return jnp.where(piece < PIECES + QUARTERS, place, core).astype(jnp.int32)


def after(value, *others):
    return lax.optimization_barrier((value,) + others)[0]


def first_hop(value, name="pieces"):
    with jax.named_scope(name):
        return lax.ppermute(value, PLANE, plane_pairs(1))


def second_hop(value, name="pieces"):
    with jax.named_scope(name):
        return lax.ppermute(value, PLANE, plane_pairs(2))


def across_cores(value, name="pieces"):
    with jax.named_scope(name):
        return lax.ppermute(value, "c", SWAP)


def with_other_core(near, far):
    other_near = across_cores(near, "other_near")
    far = after(far, other_near)
    return (near, far, other_near, across_cores(far, "other_far"))


def gather_column(shard):
    return lax.all_gather(shard, "z", axis=0, tiled=False)


def gather_whole(shard):
    full = lax.all_gather(shard, ALL, axis=0, tiled=True)
    full = full.reshape(Z_PARTS, 2, 2, 2, full.shape[0] // (Z_PARTS * PIECES), full.shape[1])
    even, odd = full[:, :, :, 0], full[:, :, :, 1]
    upper = lax.axis_index("c") == 1
    pieces = []
    for side in (jnp.where(upper, odd, even), jnp.where(upper, even, odd)):
        pieces += [jnp.swapaxes(side[:, :, second], 0, 1) for second in range(2)]
    return tuple(pieces)


def total(*parts):
    result = parts[0].astype(F32)
    for part in parts[1:]:
        result = result + part.astype(F32)
    return result


def low_total(*parts):
    return total(*parts).astype(BF16)


def scatter_column(mine):
    return lax.psum_scatter(mine, "z", scatter_dimension=0, tiled=False).astype(F32)


def scatter_whole(parts):
    mine = jnp.stack(parts, axis=1)[:, :, None]
    here = lax.broadcasted_iota(jnp.int32, (1, 1, 2, 1, 1), 2) == lax.axis_index("c")
    full = jnp.where(here, mine, jnp.zeros_like(mine))
    full = full.reshape(-1, full.shape[-1])
    return lax.psum_scatter(full, ALL, scatter_dimension=0, tiled=True).astype(F32)


COST_SHARE = 0.02


def cost(flops, bytes_accessed, transcendentals):
    return pl.CostEstimate(
        flops=int(COST_SHARE * flops), bytes_accessed=int(COST_SHARE * bytes_accessed),
        transcendentals=int(COST_SHARE * transcendentals),
    )


def in_hbm(pieces):
    return [pltpu.with_memory_space_constraint(part, pltpu.HBM) for part in pieces]


def params(name):
    return pltpu.CompilerParams(vmem_limit_bytes=VMEM_MIB[name] << 20)


HBM_SPEC = pl.BlockSpec(memory_space=pl.ANY)
SMEM_SPEC = pl.BlockSpec(memory_space=pltpu.SMEM)


def whole(shape):
    return pl.BlockSpec(
        shape, lambda *_: (0,) * len(shape), pipeline_mode=pl.Buffered(1)
    )


def low_part(shape):
    return pl.BlockSpec(shape, lambda j: (0, jnp.minimum(j, Z_PARTS // 2 - 1)))


def high_part(shape):
    return pl.BlockSpec(shape, lambda j: (0, jnp.maximum(j - Z_PARTS // 2, 0)))


def piece_copies(pieces, blocks, held, sems, columns):
    rows = pieces[0].shape[2]
    copies = []
    for piece in range(PIECES):
        own, first, second = piece >> 2, (piece >> 1) & 1, piece & 1
        source = pieces[2 * own + second].at[first, :, :, columns]
        start = pl.multiple_of(blocks[piece] * rows, rows)
        copies.append(
            pltpu.make_async_copy(source, held.at[:, pl.ds(start, rows), :], sems.at[piece])
        )
    return copies


def packed_copies(pieces, blocks, part, held, sems):
    rows = held.shape[1] // PIECES
    copies = []
    for piece in range(PIECES):
        own, first, second = piece >> 2, (piece >> 1) & 1, piece & 1
        source = pieces[2 * own + second].at[first, :, pl.ds(part * rows, rows), :]
        start = pl.multiple_of(blocks[piece] * rows, rows)
        copies.append(
            pltpu.make_async_copy(source, held.at[:, pl.ds(start, rows), :], sems.at[piece])
        )
    return copies


def part_copies(pieces, blocks, part, held, sems, by_class=False):
    rows = pieces[0].shape[2]
    copies = []
    for piece in range(PIECES):
        own, first, second = piece >> 2, (piece >> 1) & 1, piece & 1
        source = pieces[2 * own + second].at[part, first]
        place = QUARTERS * own + (blocks[piece] >> 1) if by_class else blocks[piece]
        start = pl.multiple_of(place * rows, rows)
        copies.append(
            pltpu.make_async_copy(source, held.at[pl.ds(start, rows), :], sems.at[piece])
        )
    return copies


def grad_copies(held, outs, table, columns, sems):
    rows = outs[0].shape[1]
    copies = []
    for piece in range(QUARTERS):
        target = outs[piece].at[:, :, columns]
        start = pl.multiple_of(table[PIECES + piece] * rows, rows)
        copies.append(
            pltpu.make_async_copy(held.at[:, pl.ds(start, rows), :], target, sems.at[piece])
        )
    return copies


def grad_part_copies(held, outs, table, part, sems):
    rows = outs[0].shape[1]
    copies = []
    for piece in range(QUARTERS):
        target = outs[piece].at[part]
        start = pl.multiple_of(table[PIECES + piece] * rows, rows)
        copies.append(
            pltpu.make_async_copy(held.at[pl.ds(start, rows), :], target, sems.at[piece])
        )
    return copies


def start_all(copies):
    for copy in copies:
        copy.start()


def wait_all(copies):
    for copy in copies:
        copy.wait()


def prefetch(step, steps, copies):
    @pl.when(step == 0)
    def _():
        start_all(copies(0))
        start_all(copies(1))

    for part in range(steps):

        @pl.when(step == part)
        def _():
            if part + 2 < steps:
                start_all(copies(part + 2))
            wait_all(copies(part))


def flat(block):
    return block.reshape(block.shape[0] * block.shape[1], block.shape[2])


def inverse_rms(rows):
    return lax.rsqrt(jnp.mean(rows * rows, axis=-1, keepdims=True) + EPSILON)


def store(source, target, sem):
    return pltpu.make_async_copy(source, target, sem)


def lane_pair(pair):
    return pl.ds(pl.multiple_of(pair * LANES, LANES), LANES)


def pack_kernel(w_query, w_key, w_value, w_out, gains, w_up, attn, upper):
    width = w_query.shape[1]
    rows = w_up.shape[0]
    for part, weight in enumerate((w_query, w_key, w_value, w_out)):
        attn[:, part * width : (part + 1) * width] = weight[...]
    attn[:, 4 * width :] = gains[...]
    for block in range(w_up.shape[1] // width):
        upper[block * rows : (block + 1) * rows, :] = w_up[:, block * width : (block + 1) * width]


def pack_call(w_query, w_key, w_value, w_out, gains, w_up):
    rows, width = w_query.shape
    return pl.pallas_call(
        pack_kernel,
        out_shape=[
            jax.ShapeDtypeStruct((rows, 4 * width + gains.shape[1]), BF16),
            jax.ShapeDtypeStruct((w_up.shape[1] // width * rows, width), BF16),
        ],
        name="pack",
    )(w_query, w_key, w_value, w_out, gains, w_up)


def split_turned(table, value, place, turned, own, other):
    turned[...] = value.T
    rows = turned.shape[0] // (Z_PARTS * PIECES)
    core = table[PIECES + QUARTERS]
    for block in range(Z_PARTS * QUARTERS):
        here = pl.ds(block * rows, rows)
        mine = pl.multiple_of((2 * block + core) * rows, rows)
        rest = pl.multiple_of((2 * block + 1 - core) * rows, rows)
        own[place, here, :] = turned[pl.ds(mine, rows), :]
        other[place, here, :] = turned[pl.ds(rest, rows), :]


def forward_kernel(
    blocks, length, frames, p0, p1, p2, p3,
    qkv_out, own_turned, other_turned, gains, log_totals, middle, second,
    held, gain_held, hidden, qkv, mixed, turned, sems, out_sems,
):
    pieces = (p0, p1, p2, p3)
    rows, width = frames.shape
    gain_copies = piece_copies(pieces, blocks, gain_held, sems.at[4], pl.ds(4 * width, LANES))
    copies = [
        piece_copies(pieces, blocks, held.at[part], sems.at[part], pl.ds(part * width, width))
        for part in range(4)
    ]
    start_all(gain_copies)
    for part in range(4):
        start_all(copies[part])
    value = frames[...].astype(F32)
    normal = value * inverse_rms(value)
    wait_all(gain_copies)
    across = flat(gain_held[...]).astype(F32).T
    gains[...] = across[:8]
    hidden[...] = (normal * across[0:1]).astype(BF16)
    leaving = []
    split_turned(blocks, hidden[...], 0, turned, own_turned, other_turned)
    for part in range(3):
        wait_all(copies[part])
        result = mxu(hidden[...], flat(held[part])).astype(BF16)
        if part == 0:
            result = (result.astype(F32) * FACTOR).astype(BF16)
        qkv[part] = result
        leaving.append(store(qkv.at[part], qkv_out.at[part], out_sems.at[part]))
        leaving[-1].start()

    bias = jnp.where(
        lax.broadcasted_iota(jnp.int32, (rows, 1), 0) < length[0], 0.0, -1e30
    ).astype(F32)
    lane = lax.broadcasted_iota(jnp.int32, (rows, LANES), 1)

    @pl.loop(0, width // LANES)
    def _(pair):
        here = lane_pair(pair)
        query, key, value = qkv[0, :, here], qkv[1, :, here], qkv[2, :, here]
        outs = []
        for half in range(2):
            mine = (lane < HEAD_DIM) == (half == 0)
            scores = mxu(key, jnp.where(mine, query, jnp.zeros_like(query)), NT) + bias
            peak = jnp.max(scores, axis=0, keepdims=True)
            expon = jnp.exp(scores - peak)
            sums = jnp.sum(expon, axis=0, keepdims=True)
            log_totals[pl.ds(2 * pair + half, 1), :] = peak + jnp.log(sums)
            shares = (expon * (1.0 / sums)).astype(BF16)
            outs.append(mxu(shares, value, TN))
        mixed[:, here] = jnp.where(lane < HEAD_DIM, outs[0], outs[1]).astype(BF16)

    split_turned(blocks, mixed[...], 1, turned, own_turned, other_turned)
    wait_all(copies[3])
    result = frames[...].astype(F32) + mxu(mixed[...], flat(held[3]))
    middle[...] = result
    low = (result * inverse_rms(result) * gains[1:2, :]).astype(BF16)
    second[...] = low
    split_turned(blocks, low, 2, turned, own_turned, other_turned)
    wait_all(leaving)


def forward_call(blocks, length, frames, pieces):
    rows, width = frames.shape
    turned = pltpu.HBM((3, width // 2, rows), BF16)
    return pl.pallas_call(
        forward_kernel,
        grid=(1,),
        in_specs=[SMEM_SPEC, SMEM_SPEC, whole((rows, width))] + [HBM_SPEC] * 4,
        out_specs=[HBM_SPEC, whole((3, width // 2, rows)), whole((3, width // 2, rows))]
        + [whole((8, width)), whole((HEADS, rows)), whole((rows, width)), whole((rows, width))],
        out_shape=[
            pltpu.HBM((3, rows, width), BF16),
            turned,
            turned,
            jax.ShapeDtypeStruct((8, width), F32),
            jax.ShapeDtypeStruct((HEADS, rows), F32),
            pltpu.HBM((rows, width), F32),
            pltpu.HBM((rows, width), BF16),
        ],
        scratch_shapes=[
            pltpu.VMEM((4, Z_PARTS, width // Z_PARTS, width), BF16),
            pltpu.VMEM((Z_PARTS, width // Z_PARTS, LANES), BF16),
            pltpu.VMEM((rows, width), BF16),
            pltpu.VMEM((3, rows, width), BF16),
            pltpu.VMEM((rows, width), BF16),
            pltpu.VMEM((width, rows), BF16),
            pltpu.SemaphoreType.DMA((5, PIECES)),
            pltpu.SemaphoreType.DMA((3,)),
        ],
        compiler_params=params("forward"),
        cost_estimate=cost(10 * rows * width * width, 16 * width * width, rows * rows),
        name="forward",
    )(blocks, length, *in_hbm([frames]), *pieces)


def up_kernel(
    blocks, second, p0, p1, p2, p3, slope, own, low_half, high_half, held, active, sems,
):
    step = pl.program_id(0)
    pieces = (p0, p1, p2, p3)

    def copies(part):
        return packed_copies(pieces, blocks, part, held.at[part], sems.at[part])

    prefetch(step, Z_PARTS, copies)
    value = mxu(second[...], flat(held[step]))
    square = value * value
    bend = jnp.tanh(GELU_A * value * (1.0 + GELU_B * square))
    share = 0.5 * (1.0 + bend)
    active[...] = (value * share).astype(BF16)
    slope[...] = (
        share + 0.5 * value * (1.0 - bend * bend) * (GELU_A * (1.0 + 3.0 * GELU_B * square))
    ).astype(BF16)
    core = blocks[PIECES + QUARTERS]
    width = active.shape[1] // PIECES
    for block in range(QUARTERS):
        here = pl.ds(block * width, width)
        mine = pl.multiple_of((2 * block + core) * width, width)
        rest = pl.multiple_of((2 * block + 1 - core) * width, width)
        own[:, here] = active[:, pl.ds(mine, width)]

        @pl.when(step < Z_PARTS // 2)
        def _():
            low_half[:, here] = active[:, pl.ds(rest, width)]

        @pl.when(step >= Z_PARTS // 2)
        def _():
            high_half[:, here] = active[:, pl.ds(rest, width)]


def up_call(blocks, second, pieces):
    rows, width = second.shape
    inner = pieces[0].shape[2] * pieces[0].shape[3] * PIECES * Z_PARTS // width
    columns = inner // Z_PARTS
    quarter = pltpu.HBM((rows, inner // 4), BF16)
    return pl.pallas_call(
        up_kernel,
        grid=(Z_PARTS,),
        in_specs=[SMEM_SPEC, whole((rows, width))] + [HBM_SPEC] * 4,
        out_specs=[
            pl.BlockSpec((rows, columns), lambda j: (0, j)),
            pl.BlockSpec((rows, columns // 2), lambda j: (0, j)),
            low_part((rows, columns // 2)),
            high_part((rows, columns // 2)),
        ],
        out_shape=[
            jax.ShapeDtypeStruct((rows, inner), BF16),
            jax.ShapeDtypeStruct((rows, inner // 2), BF16),
            quarter,
            quarter,
        ],
        scratch_shapes=[
            pltpu.VMEM((Z_PARTS, Z_PARTS, width // Z_PARTS, columns), BF16),
            pltpu.VMEM((rows, columns), BF16),
            pltpu.SemaphoreType.DMA((Z_PARTS, PIECES)),
        ],
        compiler_params=params("upward"),
        cost_estimate=cost(2 * rows * width * inner, 2 * width * inner, rows * inner),
        name="upward",
    )(blocks, *in_hbm([second]), *pieces)


def down_grad_kernel(
    blocks, mine, low_half, high_half, branch, other_branch, g0, g1, away, grads, grad_sems,
):
    step = pl.program_id(0)
    slot = lax.rem(step, 2)

    def leave(part, at):
        return grad_part_copies(grads.at[at], (g0, g1, away.at[0], away.at[1]), blocks, part, grad_sems.at[at])

    @pl.when(step >= 2)
    def _():
        wait_all(leave(step - 2, slot))

    for half, theirs in enumerate((low_half, high_half)):

        @pl.when((step >= Z_PARTS // 2) == (half == 1))
        def _():
            grads[slot] = (
                mxu(mine[...], branch[...], TN) + mxu(theirs[...], other_branch[...], TN)
            ).astype(BF16)

    start_all(leave(step, slot))

    @pl.when(step == Z_PARTS - 1)
    def _():
        wait_all(leave(step - 1, 1 - slot))
        wait_all(leave(step, slot))


def down_grad_call(blocks, mine, halves, branch, other_branch):
    rows, width = branch.shape
    columns = mine.shape[1] // Z_PARTS
    grad = jax.ShapeDtypeStruct((Z_PARTS, columns // QUARTERS, width), BF16)
    part = pl.BlockSpec((rows, columns), lambda j: (0, j))
    return pl.pallas_call(
        down_grad_kernel,
        grid=(Z_PARTS,),
        in_specs=[
            SMEM_SPEC,
            part,
            low_part((rows, columns)),
            high_part((rows, columns)),
            whole((rows, width)),
            whole((rows, width)),
        ],
        out_specs=[HBM_SPEC] * 3,
        out_shape=[grad, grad, jax.ShapeDtypeStruct((2,) + grad.shape, BF16)],
        scratch_shapes=[
            pltpu.VMEM((2, columns, width), BF16),
            pltpu.SemaphoreType.DMA((2, QUARTERS)),
        ],
        compiler_params=params("grads"),
        cost_estimate=cost(8 * rows * width * columns, 8 * width * columns, 0),
        name="down_grads",
    )(blocks, mine, *halves, branch, other_branch)


def down_kernel(blocks, branch, slope, p0, p1, p2, p3, low_half, high_half, held, sems):
    step = pl.program_id(0)
    pieces = (p0, p1, p2, p3)

    def copies(part):
        return part_copies(pieces, blocks, part, held.at[part], sems.at[part])

    prefetch(step, Z_PARTS, copies)
    value = mxu(branch[...], held[step], NT)
    low = (value * slope[...].astype(F32)).astype(BF16)

    @pl.when(step < Z_PARTS // 2)
    def _():
        low_half[...] = low

    @pl.when(step >= Z_PARTS // 2)
    def _():
        high_half[...] = low


def down_call(blocks, branch, slope, pieces):
    rows, width = branch.shape
    inner = slope.shape[1]
    columns = inner // Z_PARTS
    half = Z_PARTS // 2
    out = jax.ShapeDtypeStruct((rows, inner // 2), BF16)
    return pl.pallas_call(
        down_kernel,
        grid=(Z_PARTS,),
        in_specs=[
            SMEM_SPEC,
            whole((rows, width)),
            pl.BlockSpec((rows, columns), lambda j: (0, j)),
        ]
        + [HBM_SPEC] * 4,
        out_specs=[
            pl.BlockSpec((rows, columns), lambda j: (0, jnp.minimum(j, half - 1))),
            pl.BlockSpec((rows, columns), lambda j: (0, jnp.maximum(j - half, 0))),
        ],
        out_shape=[out, out],
        scratch_shapes=[
            pltpu.VMEM((Z_PARTS, columns, width), BF16),
            pltpu.SemaphoreType.DMA((Z_PARTS, PIECES)),
        ],
        compiler_params=params("downward"),
        cost_estimate=cost(2 * rows * width * inner, 2 * width * inner, 0),
        name="downward",
    )(blocks, branch, slope, *pieces)


def up_grad_kernel(
    blocks, mine, theirs, low_half, high_half, low_other, high_other, g0, g1, g2, g3, grads, grad_sems,
):
    step = pl.program_id(0)
    slot = lax.rem(step, 2)
    columns = low_half.shape[1]

    def leave(part, at):
        start = pl.multiple_of(part * columns, columns)
        return grad_copies(
            grads.at[at], (g0, g1, g2, g3), blocks, pl.ds(start, columns), grad_sems.at[at]
        )

    @pl.when(step >= 2)
    def _():
        wait_all(leave(step - 2, slot))

    for half, (near, far) in enumerate(((low_half, low_other), (high_half, high_other))):

        @pl.when((step >= Z_PARTS // 2) == (half == 1))
        def _():
            grad = mxu(mine[0], near[...]) + mxu(theirs[0], far[...])
            grads[slot] = grad.astype(BF16).reshape(grads.shape[1:])

    start_all(leave(step, slot))

    @pl.when(step == Z_PARTS - 1)
    def _():
        wait_all(leave(step - 1, 1 - slot))
        wait_all(leave(step, slot))


def up_grad_call(blocks, own_turned, other_turned, halves, other_halves):
    _, width, rows = own_turned.shape
    inner = 2 * halves[0].shape[1]
    columns = inner // Z_PARTS
    half = Z_PARTS // 2
    part_rows = width // Z_PARTS
    grad = pltpu.HBM((Z_PARTS, part_rows // QUARTERS, inner), BF16)
    turned = pl.BlockSpec((1, width, rows), lambda j: (2, 0, 0), pipeline_mode=pl.Buffered(1))
    low = pl.BlockSpec((rows, columns), lambda j: (0, jnp.minimum(j, half - 1)))
    high = pl.BlockSpec((rows, columns), lambda j: (0, jnp.maximum(j - half, 0)))
    return pl.pallas_call(
        up_grad_kernel,
        grid=(Z_PARTS,),
        in_specs=[SMEM_SPEC, turned, turned, low, high, low, high],
        out_specs=[HBM_SPEC] * QUARTERS,
        out_shape=[grad] * QUARTERS,
        scratch_shapes=[
            pltpu.VMEM((2, Z_PARTS, part_rows, columns), BF16),
            pltpu.SemaphoreType.DMA((2, QUARTERS)),
        ],
        compiler_params=params("grads"),
        cost_estimate=cost(4 * rows * width * inner, 2 * width * inner, 0),
        name="up_grads",
    )(blocks, own_turned, other_turned, *halves, *other_halves)


def result_kernel(blocks, length, middle, own, low_half, high_half, p0, p1, p2, p3, output, held, sums, sems):
    step = pl.program_id(0)
    steps = Z_PARTS
    pieces = (p0, p1, p2, p3)

    def copies(part):
        return part_copies(pieces, blocks, part, held.at[part], sems.at[part], by_class=True)

    @pl.when(step == 0)
    def _():
        for part in range(steps):
            start_all(copies(part))
        sums[...] = middle[...]

    for part in range(steps):

        @pl.when(step == part)
        def _():
            wait_all(copies(part))

    half = own.shape[1]
    for place, other in enumerate((low_half, high_half)):

        @pl.when((step >= Z_PARTS // 2) == (place == 1))
        def _():
            sums[...] += mxu(own[...], held[step, :half, :]) + mxu(
                other[...], held[step, half:, :]
            )


    @pl.when(step == steps - 1)
    def _():
        valid = lax.broadcasted_iota(jnp.int32, (sums.shape[0], 1), 0) < length[0]
        output[...] = (sums[...] * valid.astype(F32)).astype(BF16)


def result_call(blocks, length, middle, own, halves, pieces):
    rows, width = middle.shape
    inner = 2 * own.shape[1]
    columns = inner // Z_PARTS
    return pl.pallas_call(
        result_kernel,
        grid=(Z_PARTS,),
        in_specs=[
            SMEM_SPEC,
            SMEM_SPEC,
            whole((rows, width)),
            pl.BlockSpec((rows, columns // 2), lambda j: (0, j)),
            low_part((rows, columns // 2)),
            high_part((rows, columns // 2)),
        ]
        + [HBM_SPEC] * 4,
        out_specs=whole((rows, width)),
        out_shape=jax.ShapeDtypeStruct((rows, width), BF16),
        scratch_shapes=[
            pltpu.VMEM((Z_PARTS, columns, width), BF16),
            pltpu.VMEM((rows, width), F32),
            pltpu.SemaphoreType.DMA((Z_PARTS, PIECES)),
        ],
        compiler_params=params("result"),
        cost_estimate=cost(
            flops=2 * rows * width * inner, bytes_accessed=3 * width * inner, transcendentals=0
        ),
        name="result",
    )(blocks, length, middle, own, *halves, *in_hbm(pieces))


def middle_kernel(
    blocks, branch, middle, gains, low_half, high_half, u0, u1, u2, u3, p0, p1, p2, p3,
    grad_middle, grad_attn, grad_mixed, held, out_held, sums, sems, out_sems,
):
    step = pl.program_id(0)
    steps = Z_PARTS
    width = middle.shape[1]

    def copies(part):
        return packed_copies((u0, u1, u2, u3), blocks, part, held.at[part], sems.at[part])

    out_copies = piece_copies(
        (p0, p1, p2, p3), blocks, out_held, out_sems, pl.ds(3 * width, width)
    )
    prefetch(step, steps, copies)

    @pl.when(step == 1)
    def _():
        start_all(out_copies)

    @pl.when(step == 0)
    def _():
        sums[...] = mxu(low_half[...], flat(held[step]), NT)

    @pl.when((step > 0) & (step < steps // 2))
    def _():
        sums[...] += mxu(low_half[...], flat(held[step]), NT)

    @pl.when(step >= steps // 2)
    def _():
        sums[...] += mxu(high_half[...], flat(held[step]), NT)

    @pl.when(step == steps - 1)
    def _():
        value = middle[...]
        inverse = inverse_rms(value)
        normal = value * inverse
        scaled = sums[...] * gains[1:2, :]
        mean = jnp.mean(scaled * normal, axis=-1, keepdims=True)
        result = branch[...].astype(F32) + inverse * (scaled - normal * mean)
        grad_middle[...] = result
        low = result.astype(BF16)
        grad_attn[...] = low
        wait_all(out_copies)
        grad_mixed[...] = mxu(low, flat(out_held[...]), NT).astype(BF16)


def middle_call(blocks, branch, middle, gains, halves, up_pieces, pieces):
    rows, width = middle.shape
    inner = 2 * halves[0].shape[1]
    half = Z_PARTS // 2
    columns = inner // Z_PARTS
    return pl.pallas_call(
        middle_kernel,
        grid=(Z_PARTS,),
        in_specs=[
            SMEM_SPEC,
            whole((rows, width)),
            whole((rows, width)),
            whole((8, width)),
            pl.BlockSpec((rows, columns), lambda j: (0, jnp.minimum(j, half - 1))),
            pl.BlockSpec((rows, columns), lambda j: (0, jnp.maximum(j - half, 0))),
        ]
        + [HBM_SPEC] * 8,
        out_specs=[whole((rows, width))] * 3,
        out_shape=[
            pltpu.HBM((rows, width), F32),
            pltpu.HBM((rows, width), BF16),
            jax.ShapeDtypeStruct((rows, width), BF16),
        ],
        scratch_shapes=[
            pltpu.VMEM((Z_PARTS, Z_PARTS, width // Z_PARTS, columns), BF16),
            pltpu.VMEM((Z_PARTS, width // Z_PARTS, width), BF16),
            pltpu.VMEM((rows, width), F32),
            pltpu.SemaphoreType.DMA((Z_PARTS, PIECES)),
            pltpu.SemaphoreType.DMA((PIECES,)),
        ],
        compiler_params=params("middle"),
        cost_estimate=cost(2 * rows * width * (inner + width), 3 * width * inner, 0),
        name="middle",
    )(blocks, branch, middle, gains, *halves, *up_pieces, *pieces)


def attend_back_kernel(
    length, queries, keys, values, log_totals, grads, grad_query, grad_key, grad_value,
):
    rows, width = grads.shape
    bias = jnp.where(
        lax.broadcasted_iota(jnp.int32, (rows, 1), 0) < length[0], 0.0, -1e30
    ).astype(F32)
    lane = lax.broadcasted_iota(jnp.int32, (rows, LANES), 1)

    @pl.loop(0, width // LANES)
    def _(pair):
        here = lane_pair(pair)
        query, key, value, grad = queries[0, :, here], keys[0, :, here], values[0, :, here], grads[:, here]
        parts = []
        for half in range(2):
            mine = (lane < HEAD_DIM) == (half == 0)
            scores = mxu(key, jnp.where(mine, query, jnp.zeros_like(query)), NT) + bias
            chance = jnp.exp(scores - log_totals[pl.ds(2 * pair + half, 1), :])
            to_value = mxu(chance.astype(BF16), grad)
            grad_chance = mxu(value, jnp.where(mine, grad, jnp.zeros_like(grad)), NT)
            mean = jnp.sum(chance * grad_chance, axis=0, keepdims=True)
            grad_scores = (chance * (grad_chance - mean)).astype(BF16)
            to_key = mxu(grad_scores, query)
            to_query = mxu(grad_scores, key, TN) * FACTOR
            parts.append((to_query, to_key, to_value))
        for place, out in enumerate((grad_query, grad_key, grad_value)):
            out[:, here] = jnp.where(lane < HEAD_DIM, parts[0][place], parts[1][place]).astype(BF16)


def attend_back_call(length, log_totals, qkv, grad_mixed):
    rows, width = grad_mixed.shape

    def plane(place):
        return pl.BlockSpec(
            (1, rows, width), lambda j: (place, 0, 0), pipeline_mode=pl.Buffered(1)
        )

    return pl.pallas_call(
        attend_back_kernel,
        grid=(1,),
        in_specs=[
            SMEM_SPEC, plane(0), plane(1), plane(2), whole((HEADS, rows)), whole((rows, width)),
        ],
        out_specs=[whole((rows, width))] * 3,
        out_shape=[jax.ShapeDtypeStruct((rows, width), BF16)] * 3,
        compiler_params=params("attend_back"),
        cost_estimate=cost(20 * rows * width * width, 40 * width * width, rows * rows),
        name="attend_back",
    )(length, qkv, qkv, qkv, log_totals, grad_mixed)


def attn_grad_kernel(
    blocks, mine_in, theirs_in, a0, a1, a2, a3, b0, b1, b2, b3, g0, g1, g2, g3,
    turned, near, far, grads, turned_sems, load_sems, grad_sems,
):
    columns = a0.shape[1]
    turned_loads = [
        store(source.at[pl.ds(0, 2)], turned.at[at], turned_sems.at[at])
        for at, source in enumerate((mine_in, theirs_in))
    ]
    start_all(turned_loads)
    loads = []
    for part, sources in enumerate(((a0, b0), (a1, b1), (a2, b2), (a3, b3))):
        loads.append(
            [
                store(source, target.at[part], load_sems.at[at, part])
                for at, (source, target) in enumerate(zip(sources, (near, far)))
            ]
        )
        start_all(loads[part])
    wait_all(turned_loads)
    pending = []
    for part in range(4):
        wait_all(loads[part])
        left = part // 3
        grad = mxu(turned[0, left], near[part]) + mxu(turned[1, left], far[part])
        grads[part] = grad.astype(BF16).reshape(grads.shape[1:])
        pending.append(
            grad_copies(
                grads.at[part], (g0, g1, g2, g3), blocks, pl.ds(part * columns, columns), grad_sems.at[part]
            )
        )
        start_all(pending[part])
    for copies in pending:
        wait_all(copies)


def attn_grad_call(blocks, own_turned, other_turned, near, far):
    _, width, rows = own_turned.shape
    columns = near[0].shape[1]
    part_rows = width // Z_PARTS
    grad = pltpu.HBM((Z_PARTS, part_rows // QUARTERS, 4 * columns), BF16)
    return pl.pallas_call(
        attn_grad_kernel,
        grid=(1,),
        in_specs=[SMEM_SPEC] + [HBM_SPEC] * 10,
        out_specs=[HBM_SPEC] * QUARTERS,
        out_shape=[grad] * QUARTERS,
        scratch_shapes=[
            pltpu.VMEM((2, 2, width, rows), BF16),
            pltpu.VMEM((4, rows, columns), BF16),
            pltpu.VMEM((4, rows, columns), BF16),
            pltpu.VMEM((4, Z_PARTS, part_rows, columns), BF16),
            pltpu.SemaphoreType.DMA((2,)),
            pltpu.SemaphoreType.DMA((2, 4)),
            pltpu.SemaphoreType.DMA((4, QUARTERS)),
        ],
        compiler_params=params("grads"),
        cost_estimate=cost(16 * rows * width * columns, 16 * width * columns, 0),
        name="attn_grads",
    )(blocks, own_turned, other_turned, *near, *far)


def frames_kernel(
    blocks, frames, gains, grad_middle, grad_query, grad_key, grad_value, p0, p1, p2, p3, grad_frames,
    held, sums, sems,
):
    step = pl.program_id(0)
    width = frames.shape[1]

    def copies(part):
        return piece_copies(
            (p0, p1, p2, p3), blocks, held.at[part], sems.at[part], pl.ds(part * width, width)
        )

    prefetch(step, 3, copies)
    for part, grad in enumerate((grad_query, grad_key, grad_value)):

        @pl.when(step == part)
        def _():
            term = mxu(grad[...], flat(held[part]), NT)
            sums[...] = term if part == 0 else sums[...] + term

    @pl.when(step == 2)
    def _():
        rows = frames[...].astype(F32)
        inverse = inverse_rms(rows)
        normal = rows * inverse
        scaled = sums[...] * gains[0:1, :]
        mean = jnp.mean(scaled * normal, axis=-1, keepdims=True)
        grad_frames[...] = grad_middle[...] + inverse * (scaled - normal * mean)


def frames_call(blocks, frames, gains, grad_middle, grad_qkv, pieces):
    rows, width = frames.shape
    return pl.pallas_call(
        frames_kernel,
        grid=(3,),
        in_specs=[
            SMEM_SPEC,
            whole((rows, width)),
            whole((8, width)),
            whole((rows, width)),
            whole((rows, width)),
            whole((rows, width)),
            whole((rows, width)),
        ]
        + [HBM_SPEC] * 4,
        out_specs=whole((rows, width)),
        out_shape=jax.ShapeDtypeStruct((rows, width), F32),
        scratch_shapes=[
            pltpu.VMEM((3, Z_PARTS, width // Z_PARTS, width), BF16),
            pltpu.VMEM((rows, width), F32),
            pltpu.SemaphoreType.DMA((3, PIECES)),
        ],
        compiler_params=params("frames"),
        cost_estimate=cost(6 * rows * width * width, 10 * width * width, 0),
        name="frames_back",
    )(blocks, frames, gains, grad_middle, *grad_qkv, *in_hbm(pieces))


def kernels_chain(blocks, rows_in, lengths, branch, attn_pieces, up_pieces, down_pieces, swap):
    qkv, own_turned, other_turned, gain_rows, log_totals, middle, second = forward_call(
        blocks, lengths, rows_in, attn_pieces
    )
    their_turned = swap(other_turned)
    slope, active, *other_active = up_call(blocks, second, up_pieces)
    down_grads = down_grad_call(
        blocks, active, [swap(half) for half in other_active], branch, swap(branch)
    )
    halves = down_call(blocks, branch, slope, down_pieces)
    grad_middle, grad_attn, grad_mixed = middle_call(
        blocks, branch, middle, gain_rows, halves, up_pieces, attn_pieces
    )
    up_grads = up_grad_call(
        blocks, own_turned, their_turned, halves, [swap(half) for half in halves]
    )
    grad_qkv = attend_back_call(lengths, log_totals, qkv, grad_mixed)
    factors = (*grad_qkv, grad_attn)
    attn_grads = attn_grad_call(
        blocks, own_turned, their_turned, factors, [swap(factor) for factor in factors]
    )
    output = result_call(blocks, lengths, middle, active, other_active, down_pieces)
    grad_frames = frames_call(blocks, rows_in, gain_rows, grad_middle, grad_qkv, attn_pieces)
    return output, grad_frames, attn_grads, up_grads, (*down_grads[:2], *down_grads[2])


def layer_whole(blocks, rows_in, lengths, branch, attn, upper, w_down):
    attn_pieces, down_pieces = (gather_whole(part) for part in (attn, w_down))
    rows = attn.shape[0]
    parts = [gather_whole(upper[at : at + rows]) for at in range(0, upper.shape[0], rows)]
    up_pieces = tuple(jnp.concatenate(part, axis=-2) for part in zip(*parts))
    down_pieces = tuple(jnp.swapaxes(part, 0, 1) for part in down_pieces)
    output, grad_frames, *grads = kernels_chain(
        blocks, rows_in, lengths, branch, attn_pieces, up_pieces, down_pieces, across_cores
    )
    return (output, grad_frames) + tuple(scatter_whole(part) for part in grads)


def layer_plane(blocks, rows_in, lengths, branch, attn, upper, w_down):
    attn_column = gather_column(attn)
    up_column = gather_column(upper)
    down_near = jnp.stack((w_down, first_hop(w_down)))
    their_branch = across_cores(branch, "their_branch")
    attn_column = after(attn_column, down_near, their_branch)
    down_near = gather_column(down_near)
    attn_near = jnp.stack((attn_column, first_hop(attn_column)))
    attn_far = second_hop(attn_near, "attn_far")
    up_column = after(up_column, attn_near)
    up_next = first_hop(up_column, "up_next")
    attn_pieces = with_other_core(attn_near, attn_far)
    up_near = jnp.stack((up_column, up_next))
    up_far = second_hop(up_near, "up_far")

    qkv, own_turned, other_turned, gain_rows, log_totals, middle, second = forward_call(
        blocks, lengths, after(rows_in, up_near), attn_pieces
    )

    up_far = after(up_far, second, down_near)
    up_pieces = with_other_core(up_near, up_far)
    down_near = after(down_near, up_far)
    down_far = second_hop(down_near, "down_far")
    slope, active, *other_active = up_call(blocks, after(second, down_near), up_pieces)
    their_active = [across_cores(half, "their_active") for half in other_active]
    their_turned = across_cores(after(other_turned, slope), "their_turned")
    down_grads = down_grad_call(blocks, active, their_active, branch, their_branch)
    down_one = first_hop(down_grads[2], "down_one")

    down_pieces = with_other_core(down_near, after(down_far, down_grads[0]))
    halves = down_call(blocks, after(branch, down_grads[0]), slope, down_pieces)
    their_halves = [across_cores(half, "their_half") for half in halves]
    grad_middle, grad_attn, grad_mixed = middle_call(
        blocks, branch, middle, gain_rows, halves, up_pieces, attn_pieces
    )
    their_attn = across_cores(grad_attn, "their_attn")
    down_one = after(down_one, grad_mixed)
    down_away = low_total(down_grads[1], down_one[1])
    down_two = second_hop(down_away, "down_two")
    up_grads = up_grad_call(
        blocks, after(own_turned, down_away), their_turned, halves, their_halves
    )
    up_one_away = first_hop(up_grads[3], "up_one_away")
    up_one = first_hop(up_grads[2], "up_one")
    grad_qkv = attend_back_call(lengths, log_totals, qkv, after(grad_mixed, up_grads[0]))
    their_qkv = [across_cores(grad, "their_qkv") for grad in grad_qkv]

    down_two = after(down_two, grad_qkv[0])
    down_last = low_total(down_grads[0], down_one[0], down_two)
    down_rows = scatter_column(down_last)
    up_one_away = after(up_one_away, down_last, up_one)
    up_away = low_total(up_grads[1], up_one_away)
    up_two = second_hop(up_away, "up_two")
    attn_grads = attn_grad_call(
        blocks, after(own_turned, up_away), their_turned, (*grad_qkv, grad_attn),
        (*their_qkv, their_attn),
    )
    attn_one_away = first_hop(attn_grads[3], "attn_one_away")
    attn_one = first_hop(attn_grads[2], "attn_one")
    grad_frames = frames_call(
        blocks, rows_in, gain_rows, after(grad_middle, attn_grads[0]), grad_qkv, attn_pieces
    )

    up_two = after(up_two, grad_frames)
    up_last = low_total(up_grads[0], up_one, up_two)
    up_rows = scatter_column(up_last)
    attn_one_away = after(attn_one_away, up_last)
    attn_away = low_total(attn_grads[1], attn_one_away)
    attn_two = second_hop(attn_away, "attn_two")
    output = result_call(
        blocks, lengths, after(middle, attn_away), active, other_active, down_pieces
    )
    attn_one = after(attn_one, output)
    attn_last = low_total(attn_grads[0], attn_one, attn_two)
    attn_rows = scatter_column(attn_last)
    return output, grad_frames, attn_rows, up_rows, down_rows


def on_device(
    sizes, frames, lengths, w_query, w_key, w_value, w_out, w_up, w_down,
    gain_attn, gain_mlp, cotangent,
):
    width = frames.shape[-1]
    blocks = place_table(sizes)
    rows_in = frames[0]
    valid = lax.broadcasted_iota(jnp.int32, (rows_in.shape[0], 1), 0) < lengths[0]
    branch = jnp.where(valid, cotangent[0], jnp.zeros_like(cotangent[0]))
    gains = jnp.pad(jnp.stack((gain_attn, gain_mlp), axis=1), ((0, 0), (0, LANES - 2)))
    attn, upper = pack_call(w_query, w_key, w_value, w_out, gains, w_up)
    layer = layer_plane if is_plane(sizes) else layer_whole
    output, grad_frames, attn_rows, up_rows, down_rows = layer(
        blocks, rows_in, lengths, branch, attn, upper, w_down
    )
    grad_query, grad_key, grad_value, grad_out = (
        attn_rows[:, place * width : (place + 1) * width] for place in range(4)
    )
    gain_one = (
        jnp.sum(w_query.astype(F32) * grad_query, axis=1)
        + jnp.sum(w_key.astype(F32) * grad_key, axis=1)
        + jnp.sum(w_value.astype(F32) * grad_value, axis=1)
    ) / gain_attn.astype(F32)
    gain_two = jnp.sum(w_up.astype(F32) * up_rows, axis=1) / gain_mlp.astype(F32)
    return (
        output[None], grad_frames[None], grad_query, grad_key, grad_value, grad_out,
        up_rows, down_rows, gain_one, gain_two,
    )


def solution(mesh):
    wide, narrow = mesh.shape["wide"], mesh.shape["narrow"]
    y = 1
    while 4 * y * y <= wide:
        y *= 2
    sizes = {"z": wide // y, "y": y, "x": narrow // 2, "c": 2}
    fine = Mesh(mesh.devices.reshape(tuple(sizes[name] for name in ALL)), ALL)
    split = P(ALL)
    return jax.shard_map(
        functools.partial(on_device, sizes),
        mesh=fine,
        in_specs=(split,) * 11,
        out_specs=(split,) * 10,
        check_vma=False,
    )
```

```python
import functools

import jax
import jax.numpy as jnp
import numpy as np
from jax import lax
from jax.experimental import pallas as pl
from jax.experimental.pallas import tpu as pltpu
from jax.sharding import Mesh, PartitionSpec as P

HEADS = 16
HEAD_DIM = 64
EPSILON = 1e-06
FACTOR = HEAD_DIM ** (-0.5)
LANES = 128
Z_PARTS = 4
PIECES = 8
QUARTERS = 4
ALL = ("z", "y", "x", "c")
PLANE = ("y", "x", "c")
SWAP = [(0, 1), (1, 0)]
VMEM_MIB = {"forward": 32, "upward": 26, "downward": 26, "middle": 24, "attend_back": 26, "grads": 24, "result": 20, "frames": 20}
F32 = jnp.float32
BF16 = jnp.bfloat16
GELU_A = 0.7978845608028654
GELU_B = 0.044715

NN = (((1,), (0,)), ((), ()))
NT = (((1,), (1,)), ((), ()))
TN = (((0,), (0,)), ((), ()))


def mxu(left, right, dims=NN):
    return lax.dot_general(left, right, dims, preferred_element_type=F32)


def plane_pairs(step):
    pairs = []
    for y in range(2):
        for x in range(2):
            for c in range(2):
                flip_y = (c == 0) == (step == 1)
                to = (1 - y, x, c) if flip_y else (y, 1 - x, c)
                pairs.append(((y * 2 + x) * 2 + c, (to[0] * 2 + to[1]) * 2 + to[2]))
    return pairs


def is_plane(sizes):
    return sizes["x"] == 2 and sizes["y"] == 2 and sizes["c"] == 2 and sizes["z"] == Z_PARTS


def place_table(sizes):
    core = lax.axis_index("c")
    piece = jnp.arange(PIECES + QUARTERS + 1, dtype=jnp.int32)
    side = core ^ jnp.where(piece < PIECES, (piece >> 2) & 1, 0)
    first = (piece >> 1) & 1
    second = piece & 1
    if is_plane(sizes):
        y = lax.axis_index("y") ^ jnp.where(side == 0, first, second)
        x = lax.axis_index("x") ^ jnp.where(side == 0, second, first)
    else:
        y, x = first, second
    place = y * 2 + x
    place = jnp.where(piece < PIECES, place * 2 + side, place)
    return jnp.where(piece < PIECES + QUARTERS, place, core).astype(jnp.int32)


def after(value, *others):
    return lax.optimization_barrier((value,) + others)[0]


def first_hop(value, name="pieces"):
    with jax.named_scope(name):
        return lax.ppermute(value, PLANE, plane_pairs(1))


def second_hop(value, name="pieces"):
    with jax.named_scope(name):
        return lax.ppermute(value, PLANE, plane_pairs(2))


def across_cores(value, name="pieces"):
    with jax.named_scope(name):
        return lax.ppermute(value, "c", SWAP)


def with_other_core(near, far):
    other_near = across_cores(near, "other_near")
    far = after(far, other_near)
    return (near, far, other_near, across_cores(far, "other_far"))


def gather_column(shard):
    return lax.all_gather(shard, "z", axis=0, tiled=False)


def gather_whole(shard):
    full = lax.all_gather(shard, ALL, axis=0, tiled=True)
    full = full.reshape(Z_PARTS, 2, 2, 2, full.shape[0] // (Z_PARTS * PIECES), full.shape[1])
    even, odd = full[:, :, :, 0], full[:, :, :, 1]
    upper = lax.axis_index("c") == 1
    pieces = []
    for side in (jnp.where(upper, odd, even), jnp.where(upper, even, odd)):
        pieces += [jnp.swapaxes(side[:, :, second], 0, 1) for second in range(2)]
    return tuple(pieces)


def total(*parts):
    result = parts[0].astype(F32)
    for part in parts[1:]:
        result = result + part.astype(F32)
    return result


def low_total(*parts):
    return total(*parts).astype(BF16)


def scatter_column(mine):
    return lax.psum_scatter(mine, "z", scatter_dimension=0, tiled=False).astype(F32)


def scatter_whole(parts):
    mine = jnp.stack(parts, axis=1)[:, :, None]
    here = lax.broadcasted_iota(jnp.int32, (1, 1, 2, 1, 1), 2) == lax.axis_index("c")
    full = jnp.where(here, mine, jnp.zeros_like(mine))
    full = full.reshape(-1, full.shape[-1])
    return lax.psum_scatter(full, ALL, scatter_dimension=0, tiled=True).astype(F32)


COST_SHARE = 0.02


def cost(flops, bytes_accessed, transcendentals):
    return pl.CostEstimate(
        flops=int(COST_SHARE * flops), bytes_accessed=int(COST_SHARE * bytes_accessed),
        transcendentals=int(COST_SHARE * transcendentals),
    )


def in_hbm(pieces):
    return [pltpu.with_memory_space_constraint(part, pltpu.HBM) for part in pieces]


def params(name):
    return pltpu.CompilerParams(vmem_limit_bytes=VMEM_MIB[name] << 20)


HBM_SPEC = pl.BlockSpec(memory_space=pl.ANY)
SMEM_SPEC = pl.BlockSpec(memory_space=pltpu.SMEM)


def whole(shape):
    return pl.BlockSpec(
        shape, lambda *_: (0,) * len(shape), pipeline_mode=pl.Buffered(1)
    )


def low_part(shape):
    return pl.BlockSpec(shape, lambda j: (0, jnp.minimum(j, Z_PARTS // 2 - 1)))


def high_part(shape):
    return pl.BlockSpec(shape, lambda j: (0, jnp.maximum(j - Z_PARTS // 2, 0)))


def piece_copies(pieces, blocks, held, sems, columns):
    rows = pieces[0].shape[2]
    copies = []
    for piece in range(PIECES):
        own, first, second = piece >> 2, (piece >> 1) & 1, piece & 1
        source = pieces[2 * own + second].at[first, :, :, columns]
        start = pl.multiple_of(blocks[piece] * rows, rows)
        copies.append(
            pltpu.make_async_copy(source, held.at[:, pl.ds(start, rows), :], sems.at[piece])
        )
    return copies


def packed_copies(pieces, blocks, part, held, sems):
    rows = held.shape[1] // PIECES
    copies = []
    for piece in range(PIECES):
        own, first, second = piece >> 2, (piece >> 1) & 1, piece & 1
        source = pieces[2 * own + second].at[first, :, pl.ds(part * rows, rows), :]
        start = pl.multiple_of(blocks[piece] * rows, rows)
        copies.append(
            pltpu.make_async_copy(source, held.at[:, pl.ds(start, rows), :], sems.at[piece])
        )
    return copies


def part_copies(pieces, blocks, part, held, sems, by_class=False):
    rows = pieces[0].shape[2]
    copies = []
    for piece in range(PIECES):
        own, first, second = piece >> 2, (piece >> 1) & 1, piece & 1
        source = pieces[2 * own + second].at[part, first]
        place = QUARTERS * own + (blocks[piece] >> 1) if by_class else blocks[piece]
        start = pl.multiple_of(place * rows, rows)
        copies.append(
            pltpu.make_async_copy(source, held.at[pl.ds(start, rows), :], sems.at[piece])
        )
    return copies


def grad_copies(held, outs, table, columns, sems):
    rows = outs[0].shape[1]
    copies = []
    for piece in range(QUARTERS):
        target = outs[piece].at[:, :, columns]
        start = pl.multiple_of(table[PIECES + piece] * rows, rows)
        copies.append(
            pltpu.make_async_copy(held.at[:, pl.ds(start, rows), :], target, sems.at[piece])
        )
    return copies


def grad_part_copies(held, outs, table, part, sems):
    rows = outs[0].shape[1]
    copies = []
    for piece in range(QUARTERS):
        target = outs[piece].at[part]
        start = pl.multiple_of(table[PIECES + piece] * rows, rows)
        copies.append(
            pltpu.make_async_copy(held.at[pl.ds(start, rows), :], target, sems.at[piece])
        )
    return copies


def start_all(copies):
    for copy in copies:
        copy.start()


def wait_all(copies):
    for copy in copies:
        copy.wait()


def prefetch(step, steps, copies):
    @pl.when(step == 0)
    def _():
        start_all(copies(0))
        start_all(copies(1))

    for part in range(steps):

        @pl.when(step == part)
        def _():
            if part + 2 < steps:
                start_all(copies(part + 2))
            wait_all(copies(part))


def flat(block):
    return block.reshape(block.shape[0] * block.shape[1], block.shape[2])


def inverse_rms(rows):
    return lax.rsqrt(jnp.mean(rows * rows, axis=-1, keepdims=True) + EPSILON)


def store(source, target, sem):
    return pltpu.make_async_copy(source, target, sem)


def lane_pair(pair):
    return pl.ds(pl.multiple_of(pair * LANES, LANES), LANES)


def pack_kernel(w_query, w_key, w_value, w_out, gain_attn, gain_mlp, w_up, attn, upper):
    width = w_query.shape[1]
    rows = w_up.shape[0]
    for part, weight in enumerate((w_query, w_key, w_value, w_out)):
        attn[:, part * width : (part + 1) * width] = weight[...]
    place = lax.broadcasted_iota(jnp.int32, (LANES, rows), 0)
    gains = jnp.where(place == 0, gain_attn[...].astype(F32), gain_mlp[...].astype(F32))
    attn[:, 4 * width :] = jnp.where(place < 2, gains, 0.0).T.astype(BF16)
    for block in range(w_up.shape[1] // width):
        upper[block * rows : (block + 1) * rows, :] = w_up[:, block * width : (block + 1) * width]


def pack_call(w_query, w_key, w_value, w_out, gain_attn, gain_mlp, w_up):
    rows, width = w_query.shape
    return pl.pallas_call(
        pack_kernel,
        out_shape=[
            jax.ShapeDtypeStruct((rows, 4 * width + LANES), BF16),
            jax.ShapeDtypeStruct((w_up.shape[1] // width * rows, width), BF16),
        ],
        name="pack",
    )(w_query, w_key, w_value, w_out, gain_attn, gain_mlp, w_up)


def split_turned(table, value, place, turned, own, other):
    turned[...] = value.T
    rows = turned.shape[0] // (Z_PARTS * PIECES)
    core = table[PIECES + QUARTERS]
    for block in range(Z_PARTS * QUARTERS):
        here = pl.ds(block * rows, rows)
        mine = pl.multiple_of((2 * block + core) * rows, rows)
        rest = pl.multiple_of((2 * block + 1 - core) * rows, rows)
        own[place, here, :] = turned[pl.ds(mine, rows), :]
        other[place, here, :] = turned[pl.ds(rest, rows), :]


def forward_kernel(
    blocks, length, frames, p0, p1, p2, p3,
    qkv_out, own_turned, other_turned, gains, log_totals, middle, second,
    held, gain_held, hidden, qkv, mixed, turned, sems, out_sems,
):
    pieces = (p0, p1, p2, p3)
    rows, width = frames.shape
    gain_copies = piece_copies(pieces, blocks, gain_held, sems.at[4], pl.ds(4 * width, LANES))
    copies = [
        piece_copies(pieces, blocks, held.at[part], sems.at[part], pl.ds(part * width, width))
        for part in range(4)
    ]
    start_all(gain_copies)
    for part in range(4):
        start_all(copies[part])
    value = frames[...].astype(F32)
    normal = value * inverse_rms(value)
    wait_all(gain_copies)
    across = flat(gain_held[...]).astype(F32).T
    gains[...] = across[:8]
    hidden[...] = (normal * across[0:1]).astype(BF16)
    leaving = []
    split_turned(blocks, hidden[...], 0, turned, own_turned, other_turned)
    for part in range(3):
        wait_all(copies[part])
        result = mxu(hidden[...], flat(held[part])).astype(BF16)
        if part == 0:
            result = (result.astype(F32) * FACTOR).astype(BF16)
        qkv[part] = result
        leaving.append(store(qkv.at[part], qkv_out.at[part], out_sems.at[part]))
        leaving[-1].start()

    bias = jnp.where(
        lax.broadcasted_iota(jnp.int32, (rows, 1), 0) < length[0], 0.0, -1e30
    ).astype(F32)
    lane = lax.broadcasted_iota(jnp.int32, (rows, LANES), 1)

    @pl.loop(0, width // LANES)
    def _(pair):
        here = lane_pair(pair)
        query, key, value = qkv[0, :, here], qkv[1, :, here], qkv[2, :, here]
        outs = []
        for half in range(2):
            mine = (lane < HEAD_DIM) == (half == 0)
            scores = mxu(key, jnp.where(mine, query, jnp.zeros_like(query)), NT) + bias
            peak = jnp.max(scores, axis=0, keepdims=True)
            expon = jnp.exp(scores - peak)
            sums = jnp.sum(expon, axis=0, keepdims=True)
            log_totals[pl.ds(2 * pair + half, 1), :] = peak + jnp.log(sums)
            shares = (expon * (1.0 / sums)).astype(BF16)
            outs.append(mxu(shares, value, TN))
        mixed[:, here] = jnp.where(lane < HEAD_DIM, outs[0], outs[1]).astype(BF16)

    split_turned(blocks, mixed[...], 1, turned, own_turned, other_turned)
    wait_all(copies[3])
    result = frames[...].astype(F32) + mxu(mixed[...], flat(held[3]))
    middle[...] = result
    low = (result * inverse_rms(result) * gains[1:2, :]).astype(BF16)
    second[...] = low
    split_turned(blocks, low, 2, turned, own_turned, other_turned)
    wait_all(leaving)


def forward_call(blocks, length, frames, pieces):
    rows, width = frames.shape
    turned = pltpu.HBM((3, width // 2, rows), BF16)
    return pl.pallas_call(
        forward_kernel,
        grid=(1,),
        in_specs=[SMEM_SPEC, SMEM_SPEC, whole((rows, width))] + [HBM_SPEC] * 4,
        out_specs=[HBM_SPEC, whole((3, width // 2, rows)), whole((3, width // 2, rows))]
        + [whole((8, width)), whole((HEADS, rows)), whole((rows, width)), whole((rows, width))],
        out_shape=[
            pltpu.HBM((3, rows, width), BF16),
            turned,
            turned,
            jax.ShapeDtypeStruct((8, width), F32),
            jax.ShapeDtypeStruct((HEADS, rows), F32),
            pltpu.HBM((rows, width), F32),
            pltpu.HBM((rows, width), BF16),
        ],
        scratch_shapes=[
            pltpu.VMEM((4, Z_PARTS, width // Z_PARTS, width), BF16),
            pltpu.VMEM((Z_PARTS, width // Z_PARTS, LANES), BF16),
            pltpu.VMEM((rows, width), BF16),
            pltpu.VMEM((3, rows, width), BF16),
            pltpu.VMEM((rows, width), BF16),
            pltpu.VMEM((width, rows), BF16),
            pltpu.SemaphoreType.DMA((5, PIECES)),
            pltpu.SemaphoreType.DMA((3,)),
        ],
        compiler_params=params("forward"),
        cost_estimate=cost(10 * rows * width * width, 16 * width * width, rows * rows),
        name="forward",
    )(blocks, length, *in_hbm([frames]), *pieces)


def up_kernel(
    blocks, second, p0, p1, p2, p3, slope, own, low_half, high_half, held, active, sems,
):
    step = pl.program_id(0)
    pieces = (p0, p1, p2, p3)

    def copies(part):
        return packed_copies(pieces, blocks, part, held.at[part], sems.at[part])

    prefetch(step, Z_PARTS, copies)
    value = mxu(second[...], flat(held[step]))
    square = value * value
    bend = jnp.tanh(GELU_A * value * (1.0 + GELU_B * square))
    share = 0.5 * (1.0 + bend)
    active[...] = (value * share).astype(BF16)
    slope[...] = (
        share + 0.5 * value * (1.0 - bend * bend) * (GELU_A * (1.0 + 3.0 * GELU_B * square))
    ).astype(BF16)
    core = blocks[PIECES + QUARTERS]
    width = active.shape[1] // PIECES
    for block in range(QUARTERS):
        here = pl.ds(block * width, width)
        mine = pl.multiple_of((2 * block + core) * width, width)
        rest = pl.multiple_of((2 * block + 1 - core) * width, width)
        own[:, here] = active[:, pl.ds(mine, width)]

        @pl.when(step < Z_PARTS // 2)
        def _():
            low_half[:, here] = active[:, pl.ds(rest, width)]

        @pl.when(step >= Z_PARTS // 2)
        def _():
            high_half[:, here] = active[:, pl.ds(rest, width)]


def up_call(blocks, second, pieces):
    rows, width = second.shape
    inner = pieces[0].shape[2] * pieces[0].shape[3] * PIECES * Z_PARTS // width
    columns = inner // Z_PARTS
    quarter = pltpu.HBM((rows, inner // 4), BF16)
    return pl.pallas_call(
        up_kernel,
        grid=(Z_PARTS,),
        in_specs=[SMEM_SPEC, whole((rows, width))] + [HBM_SPEC] * 4,
        out_specs=[
            pl.BlockSpec((rows, columns), lambda j: (0, j)),
            pl.BlockSpec((rows, columns // 2), lambda j: (0, j)),
            low_part((rows, columns // 2)),
            high_part((rows, columns // 2)),
        ],
        out_shape=[
            jax.ShapeDtypeStruct((rows, inner), BF16),
            jax.ShapeDtypeStruct((rows, inner // 2), BF16),
            quarter,
            quarter,
        ],
        scratch_shapes=[
            pltpu.VMEM((Z_PARTS, Z_PARTS, width // Z_PARTS, columns), BF16),
            pltpu.VMEM((rows, columns), BF16),
            pltpu.SemaphoreType.DMA((Z_PARTS, PIECES)),
        ],
        compiler_params=params("upward"),
        cost_estimate=cost(2 * rows * width * inner, 2 * width * inner, rows * inner),
        name="upward",
    )(blocks, *in_hbm([second]), *pieces)


def down_grad_kernel(
    blocks, mine, low_half, high_half, branch, other_branch, g0, g1, away, grads, grad_sems,
):
    step = pl.program_id(0)
    slot = lax.rem(step, 2)

    def leave(part, at):
        return grad_part_copies(grads.at[at], (g0, g1, away.at[0], away.at[1]), blocks, part, grad_sems.at[at])

    @pl.when(step >= 2)
    def _():
        wait_all(leave(step - 2, slot))

    for half, theirs in enumerate((low_half, high_half)):

        @pl.when((step >= Z_PARTS // 2) == (half == 1))
        def _():
            grads[slot] = (
                mxu(mine[...], branch[...], TN) + mxu(theirs[...], other_branch[...], TN)
            ).astype(BF16)

    start_all(leave(step, slot))

    @pl.when(step == Z_PARTS - 1)
    def _():
        wait_all(leave(step - 1, 1 - slot))
        wait_all(leave(step, slot))


def down_grad_call(blocks, mine, halves, branch, other_branch):
    rows, width = branch.shape
    columns = mine.shape[1] // Z_PARTS
    grad = jax.ShapeDtypeStruct((Z_PARTS, columns // QUARTERS, width), BF16)
    part = pl.BlockSpec((rows, columns), lambda j: (0, j))
    return pl.pallas_call(
        down_grad_kernel,
        grid=(Z_PARTS,),
        in_specs=[
            SMEM_SPEC,
            part,
            low_part((rows, columns)),
            high_part((rows, columns)),
            whole((rows, width)),
            whole((rows, width)),
        ],
        out_specs=[HBM_SPEC] * 3,
        out_shape=[grad, grad, jax.ShapeDtypeStruct((2,) + grad.shape, BF16)],
        scratch_shapes=[
            pltpu.VMEM((2, columns, width), BF16),
            pltpu.SemaphoreType.DMA((2, QUARTERS)),
        ],
        compiler_params=params("grads"),
        cost_estimate=cost(8 * rows * width * columns, 8 * width * columns, 0),
        name="down_grads",
    )(blocks, mine, *halves, branch, other_branch)


def down_kernel(blocks, branch, slope, p0, p1, p2, p3, low_half, high_half, held, sems):
    step = pl.program_id(0)
    pieces = (p0, p1, p2, p3)

    def copies(part):
        return part_copies(pieces, blocks, part, held.at[part], sems.at[part])

    prefetch(step, Z_PARTS, copies)
    value = mxu(branch[...], held[step], NT)
    low = (value * slope[...].astype(F32)).astype(BF16)

    @pl.when(step < Z_PARTS // 2)
    def _():
        low_half[...] = low

    @pl.when(step >= Z_PARTS // 2)
    def _():
        high_half[...] = low


def down_call(blocks, branch, slope, pieces):
    rows, width = branch.shape
    inner = slope.shape[1]
    columns = inner // Z_PARTS
    half = Z_PARTS // 2
    out = jax.ShapeDtypeStruct((rows, inner // 2), BF16)
    return pl.pallas_call(
        down_kernel,
        grid=(Z_PARTS,),
        in_specs=[
            SMEM_SPEC,
            whole((rows, width)),
            pl.BlockSpec((rows, columns), lambda j: (0, j)),
        ]
        + [HBM_SPEC] * 4,
        out_specs=[
            pl.BlockSpec((rows, columns), lambda j: (0, jnp.minimum(j, half - 1))),
            pl.BlockSpec((rows, columns), lambda j: (0, jnp.maximum(j - half, 0))),
        ],
        out_shape=[out, out],
        scratch_shapes=[
            pltpu.VMEM((Z_PARTS, columns, width), BF16),
            pltpu.SemaphoreType.DMA((Z_PARTS, PIECES)),
        ],
        compiler_params=params("downward"),
        cost_estimate=cost(2 * rows * width * inner, 2 * width * inner, 0),
        name="downward",
    )(blocks, branch, slope, *pieces)


def up_grad_kernel(
    blocks, mine, theirs, low_half, high_half, low_other, high_other, g0, g1, g2, g3, grads, grad_sems,
):
    step = pl.program_id(0)
    slot = lax.rem(step, 2)
    columns = low_half.shape[1]

    def leave(part, at):
        start = pl.multiple_of(part * columns, columns)
        return grad_copies(
            grads.at[at], (g0, g1, g2, g3), blocks, pl.ds(start, columns), grad_sems.at[at]
        )

    @pl.when(step >= 2)
    def _():
        wait_all(leave(step - 2, slot))

    for half, (near, far) in enumerate(((low_half, low_other), (high_half, high_other))):

        @pl.when((step >= Z_PARTS // 2) == (half == 1))
        def _():
            grad = mxu(mine[0], near[...]) + mxu(theirs[0], far[...])
            grads[slot] = grad.astype(BF16).reshape(grads.shape[1:])

    start_all(leave(step, slot))

    @pl.when(step == Z_PARTS - 1)
    def _():
        wait_all(leave(step - 1, 1 - slot))
        wait_all(leave(step, slot))


def up_grad_call(blocks, own_turned, other_turned, halves, other_halves):
    _, width, rows = own_turned.shape
    inner = 2 * halves[0].shape[1]
    columns = inner // Z_PARTS
    half = Z_PARTS // 2
    part_rows = width // Z_PARTS
    grad = pltpu.HBM((Z_PARTS, part_rows // QUARTERS, inner), BF16)
    turned = pl.BlockSpec((1, width, rows), lambda j: (2, 0, 0), pipeline_mode=pl.Buffered(1))
    low = pl.BlockSpec((rows, columns), lambda j: (0, jnp.minimum(j, half - 1)))
    high = pl.BlockSpec((rows, columns), lambda j: (0, jnp.maximum(j - half, 0)))
    return pl.pallas_call(
        up_grad_kernel,
        grid=(Z_PARTS,),
        in_specs=[SMEM_SPEC, turned, turned, low, high, low, high],
        out_specs=[HBM_SPEC] * QUARTERS,
        out_shape=[grad] * QUARTERS,
        scratch_shapes=[
            pltpu.VMEM((2, Z_PARTS, part_rows, columns), BF16),
            pltpu.SemaphoreType.DMA((2, QUARTERS)),
        ],
        compiler_params=params("grads"),
        cost_estimate=cost(4 * rows * width * inner, 2 * width * inner, 0),
        name="up_grads",
    )(blocks, own_turned, other_turned, *halves, *other_halves)


def result_kernel(blocks, length, middle, own, low_half, high_half, p0, p1, p2, p3, output, held, sums, sems):
    step = pl.program_id(0)
    steps = Z_PARTS
    pieces = (p0, p1, p2, p3)

    def copies(part):
        return part_copies(pieces, blocks, part, held.at[part], sems.at[part], by_class=True)

    @pl.when(step == 0)
    def _():
        for part in range(steps):
            start_all(copies(part))
        sums[...] = middle[...]

    for part in range(steps):

        @pl.when(step == part)
        def _():
            wait_all(copies(part))

    half = own.shape[1]
    for place, other in enumerate((low_half, high_half)):

        @pl.when((step >= Z_PARTS // 2) == (place == 1))
        def _():
            sums[...] += mxu(own[...], held[step, :half, :]) + mxu(
                other[...], held[step, half:, :]
            )


    @pl.when(step == steps - 1)
    def _():
        valid = lax.broadcasted_iota(jnp.int32, (sums.shape[0], 1), 0) < length[0]
        output[...] = (sums[...] * valid.astype(F32)).astype(BF16)


def result_call(blocks, length, middle, own, halves, pieces):
    rows, width = middle.shape
    inner = 2 * own.shape[1]
    columns = inner // Z_PARTS
    return pl.pallas_call(
        result_kernel,
        grid=(Z_PARTS,),
        in_specs=[
            SMEM_SPEC,
            SMEM_SPEC,
            whole((rows, width)),
            pl.BlockSpec((rows, columns // 2), lambda j: (0, j)),
            low_part((rows, columns // 2)),
            high_part((rows, columns // 2)),
        ]
        + [HBM_SPEC] * 4,
        out_specs=whole((rows, width)),
        out_shape=jax.ShapeDtypeStruct((rows, width), BF16),
        scratch_shapes=[
            pltpu.VMEM((Z_PARTS, columns, width), BF16),
            pltpu.VMEM((rows, width), F32),
            pltpu.SemaphoreType.DMA((Z_PARTS, PIECES)),
        ],
        compiler_params=params("result"),
        cost_estimate=cost(
            flops=2 * rows * width * inner, bytes_accessed=3 * width * inner, transcendentals=0
        ),
        name="result",
    )(blocks, length, middle, own, *halves, *in_hbm(pieces))


def middle_kernel(
    blocks, branch, middle, gains, low_half, high_half, u0, u1, u2, u3, p0, p1, p2, p3,
    grad_middle, grad_attn, grad_mixed, held, out_held, sums, sems, out_sems,
):
    step = pl.program_id(0)
    steps = Z_PARTS
    width = middle.shape[1]

    def copies(part):
        return packed_copies((u0, u1, u2, u3), blocks, part, held.at[part], sems.at[part])

    out_copies = piece_copies(
        (p0, p1, p2, p3), blocks, out_held, out_sems, pl.ds(3 * width, width)
    )
    prefetch(step, steps, copies)

    @pl.when(step == 1)
    def _():
        start_all(out_copies)

    @pl.when(step == 0)
    def _():
        sums[...] = mxu(low_half[...], flat(held[step]), NT)

    @pl.when((step > 0) & (step < steps // 2))
    def _():
        sums[...] += mxu(low_half[...], flat(held[step]), NT)

    @pl.when(step >= steps // 2)
    def _():
        sums[...] += mxu(high_half[...], flat(held[step]), NT)

    @pl.when(step == steps - 1)
    def _():
        value = middle[...]
        inverse = inverse_rms(value)
        normal = value * inverse
        scaled = sums[...] * gains[1:2, :]
        mean = jnp.mean(scaled * normal, axis=-1, keepdims=True)
        result = branch[...].astype(F32) + inverse * (scaled - normal * mean)
        grad_middle[...] = result
        low = result.astype(BF16)
        grad_attn[...] = low
        wait_all(out_copies)
        grad_mixed[...] = mxu(low, flat(out_held[...]), NT).astype(BF16)


def middle_call(blocks, branch, middle, gains, halves, up_pieces, pieces):
    rows, width = middle.shape
    inner = 2 * halves[0].shape[1]
    half = Z_PARTS // 2
    columns = inner // Z_PARTS
    return pl.pallas_call(
        middle_kernel,
        grid=(Z_PARTS,),
        in_specs=[
            SMEM_SPEC,
            whole((rows, width)),
            whole((rows, width)),
            whole((8, width)),
            pl.BlockSpec((rows, columns), lambda j: (0, jnp.minimum(j, half - 1))),
            pl.BlockSpec((rows, columns), lambda j: (0, jnp.maximum(j - half, 0))),
        ]
        + [HBM_SPEC] * 8,
        out_specs=[whole((rows, width))] * 3,
        out_shape=[
            pltpu.HBM((rows, width), F32),
            pltpu.HBM((rows, width), BF16),
            jax.ShapeDtypeStruct((rows, width), BF16),
        ],
        scratch_shapes=[
            pltpu.VMEM((Z_PARTS, Z_PARTS, width // Z_PARTS, columns), BF16),
            pltpu.VMEM((Z_PARTS, width // Z_PARTS, width), BF16),
            pltpu.VMEM((rows, width), F32),
            pltpu.SemaphoreType.DMA((Z_PARTS, PIECES)),
            pltpu.SemaphoreType.DMA((PIECES,)),
        ],
        compiler_params=params("middle"),
        cost_estimate=cost(2 * rows * width * (inner + width), 3 * width * inner, 0),
        name="middle",
    )(blocks, branch, middle, gains, *halves, *up_pieces, *pieces)


def attend_back_kernel(
    length, queries, keys, values, log_totals, grads, grad_query, grad_key, grad_value,
):
    rows, width = grads.shape
    bias = jnp.where(
        lax.broadcasted_iota(jnp.int32, (rows, 1), 0) < length[0], 0.0, -1e30
    ).astype(F32)
    lane = lax.broadcasted_iota(jnp.int32, (rows, LANES), 1)

    @pl.loop(0, width // LANES)
    def _(pair):
        here = lane_pair(pair)
        query, key, value, grad = queries[0, :, here], keys[0, :, here], values[0, :, here], grads[:, here]
        parts = []
        for half in range(2):
            mine = (lane < HEAD_DIM) == (half == 0)
            scores = mxu(key, jnp.where(mine, query, jnp.zeros_like(query)), NT) + bias
            chance = jnp.exp(scores - log_totals[pl.ds(2 * pair + half, 1), :])
            to_value = mxu(chance.astype(BF16), grad)
            grad_chance = mxu(value, jnp.where(mine, grad, jnp.zeros_like(grad)), NT)
            mean = jnp.sum(chance * grad_chance, axis=0, keepdims=True)
            grad_scores = (chance * (grad_chance - mean)).astype(BF16)
            to_key = mxu(grad_scores, query)
            to_query = mxu(grad_scores, key, TN) * FACTOR
            parts.append((to_query, to_key, to_value))
        for place, out in enumerate((grad_query, grad_key, grad_value)):
            out[:, here] = jnp.where(lane < HEAD_DIM, parts[0][place], parts[1][place]).astype(BF16)


def attend_back_call(length, log_totals, qkv, grad_mixed):
    rows, width = grad_mixed.shape

    def plane(place):
        return pl.BlockSpec(
            (1, rows, width), lambda j: (place, 0, 0), pipeline_mode=pl.Buffered(1)
        )

    return pl.pallas_call(
        attend_back_kernel,
        grid=(1,),
        in_specs=[
            SMEM_SPEC, plane(0), plane(1), plane(2), whole((HEADS, rows)), whole((rows, width)),
        ],
        out_specs=[whole((rows, width))] * 3,
        out_shape=[jax.ShapeDtypeStruct((rows, width), BF16)] * 3,
        compiler_params=params("attend_back"),
        cost_estimate=cost(20 * rows * width * width, 40 * width * width, rows * rows),
        name="attend_back",
    )(length, qkv, qkv, qkv, log_totals, grad_mixed)


def attn_grad_kernel(
    blocks, mine_in, theirs_in, a0, a1, a2, a3, b0, b1, b2, b3, g0, g1, g2, g3,
    turned, near, far, grads, turned_sems, load_sems, grad_sems,
):
    columns = a0.shape[1]
    turned_loads = [
        store(source.at[pl.ds(0, 2)], turned.at[at], turned_sems.at[at])
        for at, source in enumerate((mine_in, theirs_in))
    ]
    start_all(turned_loads)
    loads = []
    for part, sources in enumerate(((a0, b0), (a1, b1), (a2, b2), (a3, b3))):
        loads.append(
            [
                store(source, target.at[part], load_sems.at[at, part])
                for at, (source, target) in enumerate(zip(sources, (near, far)))
            ]
        )
        start_all(loads[part])
    wait_all(turned_loads)
    pending = []
    for part in range(4):
        wait_all(loads[part])
        left = part // 3
        grad = mxu(turned[0, left], near[part]) + mxu(turned[1, left], far[part])
        grads[part] = grad.astype(BF16).reshape(grads.shape[1:])
        pending.append(
            grad_copies(
                grads.at[part], (g0, g1, g2, g3), blocks, pl.ds(part * columns, columns), grad_sems.at[part]
            )
        )
        start_all(pending[part])
    for copies in pending:
        wait_all(copies)


def attn_grad_call(blocks, own_turned, other_turned, near, far):
    _, width, rows = own_turned.shape
    columns = near[0].shape[1]
    part_rows = width // Z_PARTS
    grad = pltpu.HBM((Z_PARTS, part_rows // QUARTERS, 4 * columns), BF16)
    return pl.pallas_call(
        attn_grad_kernel,
        grid=(1,),
        in_specs=[SMEM_SPEC] + [HBM_SPEC] * 10,
        out_specs=[HBM_SPEC] * QUARTERS,
        out_shape=[grad] * QUARTERS,
        scratch_shapes=[
            pltpu.VMEM((2, 2, width, rows), BF16),
            pltpu.VMEM((4, rows, columns), BF16),
            pltpu.VMEM((4, rows, columns), BF16),
            pltpu.VMEM((4, Z_PARTS, part_rows, columns), BF16),
            pltpu.SemaphoreType.DMA((2,)),
            pltpu.SemaphoreType.DMA((2, 4)),
            pltpu.SemaphoreType.DMA((4, QUARTERS)),
        ],
        compiler_params=params("grads"),
        cost_estimate=cost(16 * rows * width * columns, 16 * width * columns, 0),
        name="attn_grads",
    )(blocks, own_turned, other_turned, *near, *far)


def frames_kernel(
    blocks, frames, gains, grad_middle, grad_query, grad_key, grad_value, p0, p1, p2, p3, grad_frames,
    held, sums, sems,
):
    step = pl.program_id(0)
    width = frames.shape[1]

    def copies(part):
        return piece_copies(
            (p0, p1, p2, p3), blocks, held.at[part], sems.at[part], pl.ds(part * width, width)
        )

    prefetch(step, 3, copies)
    for part, grad in enumerate((grad_query, grad_key, grad_value)):

        @pl.when(step == part)
        def _():
            term = mxu(grad[...], flat(held[part]), NT)
            sums[...] = term if part == 0 else sums[...] + term

    @pl.when(step == 2)
    def _():
        rows = frames[...].astype(F32)
        inverse = inverse_rms(rows)
        normal = rows * inverse
        scaled = sums[...] * gains[0:1, :]
        mean = jnp.mean(scaled * normal, axis=-1, keepdims=True)
        grad_frames[...] = grad_middle[...] + inverse * (scaled - normal * mean)


def frames_call(blocks, frames, gains, grad_middle, grad_qkv, pieces):
    rows, width = frames.shape
    return pl.pallas_call(
        frames_kernel,
        grid=(3,),
        in_specs=[
            SMEM_SPEC,
            whole((rows, width)),
            whole((8, width)),
            whole((rows, width)),
            whole((rows, width)),
            whole((rows, width)),
            whole((rows, width)),
        ]
        + [HBM_SPEC] * 4,
        out_specs=whole((rows, width)),
        out_shape=jax.ShapeDtypeStruct((rows, width), F32),
        scratch_shapes=[
            pltpu.VMEM((3, Z_PARTS, width // Z_PARTS, width), BF16),
            pltpu.VMEM((rows, width), F32),
            pltpu.SemaphoreType.DMA((3, PIECES)),
        ],
        compiler_params=params("frames"),
        cost_estimate=cost(6 * rows * width * width, 10 * width * width, 0),
        name="frames_back",
    )(blocks, frames, gains, grad_middle, *grad_qkv, *in_hbm(pieces))


def kernels_chain(blocks, rows_in, lengths, branch, attn_pieces, up_pieces, down_pieces, swap):
    qkv, own_turned, other_turned, gain_rows, log_totals, middle, second = forward_call(
        blocks, lengths, rows_in, attn_pieces
    )
    their_turned = swap(other_turned)
    slope, active, *other_active = up_call(blocks, second, up_pieces)
    down_grads = down_grad_call(
        blocks, active, [swap(half) for half in other_active], branch, swap(branch)
    )
    halves = down_call(blocks, branch, slope, down_pieces)
    grad_middle, grad_attn, grad_mixed = middle_call(
        blocks, branch, middle, gain_rows, halves, up_pieces, attn_pieces
    )
    up_grads = up_grad_call(
        blocks, own_turned, their_turned, halves, [swap(half) for half in halves]
    )
    grad_qkv = attend_back_call(lengths, log_totals, qkv, grad_mixed)
    factors = (*grad_qkv, grad_attn)
    attn_grads = attn_grad_call(
        blocks, own_turned, their_turned, factors, [swap(factor) for factor in factors]
    )
    output = result_call(blocks, lengths, middle, active, other_active, down_pieces)
    grad_frames = frames_call(blocks, rows_in, gain_rows, grad_middle, grad_qkv, attn_pieces)
    return output, grad_frames, attn_grads, up_grads, (*down_grads[:2], *down_grads[2])


def layer_whole(blocks, rows_in, lengths, branch, attn, upper, w_down):
    attn_pieces, down_pieces = (gather_whole(part) for part in (attn, w_down))
    rows = attn.shape[0]
    parts = [gather_whole(upper[at : at + rows]) for at in range(0, upper.shape[0], rows)]
    up_pieces = tuple(jnp.concatenate(part, axis=-2) for part in zip(*parts))
    down_pieces = tuple(jnp.swapaxes(part, 0, 1) for part in down_pieces)
    output, grad_frames, *grads = kernels_chain(
        blocks, rows_in, lengths, branch, attn_pieces, up_pieces, down_pieces, across_cores
    )
    return (output, grad_frames) + tuple(scatter_whole(part) for part in grads)


def layer_plane(blocks, rows_in, lengths, branch, attn, upper, w_down):
    attn_column = gather_column(attn)
    up_column = gather_column(upper)
    down_near = jnp.stack((w_down, first_hop(w_down)))
    their_branch = across_cores(branch, "their_branch")
    attn_column = after(attn_column, down_near, their_branch)
    down_near = gather_column(down_near)
    attn_near = jnp.stack((attn_column, first_hop(attn_column)))
    attn_far = second_hop(attn_near, "attn_far")
    up_column = after(up_column, attn_near)
    up_next = first_hop(up_column, "up_next")
    attn_pieces = with_other_core(attn_near, attn_far)
    up_near = jnp.stack((up_column, up_next))
    up_far = second_hop(up_near, "up_far")

    qkv, own_turned, other_turned, gain_rows, log_totals, middle, second = forward_call(
        blocks, lengths, after(rows_in, up_near), attn_pieces
    )

    up_far = after(up_far, second, down_near)
    up_pieces = with_other_core(up_near, up_far)
    down_near = after(down_near, up_far)
    down_far = second_hop(down_near, "down_far")
    slope, active, *other_active = up_call(blocks, after(second, down_near), up_pieces)
    their_active = [across_cores(half, "their_active") for half in other_active]
    their_turned = across_cores(after(other_turned, slope), "their_turned")
    down_grads = down_grad_call(blocks, active, their_active, branch, their_branch)
    down_one = first_hop(down_grads[2], "down_one")

    down_pieces = with_other_core(down_near, after(down_far, down_grads[0]))
    halves = down_call(blocks, after(branch, down_grads[0]), slope, down_pieces)
    their_halves = [across_cores(half, "their_half") for half in halves]
    grad_middle, grad_attn, grad_mixed = middle_call(
        blocks, branch, middle, gain_rows, halves, up_pieces, attn_pieces
    )
    their_attn = across_cores(grad_attn, "their_attn")
    down_one = after(down_one, grad_mixed)
    down_away = low_total(down_grads[1], down_one[1])
    down_two = second_hop(down_away, "down_two")
    up_grads = up_grad_call(
        blocks, after(own_turned, down_away), their_turned, halves, their_halves
    )
    up_one_away = first_hop(up_grads[3], "up_one_away")
    up_one = first_hop(up_grads[2], "up_one")
    grad_qkv = attend_back_call(lengths, log_totals, qkv, after(grad_mixed, up_grads[0]))
    their_qkv = [across_cores(grad, "their_qkv") for grad in grad_qkv]

    down_two = after(down_two, grad_qkv[0])
    down_last = low_total(down_grads[0], down_one[0], down_two)
    down_rows = scatter_column(down_last)
    up_one_away = after(up_one_away, down_last, up_one)
    up_away = low_total(up_grads[1], up_one_away)
    up_two = second_hop(up_away, "up_two")
    attn_grads = attn_grad_call(
        blocks, after(own_turned, up_away), their_turned, (*grad_qkv, grad_attn),
        (*their_qkv, their_attn),
    )
    attn_one_away = first_hop(attn_grads[3], "attn_one_away")
    attn_one = first_hop(attn_grads[2], "attn_one")
    grad_frames = frames_call(
        blocks, rows_in, gain_rows, after(grad_middle, attn_grads[0]), grad_qkv, attn_pieces
    )

    up_two = after(up_two, grad_frames)
    up_last = low_total(up_grads[0], up_one, up_two)
    up_rows = scatter_column(up_last)
    attn_one_away = after(attn_one_away, up_last)
    attn_away = low_total(attn_grads[1], attn_one_away)
    attn_two = second_hop(attn_away, "attn_two")
    output = result_call(
        blocks, lengths, after(middle, attn_away), active, other_active, down_pieces
    )
    attn_one = after(attn_one, output)
    attn_last = low_total(attn_grads[0], attn_one, attn_two)
    attn_rows = scatter_column(attn_last)
    return output, grad_frames, attn_rows, up_rows, down_rows


def on_device(
    sizes, frames, lengths, w_query, w_key, w_value, w_out, w_up, w_down,
    gain_attn, gain_mlp, cotangent,
):
    width = frames.shape[-1]
    blocks = place_table(sizes)
    rows_in = frames[0]
    valid = lax.broadcasted_iota(jnp.int32, (rows_in.shape[0], 1), 0) < lengths[0]
    branch = jnp.where(valid, cotangent[0], jnp.zeros_like(cotangent[0]))
    attn, upper = pack_call(
        w_query, w_key, w_value, w_out, gain_attn[None], gain_mlp[None], w_up
    )
    layer = layer_plane if is_plane(sizes) else layer_whole
    output, grad_frames, attn_rows, up_rows, down_rows = layer(
        blocks, rows_in, lengths, branch, attn, upper, w_down
    )
    grad_query, grad_key, grad_value, grad_out = (
        attn_rows[:, place * width : (place + 1) * width] for place in range(4)
    )
    gain_one = (
        jnp.sum(w_query.astype(F32) * grad_query, axis=1)
        + jnp.sum(w_key.astype(F32) * grad_key, axis=1)
        + jnp.sum(w_value.astype(F32) * grad_value, axis=1)
    ) / gain_attn.astype(F32)
    gain_two = jnp.sum(w_up.astype(F32) * up_rows, axis=1) / gain_mlp.astype(F32)
    return (
        output[None], grad_frames[None], grad_query, grad_key, grad_value, grad_out,
        up_rows, down_rows, gain_one, gain_two,
    )


def solution(mesh):
    wide, narrow = mesh.shape["wide"], mesh.shape["narrow"]
    y = 1
    while 4 * y * y <= wide:
        y *= 2
    sizes = {"z": wide // y, "y": y, "x": narrow // 2, "c": 2}
    fine = Mesh(mesh.devices.reshape(tuple(sizes[name] for name in ALL)), ALL)
    split = P(ALL)
    return jax.shard_map(
        functools.partial(on_device, sizes),
        mesh=fine,
        in_specs=(split,) * 11,
        out_specs=(split,) * 10,
        check_vma=False,
    )
```
